32 devices in a mesh: dp: 8 (over z, y), mp: 4 (over x, core).
Axes of the slice: x: 2, y: 2, z: 4, core: 2. Of those that a mesh axis runs over, the one named last changes fastest.
Arguments:
- tokens: bfloat16 [32768, 512], P(('dp', 'mp')), may hold values from -6 to 6
- cotangent: bfloat16 [32768, 512], P(('dp', 'mp')), may hold values from -6 to 6
- routes: int32 [32768, 8], P(('dp', 'mp')), may hold values from 0 to 23, all different within a row
- starts: int32 [32768], P(('dp', 'mp')), may hold values from 0 to 3072, as said below
- attn_param: float32 [512, 3226], P(('dp', 'mp'))
- attn_first: float32 [512, 3226], P(('dp', 'mp'))
- attn_second: float32 [512, 3226], P(('dp', 'mp')), as said below
- ffn_param: float32 [2, 512, 2048], P(None, 'dp', 'mp')
- ffn_first: float32 [2, 512, 2048], P(None, 'dp', 'mp')
- ffn_second: float32 [2, 512, 2048], P(None, 'dp', 'mp'), as said below
- rates: float32 [7], replicated, as said below
Outputs:
- layer_out: bfloat16 [32768, 512], P(('dp', 'mp'))
- input_grad: float32 [32768, 512], P(('dp', 'mp'))
- attn_grad: float32 [512, 3226], P(('dp', 'mp'))
- attn_second_new: float32 [512, 3226], P(('dp', 'mp'))
- attn_new: float32 [512, 3226], P(('dp', 'mp'))
- ffn_grad: float32 [2, 512, 2048], P(None, 'dp', 'mp')
- ffn_second_new: float32 [2, 512, 2048], P(None, 'dp', 'mp')
- ffn_new: float32 [2, 512, 2048], P(None, 'dp', 'mp')
- grad_norm: float32 [], replicated
- gain_grad: float32 [512, 2], P(('dp', 'mp'))
The draws below stay inside these ranges and needn't reach their ends.
Inputs may be any that keep to these rules, and one draw needn't show every extreme that they name: `routes`: each row names 8 different experts. `starts`: sequences are contiguous within each group of 4096 tokens; in half of the groups one sequence fills the group, in the others every sequence has 1024 tokens. `attn_second`: positive. `ffn_second`: positive. `rates`: positive.
All inputs are finite; a program needn't handle non-finite values.
Results may differ from the reference program's by a relative error of at most 0.012.
The reference program's roundings to bfloat16 on the way count: a program that leaves them out, or rounds other values in their place, can miss the bound.
Values may be sent and summed in bfloat16 or wider, within the bound.
No kernel may reach another device: no remote copies, remote signals or barrier semaphores. Data moves between devices by JAX's collectives and lax.ppermute only.
A program may use at most 128 MiB of HBM per device.

```python
import math
import jax
import jax.numpy as jnp
from jax import lax

D = 512
HD = 64
E = 24
TOPK = 8
FF = 2048
SHORT = 1024
ADAM_STEP = 7
GROUP = 4096
GROUPS = 8
TOKENS = 32768
AC = 3226


CLIP_LEVEL = 0.1


def output_scale():
    return (TOPK * SHORT / (4.0 * HD)) ** 0.5


def column_scales():
    span = E * HD
    return jnp.concatenate([jnp.full((span,), D ** (-0.5)), jnp.full((span,), output_scale()), jnp.full((2 * HD,), D ** (-0.5)), jnp.full((E,), 0.5 * D ** (-0.5))]).astype(jnp.float32)


def kind_sizes():
    span = E * HD
    size_query = CLIP_LEVEL / (D * span) ** 0.5
    size_output = CLIP_LEVEL / (D * span) ** 0.5
    size_keyval = CLIP_LEVEL / (D * 2 * HD) ** 0.5
    size_router = CLIP_LEVEL / (D * E) ** 0.5
    size_gain = CLIP_LEVEL / D ** 0.5
    size_ffn = CLIP_LEVEL / (8 * D * FF) ** 0.5
    attn_cols = jnp.concatenate([jnp.full((span,), size_query), jnp.full((span,), size_output), jnp.full((2 * HD,), size_keyval), jnp.full((E,), size_router), jnp.full((2,), size_gain)]).astype(jnp.float32)
    ffn_kinds = jnp.array([size_ffn, size_ffn], jnp.float32)
    return (attn_cols, ffn_kinds)


def draw_starts(key, part):
    order = jax.random.permutation(jax.random.fold_in(key, 18), GROUPS)
    longer = order < GROUPS // 2
    place = jnp.arange(GROUP, dtype=jnp.int32)
    short_start = place // SHORT * SHORT
    result = jnp.where(longer[:, None], jnp.zeros_like(short_start)[None, :], short_start[None, :])
    return result.reshape(TOKENS).astype(jnp.int32)


def draw_attn_param(key, part):
    first_key, second_key = jax.random.split(jax.random.fold_in(key, 11))
    weights = jax.random.normal(first_key, (D, AC - 2), jnp.float32) * column_scales()[None, :]
    trend = -0.6 + 1.2 * jnp.arange(D, dtype=jnp.float32) / (D - 1)
    noise = jax.random.uniform(second_key, (D, 2), jnp.float32, -0.3, 0.3)
    gains = jnp.exp(trend[:, None] + noise)
    return jnp.concatenate([weights, gains], 1)


def draw_attn_first(key, part):
    values = jax.random.normal(jax.random.fold_in(key, 12), (D, AC), jnp.float32)
    return values * (0.1 / 0.9) * kind_sizes()[0][None, :]


def draw_attn_second(key, part):
    spread = jax.random.uniform(jax.random.fold_in(key, 13), (D, AC), jnp.float32, 0.0, math.log(4.0))
    return 0.05 / 0.95 * kind_sizes()[0][None, :] ** 2 * jnp.exp(spread)


def draw_ffn_param(key, part):
    values = jax.random.normal(jax.random.fold_in(key, 14), (2, D, FF), jnp.float32)
    scales = jnp.array([D ** (-0.5), FF ** (-0.5)], jnp.float32)
    return values * scales[:, None, None]


def draw_ffn_first(key, part):
    values = jax.random.normal(jax.random.fold_in(key, 15), (2, D, FF), jnp.float32)
    return values * (0.1 / 0.9) * kind_sizes()[1][:, None, None]


def draw_ffn_second(key, part):
    spread = jax.random.uniform(jax.random.fold_in(key, 16), (2, D, FF), jnp.float32, 0.0, math.log(4.0))
    return 0.05 / 0.95 * kind_sizes()[1][:, None, None] ** 2 * jnp.exp(spread)


def draw_rates(key, part):
    bases = jnp.array([D ** (-0.5), output_scale(), D ** (-0.5), 0.5 * D ** (-0.5), 0.1, D ** (-0.5), FF ** (-0.5)], jnp.float32)
    return bases * jax.random.uniform(jax.random.fold_in(key, 17), (7,), jnp.float32, 0.7, 1.4)


def block_levels(stream_key, dims, cuts, smallest, top_value):
    level = 1.0
    for position, blocks in cuts:
        draws = jax.random.uniform(jax.random.fold_in(jax.random.fold_in(stream_key, 6), position), (blocks,), jnp.float32, smallest / len(cuts), top_value / len(cuts))
        level = level * jnp.repeat(jnp.exp(draws), dims[position] // blocks).reshape((-1,) + (1,) * (len(dims) - 1 - position))
    return level


def picks_of(rng, rows, amount, top, lift):
    ranking = jax.random.permutation(jax.random.fold_in(rng, 1), amount)
    boost = ranking
    for power in range(3):
        boost = boost * boost // amount
    boost = boost * lift // amount
    chance = jax.random.randint(jax.random.fold_in(rng, 2), (rows, amount), 0, 4096) + boost
    sure = jax.random.permutation(jax.random.fold_in(rng, 3), rows)[jnp.arange(amount) % rows]
    chance = jnp.where(jnp.arange(rows)[:, None] == sure[None, :], 1 << 14, chance)
    score = chance * amount + jnp.arange(amount)
    return lax.top_k(score.astype(jnp.int32), top)[1].astype(jnp.int32)


def normal_values(key, dims, scale, limit, shards=(), held_as=jnp.bfloat16):
    values = jax.random.normal(key, dims, jnp.float32) * scale
    if len(shards) > 0:
        values = block_levels(key, dims, shards, -0.22, 0.18) * values
    return jnp.clip(values, min=-limit, max=limit).astype(held_as)


def setup_inputs(seed: int = 0) -> dict:
    splits = jax.random.split(jax.random.key(seed), 12)
    return {
        "tokens": normal_values(splits[0], (TOKENS, D), 1.0, 6.0, ((0, 32),)),
        "cotangent": normal_values(splits[1], (TOKENS, D), 1.0, 6.0, ((0, 32),)),
        "routes": picks_of(splits[2], TOKENS, E, TOPK, 0),
        "starts": draw_starts(jax.random.fold_in(splits[11], 71), 0),
        "attn_param": draw_attn_param(jax.random.fold_in(splits[11], 71), 0),
        "attn_first": draw_attn_first(jax.random.fold_in(splits[11], 71), 0),
        "attn_second": draw_attn_second(jax.random.fold_in(splits[11], 71), 0),
        "ffn_param": draw_ffn_param(jax.random.fold_in(splits[11], 71), 0),
        "ffn_first": draw_ffn_first(jax.random.fold_in(splits[11], 71), 0),
        "ffn_second": draw_ffn_second(jax.random.fold_in(splits[11], 71), 0),
        "rates": draw_rates(jax.random.fold_in(splits[11], 71), 0),
    }


precise = lax.Precision.HIGHEST
NORM_EPS = 1e-05
MASKED = -1e+30
CLIP_NORM = 0.1
BETA_FIRST = 0.9
BETA_SECOND = 0.95
ADAM_EPS = 1e-08
WEIGHT_DECAY = 0.1

@jax.custom_vjp
def low(v):
    return lax.optimization_barrier(v.astype(jnp.bfloat16)).astype(jnp.float32)

@jax.custom_vjp
def low_back(v):
    return v

def low_keep(v):
    return (low(v), None)

def low_pass(kept, grad):
    return (grad,)

def back_keep(v):
    return (v, None)

def back_low(kept, grad):
    return (low(grad),)
low.defvjp(low_keep, low_pass)
low_back.defvjp(back_keep, back_low)

def layer_norm(values, gain):
    centred = values - lax.optimization_barrier(jnp.mean(values, -1, keepdims=True))
    variance = lax.optimization_barrier(jnp.mean(centred * centred, -1, keepdims=True))
    return centred * lax.rsqrt(variance + NORM_EPS) * gain

def attend_group(queries, key_rows, value_rows, start_rows):
    group_len = queries.shape[0]
    stacked = queries.transpose(1, 0, 2).reshape(-1, HD)
    lower_all = jnp.tile(start_rows, TOPK)
    upper_all = jnp.tile(jnp.arange(group_len, dtype=jnp.int32), TOPK)
    block_rows = min(512, stacked.shape[0])
    blocks = stacked.shape[0] // block_rows
    key_place = jnp.arange(group_len, dtype=jnp.int32)
    scale = HD ** (-0.5)

    def one_block(args):
        query_blk, lower, upper = args
        scores = low_back(jnp.dot(query_blk, key_rows.T, precision=precise)) * scale
        allowed = (key_place[None, :] >= lower[:, None]) & (key_place[None, :] <= upper[:, None])
        scores = jnp.where(allowed, scores, MASKED)
        peak = lax.optimization_barrier(jnp.max(scores, -1, keepdims=True))
        expo = jnp.exp(scores - peak)
        probs = expo / lax.optimization_barrier(jnp.sum(expo, -1, keepdims=True))
        return jnp.dot(low(probs), value_rows, precision=precise)
    result = lax.map(jax.checkpoint(one_block), (stacked.reshape(blocks, block_rows, HD), lower_all.reshape(blocks, block_rows), upper_all.reshape(blocks, block_rows)))
    return result.reshape(TOPK, group_len, HD).transpose(1, 0, 2)

def forward(inputs, attn_weights, ffn_weights, routes, starts):
    total = inputs.shape[0]
    span = E * HD
    weights = low(attn_weights)
    ffn_low = low(ffn_weights)
    w_query = weights[:, :span]
    w_output = weights[:, span:2 * span]
    w_key = weights[:, 2 * span:2 * span + HD]
    w_value = weights[:, 2 * span + HD:2 * span + 2 * HD]
    w_router = weights[:, 2 * span + 2 * HD:2 * span + 2 * HD + E]
    gain_first = weights[:, AC - 2]
    gain_second = weights[:, AC - 1]
    normed = low(layer_norm(inputs, gain_first))
    query_all = jnp.dot(normed, w_query, precision=precise).reshape(total, E, HD)
    query_sel = jnp.take_along_axis(query_all, routes[:, :, None], axis=1)
    query_sel = low(low_back(query_sel))
    key_rows = low(low_back(jnp.dot(normed, w_key, precision=precise)))
    value_rows = low(low_back(jnp.dot(normed, w_value, precision=precise)))
    logits = low_back(jnp.dot(normed, w_router, precision=precise))
    gates = jax.nn.softmax(jnp.take_along_axis(logits, routes, axis=1), axis=-1)
    attended = lax.map(jax.checkpoint(lambda group: attend_group(*group)), (query_sel.reshape(GROUPS, GROUP, TOPK, HD), key_rows.reshape(GROUPS, GROUP, HD), value_rows.reshape(GROUPS, GROUP, HD), starts.reshape(GROUPS, GROUP)))
    attended = low_back(attended.reshape(total, TOPK, HD))
    weighted = gates[:, :, None] * attended
    onehot = (routes[:, :, None] == jnp.arange(E, dtype=jnp.int32)[None, None, :]).astype(jnp.float32)
    combined = low(jnp.einsum('tke,tkh->teh', onehot, weighted, precision=precise).reshape(total, span))
    branch = low_back(jnp.dot(combined, w_output.T, precision=precise))
    middle = inputs + branch
    normed_second = low(layer_norm(middle, gain_second))
    hidden = low_back(jnp.dot(normed_second, ffn_low[0], precision=precise))
    active = low(jax.nn.silu(hidden))
    return middle + jnp.dot(active, ffn_low[1].T, precision=precise)

def rate_columns(rates):
    span = E * HD
    return jnp.concatenate([jnp.full((span,), rates[0]), jnp.full((span,), rates[1]), jnp.full((2 * HD,), rates[2]), jnp.full((E,), rates[3]), jnp.full((2,), rates[4])])

def decay_columns():
    return jnp.concatenate([jnp.full((AC - 2,), WEIGHT_DECAY, jnp.float32), jnp.zeros((2,), jnp.float32)])

def adam_step(param, first, second, grad, rate, decay):
    first_new = BETA_FIRST * first + (1.0 - BETA_FIRST) * grad
    second_new = BETA_SECOND * second + (1.0 - BETA_SECOND) * grad * grad
    first_hat = first_new / (1.0 - BETA_FIRST ** ADAM_STEP)
    second_hat = second_new / (1.0 - BETA_SECOND ** ADAM_STEP)
    param_new = param - rate * (first_hat / (jnp.sqrt(second_hat) + ADAM_EPS) + decay * param)
    return (second_new, param_new)

def reference(tokens, cotangent, routes, starts, attn_param, attn_first, attn_second, ffn_param, ffn_first, ffn_second, rates):
    inputs = tokens.astype(jnp.float32)

    def run(values, attn_weights, ffn_weights):
        return forward(values, attn_weights, ffn_weights, routes, starts)
    result, pull = jax.vjp(run, inputs, attn_param, ffn_param)
    input_grad, attn_raw, ffn_raw = pull(cotangent.astype(jnp.float32))
    grad_norm = jnp.sqrt(jnp.sum(attn_raw * attn_raw) + jnp.sum(ffn_raw * ffn_raw))
    factor = jnp.minimum(1.0, CLIP_NORM / grad_norm)
    attn_grad = attn_raw * factor
    ffn_grad = ffn_raw * factor
    attn_second_new, attn_new = adam_step(attn_param, attn_first, attn_second, attn_grad, rate_columns(rates)[None, :], decay_columns()[None, :])
    ffn_rates = jnp.stack([rates[5], rates[6]])[:, None, None]
    ffn_second_new, ffn_new = adam_step(ffn_param, ffn_first, ffn_second, ffn_grad, ffn_rates, WEIGHT_DECAY)
    gain_grad = attn_grad[:, AC - 2:]
    return (result.astype(jnp.bfloat16), input_grad, attn_grad, attn_second_new, attn_new, ffn_grad, ffn_second_new, ffn_new, grad_norm, gain_grad)
```

```python
import functools
import math

import jax
import jax.numpy as jnp
from jax import lax
from jax.experimental import pallas as pl
from jax.experimental.pallas import tpu as pltpu
from jax.sharding import PartitionSpec as P

HD = 64
E = 24
TOPK = 8
ADAM_STEP = 7
AC = 3226
SPAN = E * HD
PAIRS = E // 2
LANES = 128

NORM_EPS = 1e-05
MASKED = -1e30
CLIP_NORM = 0.1
BETA_FIRST = 0.9
BETA_SECOND = 0.95
ADAM_EPS = 1e-08
WEIGHT_DECAY = 0.1

SCALE = HD ** (-0.5)
LOG2E = math.log2(math.e)
SAFE_SCORE = 40.0
SAFE_VALUE = 1e15
VMEM = 58 << 20

F32 = jnp.float32
BF16 = jnp.bfloat16


def dot(left, right):
    return jnp.dot(left, right, preferred_element_type=F32)


def dot_last(left, right):
    return lax.dot_general(left, right, (((1,), (1,)), ((), ())), preferred_element_type=F32)


def turned(values):
    return values.astype(F32).T.astype(values.dtype)


def standardize(values):
    centred = values - jnp.mean(values, -1, keepdims=True)
    factor = lax.rsqrt(jnp.mean(centred * centred, -1, keepdims=True) + NORM_EPS)
    return (centred * factor, factor)


def norm_back(grad_normal, normal, factor):
    return factor * (
        grad_normal
        - jnp.mean(grad_normal, -1, keepdims=True)
        - normal * jnp.mean(grad_normal * normal, -1, keepdims=True)
    )


def lane_index(rows):
    return lax.broadcasted_iota(jnp.int32, (rows, LANES), 1)


def column(values, index, rows):
    return jnp.broadcast_to(values[:, index : index + 1], (rows, LANES))


def pick_pairs(table, chosen):
    picked = jnp.zeros(chosen.shape, F32)
    for pair in range(PAIRS):
        picked = jnp.where(chosen == 2 * pair, table[:, pair * LANES : (pair + 1) * LANES], picked)
    return picked


def gains_of(tail):
    return tail.astype(F32).T


def pre_kernel(x_ref, routes_ref, w_ref, h_ref, q_ref, kv_ref, gate_ref):
    rows = x_ref.shape[0]
    gain = gains_of(w_ref[:, SPAN + LANES :])[E : E + 1]
    normal, _ = standardize(x_ref[...].astype(F32))
    h = (normal * gain).astype(BF16)
    h_ref[...] = h
    proj = dot(h, w_ref[...])
    kv_ref[...] = proj[:, SPAN : SPAN + LANES].astype(BF16)
    logits = proj[:, SPAN + LANES :]
    routes = routes_ref[...]
    lane = lane_index(rows)
    half = (lane >= HD).astype(jnp.int32)
    chosen = jnp.zeros((rows, LANES), jnp.bool_)
    for slot in range(TOPK):
        route = column(routes, slot, rows)
        q_ref[slot] = pick_pairs(proj, route - half).astype(BF16)
        chosen = chosen | (lane == route)
    peak = jnp.max(jnp.where(chosen, logits, MASKED), -1, keepdims=True)
    expo = jnp.where(chosen, jnp.exp(jnp.where(chosen, logits - peak, 0.0)), 0.0)
    dense = expo / jnp.sum(expo, -1, keepdims=True)
    gates = jnp.zeros((rows, LANES), F32)
    for slot in range(TOPK):
        hit = jnp.where(lane == column(routes, slot, rows), dense, 0.0)
        gates = jnp.where(lane == slot, jnp.sum(hit, -1, keepdims=True), gates)
    gate_ref[...] = gates


def pre_call(x, routes, weights, tile=256):
    rows, width = x.shape
    cols = weights.shape[1]
    return pl.pallas_call(
        pre_kernel,
        grid=(rows // tile,),
        in_specs=[
            pl.BlockSpec((tile, width), lambda i: (i, 0)),
            pl.BlockSpec((tile, TOPK), lambda i: (i, 0)),
            pl.BlockSpec((width, cols), lambda i: (0, 0)),
        ],
        out_specs=[
            pl.BlockSpec((tile, width), lambda i: (i, 0)),
            pl.BlockSpec((TOPK, tile, LANES), lambda i: (0, i, 0)),
            pl.BlockSpec((tile, LANES), lambda i: (i, 0)),
            pl.BlockSpec((tile, LANES), lambda i: (i, 0)),
        ],
        out_shape=[
            jax.ShapeDtypeStruct((rows, width), BF16),
            jax.ShapeDtypeStruct((TOPK, rows, LANES), BF16),
            jax.ShapeDtypeStruct((rows, LANES), BF16),
            jax.ShapeDtypeStruct((rows, LANES), F32),
        ],
        compiler_params=pltpu.CompilerParams(vmem_limit_bytes=VMEM),
        cost_estimate=pl.CostEstimate(
            flops=2 * rows * width * cols, bytes_accessed=8 * rows * width + 2 * width * cols, transcendentals=0
        ),
        name="project",
    )(x, routes, weights)


def spread_keyval(kv_ref, key_ref, value_ref, with_ones):
    block = kv_ref.shape[1]
    devices = kv_ref.shape[0] // 2
    low_half = lane_index(block) < HD
    for index in range(2 * devices):
        place = index // 2 if index % 2 == 0 else 2 * devices - 1 - index // 2
        rows = kv_ref[index].astype(F32)
        rolled = pltpu.roll(rows, HD, 1)
        span = pl.ds(place * block, block)
        key_ref[span, :] = jnp.where(low_half, rows, rolled).astype(BF16)
        value_ref[span, :LANES] = jnp.where(low_half, rolled, rows).astype(BF16)
        if with_ones:
            value_ref[span, LANES:] = jnp.ones((block, LANES), BF16)


def attend_kernel(place_ref, q_ref, kv_ref, o_ref, log_ref, key_ref, value_ref, acc_ref, peak_ref, bound_ref):
    step = pl.program_id(0)
    slots, tile, _ = q_ref.shape
    rows = slots * tile
    width = 512

    @pl.when(step == 0)
    def _():
        spread_keyval(kv_ref, key_ref, value_ref, True)
        keys = key_ref[...].astype(F32)
        bound_ref[0] = jnp.max(jnp.sum(keys * keys, -1, keepdims=True)) * 0.5
        bound_ref[1] = jnp.max(jnp.abs(value_ref[:, :LANES].astype(F32)))

    here = place_ref[0, step]
    lower = place_ref[1, step]
    q = q_ref[...].reshape(rows, LANES)
    qf = q.astype(F32)
    longest = jnp.max(jnp.sum(qf * qf, -1, keepdims=True))
    plain = (longest * bound_ref[0] <= (SAFE_SCORE / SCALE) ** 2) & (bound_ref[1] <= SAFE_VALUE)
    full = (here - lower) // width
    last = pl.multiple_of(lower + full * width, width)
    token = lax.broadcasted_iota(jnp.int32, (tile, width), 0) + here
    allowed = (lax.broadcasted_iota(jnp.int32, (tile, width), 1) + last) <= token
    allowed = jnp.broadcast_to(allowed[None], (slots, tile, width)).reshape(rows, width)

    @pl.when(plain)
    def _():
        expo = jnp.exp2(dot_last(q, key_ref[pl.ds(last, width), :]) * (SCALE * LOG2E))
        expo = jnp.where(allowed, expo, 0.0).astype(BF16)
        acc_ref[...] = dot(expo, value_ref[pl.ds(last, width), :])

        def body(index, carry):
            span = pl.ds(pl.multiple_of(lower + index * width, width), width)
            expo = jnp.exp2(dot_last(q, key_ref[span, :]) * (SCALE * LOG2E)).astype(BF16)
            acc_ref[...] += dot(expo, value_ref[span, :])
            return carry

        lax.fori_loop(0, full, body, 0)
        peak_ref[...] = jnp.zeros_like(peak_ref)

    @pl.when(jnp.logical_not(plain))
    def _():
        def scaled(span):
            return dot_last(q, key_ref[span, :]) * (SCALE * LOG2E)

        scores = jnp.where(allowed, scaled(pl.ds(last, width)), MASKED)
        peak = jnp.max(scores, -1, keepdims=True)
        peak_ref[...] = jnp.broadcast_to(peak, (rows, LANES))
        acc_ref[...] = dot(jnp.exp2(scores - peak).astype(BF16), value_ref[pl.ds(last, width), :])

        def body(index, carry):
            span = pl.ds(pl.multiple_of(lower + index * width, width), width)
            scores = scaled(span)
            before = peak_ref[:, :1]
            peak = jnp.maximum(before, jnp.max(scores, -1, keepdims=True))
            peak_ref[...] = jnp.broadcast_to(peak, (rows, LANES))
            expo = jnp.exp2(scores - peak).astype(BF16)
            acc_ref[...] = acc_ref[...] * jnp.exp2(before - peak) + dot(expo, value_ref[span, :])
            return carry

        lax.fori_loop(0, full, body, 0)

    total = acc_ref[:, LANES:]
    o_ref[...] = (acc_ref[:, :LANES] / total).reshape(slots, tile, LANES)
    logs = (peak_ref[...] + jnp.log2(total)).reshape(slots, tile, LANES)
    lane = lane_index(tile)
    packed = jnp.zeros((tile, LANES), F32)
    for slot in range(slots):
        packed = jnp.where(lane == slot, logs[slot], packed)
    log_ref[...] = packed


def attend_call(place, q, kv, tile=128):
    slots, rows, _ = q.shape
    count = kv.shape[0] * kv.shape[1]
    return pl.pallas_call(
        attend_kernel,
        grid_spec=pltpu.PrefetchScalarGridSpec(
            num_scalar_prefetch=1,
            grid=(rows // tile,),
            in_specs=[
                pl.BlockSpec((slots, tile, LANES), lambda i, s: (0, i, 0)),
                pl.BlockSpec(kv.shape, lambda i, s: (0, 0, 0)),
            ],
            out_specs=[
                pl.BlockSpec((slots, tile, LANES), lambda i, s: (0, i, 0)),
                pl.BlockSpec((tile, LANES), lambda i, s: (i, 0)),
            ],
            scratch_shapes=[
                pltpu.VMEM((count, LANES), BF16),
                pltpu.VMEM((count, 2 * LANES), BF16),
                pltpu.VMEM((slots * tile, 2 * LANES), F32),
                pltpu.VMEM((slots * tile, LANES), F32),
                pltpu.SMEM((2,), F32),
            ],
        ),
        out_shape=[
            jax.ShapeDtypeStruct((slots, rows, LANES), F32),
            jax.ShapeDtypeStruct((rows, LANES), F32),
        ],
        compiler_params=pltpu.CompilerParams(vmem_limit_bytes=VMEM),
        cost_estimate=pl.CostEstimate(
            flops=8 * slots * rows * count * LANES, bytes_accessed=8 * slots * rows * LANES, transcendentals=0
        ),
        name="attend",
    )(place, q, kv)


def attend_back_kernel(
    place_ref, q_ref, do_ref, log_ref, delta_ref, routes_ref, h_ref, dlog_ref, kv_ref, w_ref,
    dh_ref, gq_ref, dkv_ref,
    key_ref, value_ref, dq_ref, dkey_ref, dvalue_ref, all_ref, turn_ref,
):
    step = pl.program_id(0)
    slots, tile, _ = q_ref.shape
    rows = slots * tile
    width = 512

    @pl.when(step == 0)
    def _():
        spread_keyval(kv_ref, key_ref, value_ref, False)
        dkey_ref[...] = jnp.zeros_like(dkey_ref)
        dvalue_ref[...] = jnp.zeros_like(dvalue_ref)

    here = place_ref[0, step]
    lower = place_ref[1, step]
    q = q_ref[...].reshape(rows, LANES)
    do = do_ref[...].reshape(rows, LANES)
    q_turned = turned(q)
    do_turned = turned(do)
    logs = log_ref[...]
    deltas = delta_ref[...]
    logs = jnp.concatenate([column(logs, slot, tile) for slot in range(slots)], 0)
    deltas = jnp.concatenate([column(deltas, slot, tile) for slot in range(slots)], 0)
    full = (here - lower) // width
    last = pl.multiple_of(lower + full * width, width)
    token = lax.broadcasted_iota(jnp.int32, (tile, width), 0) + here
    allowed = (lax.broadcasted_iota(jnp.int32, (tile, width), 1) + last) <= token
    allowed = jnp.broadcast_to(allowed[None], (slots, tile, width)).reshape(rows, width)

    def wide(values):
        return jnp.concatenate([values] * (width // LANES), 1)

    def one(first, masked):
        span = pl.ds(first, width)
        keys = key_ref[span, :]
        scores = dot_last(q, keys)
        probs = jnp.exp2(scores * (SCALE * LOG2E) - wide(logs))
        if masked:
            probs = jnp.where(allowed, probs, 0.0)
        dprobs = dot_last(do, value_ref[span, :])
        dscores = (probs * (dprobs - wide(deltas))).astype(BF16)
        dvalue_ref[:, span] += dot(do_turned, probs.astype(BF16))
        dkey_ref[:, span] += dot(q_turned, dscores)
        return dot(dscores, keys)

    dq_ref[...] = one(last, True)

    def body(index, carry):
        dq_ref[...] += one(pl.multiple_of(lower + index * width, width), False)
        return carry

    lax.fori_loop(0, full, body, 0)

    routes = routes_ref[...]
    half = (lane_index(tile) >= HD).astype(jnp.int32)
    chosen = [column(routes, slot, tile) - half for slot in range(slots)]
    dq = (dq_ref[...] * SCALE).reshape(slots, tile, LANES)
    mine = pl.ds(pl.multiple_of(step * tile, tile), tile)
    for pair in range(PAIRS):
        total = jnp.zeros((tile, LANES), F32)
        for slot in range(slots):
            total = jnp.where(chosen[slot] == 2 * pair, dq[slot], total)
        all_ref[mine, pair * LANES : (pair + 1) * LANES] = total.astype(BF16)
    turn_ref[:, mine] = turned(h_ref[...])
    dh_ref[...] = dot_last(all_ref[mine, :], w_ref[:, :SPAN]) + dot_last(dlog_ref[...], w_ref[:, SPAN + LANES :])

    @pl.when(step == pl.num_programs(0) - 1)
    def _():
        gq_ref[...] = dot(turn_ref[...], all_ref[...]).astype(BF16)
        block = dkv_ref.shape[1]
        devices = dkv_ref.shape[0] // 2
        for index in range(2 * devices):
            place = index // 2 if index % 2 == 0 else 2 * devices - 1 - index // 2
            span = slice(place * block, (place + 1) * block)
            dkeys = (dkey_ref[:HD, span] + dkey_ref[HD:, span]) * SCALE
            dvalues = dvalue_ref[:HD, span] + dvalue_ref[HD:, span]
            dkv_ref[index] = jnp.concatenate([dkeys, dvalues], 0).T.astype(BF16)


def attend_back_call(place, q, do, logs, deltas, routes, h, dlogits, kv, weights, tile=128):
    slots, rows, _ = q.shape
    count = kv.shape[0] * kv.shape[1]
    width = h.shape[1]
    whole = lambda shape: pl.BlockSpec(shape, lambda i, s: (0,) * len(shape))
    by_slot = pl.BlockSpec((slots, tile, LANES), lambda i, s: (0, i, 0))
    by_row = lambda cols: pl.BlockSpec((tile, cols), lambda i, s: (i, 0))
    return pl.pallas_call(
        attend_back_kernel,
        grid_spec=pltpu.PrefetchScalarGridSpec(
            num_scalar_prefetch=1,
            grid=(rows // tile,),
            in_specs=[
                by_slot, by_slot, by_row(LANES), by_row(LANES), by_row(TOPK), by_row(width), by_row(LANES),
                whole(kv.shape), whole(weights.shape),
            ],
            out_specs=[by_row(width), whole((width, SPAN)), whole(kv.shape)],
            scratch_shapes=[
                pltpu.VMEM((count, LANES), BF16),
                pltpu.VMEM((count, LANES), BF16),
                pltpu.VMEM((slots * tile, LANES), F32),
                pltpu.VMEM((LANES, count), F32),
                pltpu.VMEM((LANES, count), F32),
                pltpu.VMEM((rows, SPAN), BF16),
                pltpu.VMEM((width, rows), BF16),
            ],
        ),
        out_shape=[
            jax.ShapeDtypeStruct((rows, width), F32),
            jax.ShapeDtypeStruct((width, SPAN), BF16),
            jax.ShapeDtypeStruct(kv.shape, BF16),
        ],
        compiler_params=pltpu.CompilerParams(vmem_limit_bytes=VMEM),
        cost_estimate=pl.CostEstimate(
            flops=10 * slots * rows * count * LANES, bytes_accessed=8 * slots * rows * LANES, transcendentals=0
        ),
        name="attend_back",
    )(place, q, do, logs, deltas, routes, h, dlogits, kv, weights)


def middle_kernel(
    x_ref, dy_ref, o_ref, gate_ref, routes_ref, tail_ref, wo_ref, w1_ref, w2_ref,
    out_ref, dmid_ref, do_ref, delta_ref, dlog_ref, g1_ref, g2_ref, go_ref, gain_ref,
    s1_ref, s2_ref, so_ref,
):
    step = pl.program_id(0)
    tile = x_ref.shape[0]
    gain = gains_of(tail_ref[...])[E + 1 : E + 2]
    routes = routes_ref[...]
    gates = gate_ref[...]
    lane = lane_index(tile)
    half = (lane >= HD).astype(jnp.int32)
    chosen = [column(routes, slot, tile) - half for slot in range(TOPK)]
    weighted = [column(gates, slot, tile) * o_ref[slot] for slot in range(TOPK)]
    parts = []
    for pair in range(PAIRS):
        total = jnp.zeros((tile, LANES), F32)
        for slot in range(TOPK):
            total = jnp.where(chosen[slot] == 2 * pair, weighted[slot], total)
        parts.append(total.astype(BF16))
    combined = jnp.concatenate(parts, 1)
    mid = x_ref[...].astype(F32) + dot_last(combined, wo_ref[...])
    normal, factor = standardize(mid)
    h2 = (normal * gain).astype(BF16)
    pre = dot(h2, w1_ref[...])
    sigma = jax.nn.sigmoid(pre)
    act = (pre * sigma).astype(BF16)
    out_ref[...] = (mid + dot_last(act, w2_ref[...])).astype(BF16)
    dy = dy_ref[...]
    dact = dot(dy, w2_ref[...])
    dpre = (dact * (sigma * (1.0 + pre * (1.0 - sigma)))).astype(BF16)
    dh2 = dot_last(dpre, w1_ref[...])
    dmid = dy.astype(F32) + norm_back(dh2 * gain, normal, factor)
    dmid_ref[...] = dmid
    dmid_b = dmid.astype(BF16)
    dcomb = dot(dmid_b, wo_ref[...])
    p1 = dot(turned(h2), dpre)
    p2 = dot(turned(dy), act)
    po = dot(turned(dmid_b), combined)
    pg = jnp.sum(dh2 * normal, 0, keepdims=True)

    @pl.when(step == 0)
    def _():
        s1_ref[...] = p1
        s2_ref[...] = p2
        so_ref[...] = po
        gain_ref[...] = pg

    @pl.when(step > 0)
    def _():
        s1_ref[...] += p1
        s2_ref[...] += p2
        so_ref[...] += po
        gain_ref[...] += pg

    weighted_total = jnp.zeros((tile, 1), F32)
    gate_grads = []
    deltas = jnp.zeros((tile, LANES), F32)
    for slot in range(TOPK):
        picked = pick_pairs(dcomb, chosen[slot])
        o = o_ref[slot]
        gate = column(gates, slot, tile)
        do = (gate * picked).astype(BF16)
        do_ref[slot] = do
        deltas = jnp.where(lane == slot, jnp.sum(o * do.astype(F32), -1, keepdims=True), deltas)
        gate_grad = jnp.sum(o * picked, -1, keepdims=True)
        gate_grads.append(gate_grad)
        weighted_total = weighted_total + gates[:, slot : slot + 1] * gate_grad
    delta_ref[...] = deltas
    dlogits = jnp.zeros((tile, LANES), F32)
    for slot in range(TOPK):
        dsel = gates[:, slot : slot + 1] * (gate_grads[slot] - weighted_total)
        dlogits = jnp.where(lane == column(routes, slot, tile), dsel, dlogits)
    dlog_ref[...] = dlogits.astype(BF16)

    @pl.when(step == pl.num_programs(0) - 1)
    def _():
        g1_ref[...] = s1_ref[...].astype(BF16)
        g2_ref[...] = s2_ref[...].astype(BF16)
        go_ref[...] = so_ref[...].astype(BF16)


def middle_call(x, dy, o, gates, routes, tail, wo, w1, w2, tile=256):
    rows, width = x.shape
    hidden = w1.shape[1]
    whole = lambda shape: pl.BlockSpec(shape, lambda i: (0,) * len(shape))
    by_slot = pl.BlockSpec((TOPK, tile, LANES), lambda i: (0, i, 0))
    by_row = lambda cols: pl.BlockSpec((tile, cols), lambda i: (i, 0))
    return pl.pallas_call(
        middle_kernel,
        grid=(rows // tile,),
        in_specs=[
            by_row(width), by_row(width), by_slot, by_row(LANES), by_row(TOPK),
            whole(tail.shape), whole(wo.shape), whole(w1.shape), whole(w2.shape),
        ],
        out_specs=[
            by_row(width), by_row(width), by_slot, by_row(LANES), by_row(LANES),
            whole((width, hidden)), whole((width, hidden)), whole((width, SPAN)), whole((1, width)),
        ],
        out_shape=[
            jax.ShapeDtypeStruct((rows, width), BF16),
            jax.ShapeDtypeStruct((rows, width), F32),
            jax.ShapeDtypeStruct((TOPK, rows, LANES), BF16),
            jax.ShapeDtypeStruct((rows, LANES), F32),
            jax.ShapeDtypeStruct((rows, LANES), BF16),
            jax.ShapeDtypeStruct((width, hidden), BF16),
            jax.ShapeDtypeStruct((width, hidden), BF16),
            jax.ShapeDtypeStruct((width, SPAN), BF16),
            jax.ShapeDtypeStruct((1, width), F32),
        ],
        scratch_shapes=[
            pltpu.VMEM((width, hidden), F32),
            pltpu.VMEM((width, hidden), F32),
            pltpu.VMEM((width, SPAN), F32),
        ],
        compiler_params=pltpu.CompilerParams(vmem_limit_bytes=VMEM),
        cost_estimate=pl.CostEstimate(
            flops=2 * rows * width * (6 * hidden + 3 * SPAN), bytes_accessed=16 * rows * width, transcendentals=0
        ),
        name="middle",
    )(x, dy, o, gates, routes, tail, wo, w1, w2)


def post_kernel(x_ref, h_ref, dmid_ref, dh_ref, dkv_ref, dlog_ref, gain2_ref, w_ref, grad_ref, gk_ref):
    gain = gains_of(w_ref[:, LANES:])[E : E + 1]
    normal, factor = standardize(x_ref[...].astype(F32))
    dkv = dkv_ref[...]
    dh = dh_ref[...] + dot_last(dkv, w_ref[:, :LANES])
    grad_ref[...] = (dmid_ref[...] + norm_back(dh * gain, normal, factor)).astype(grad_ref.dtype)
    gain1 = jnp.sum(dh * normal, 0, keepdims=True)
    width = gain1.shape[1]
    row = lax.broadcasted_iota(jnp.int32, (LANES, width), 0)
    gains = jnp.where(row == E, gain1, jnp.where(row == E + 1, gain2_ref[...], 0.0))
    h_turned = turned(h_ref[...])
    gk_ref[:, :LANES] = dot(h_turned, dkv).astype(BF16)
    gk_ref[:, LANES:] = (dot(h_turned, dlog_ref[...]) + gains.T).astype(BF16)


def post_call(x, h, dmid, dh, dkv, dlogits, gain2, weights):
    rows, width = x.shape
    return pl.pallas_call(
        post_kernel,
        out_shape=[
            jax.ShapeDtypeStruct((rows, width), BF16),
            jax.ShapeDtypeStruct((width, 2 * LANES), BF16),
        ],
        compiler_params=pltpu.CompilerParams(vmem_limit_bytes=VMEM),
        cost_estimate=pl.CostEstimate(
            flops=6 * rows * width * LANES, bytes_accessed=16 * rows * width, transcendentals=0
        ),
        name="finish",
    )(x, h, dmid, dh, dkv, dlogits, gain2, weights)


RING = ((0, 1), (1, 2), (2, 3), (3, 0))
SWAP = ((1, 3), (3, 1))


def deal(rows, place):
    half = rows.shape[0] // 2
    outer = (place == 0) | (place == 3)
    first = lax.dynamic_slice_in_dim(rows, jnp.where(outer, half, 0), half, 0)
    second = lax.dynamic_slice_in_dim(rows, jnp.where(place == 1, half, 0), half, 0)
    ring = lax.ppermute(first, "mp", RING)
    swap = lax.ppermute(second, "mp", SWAP)
    low = jnp.where(place == 0, rows[:half], jnp.where(place == 3, swap, ring))
    high = jnp.where(place == 2, rows[half:], jnp.where(place == 1, swap, ring))
    return jnp.concatenate([low, high], 0)


def gather_back(rows, place):
    half = rows.shape[0] // 2
    outer = (place == 0) | (place == 3)
    first = lax.dynamic_slice_in_dim(rows, jnp.where(outer, half, 0), half, 0)
    second = lax.dynamic_slice_in_dim(rows, jnp.where(place == 1, half, 0), half, 0)
    ring = lax.ppermute(first, "mp", tuple((b, a) for a, b in RING))
    swap = lax.ppermute(second, "mp", SWAP)
    top = jnp.where(place == 0, rows[:half], jnp.where(place == 3, swap, ring))
    bottom = jnp.where(place == 2, rows[half:], jnp.where(place == 1, swap, ring))
    return jnp.concatenate([top, bottom], 0)


def rate_columns(rates):
    return jnp.concatenate(
        [
            jnp.full((SPAN,), rates[0]),
            jnp.full((SPAN,), rates[1]),
            jnp.full((2 * HD,), rates[2]),
            jnp.full((E,), rates[3]),
            jnp.full((2,), rates[4]),
        ]
    )


def decay_columns():
    return jnp.concatenate([jnp.full((AC - 2,), WEIGHT_DECAY, F32), jnp.zeros((2,), F32)])


def adam_step(param, first, second, grad, rate, decay):
    first_new = BETA_FIRST * first + (1.0 - BETA_FIRST) * grad
    second_new = BETA_SECOND * second + (1.0 - BETA_SECOND) * grad * grad
    first_hat = first_new / (1.0 - BETA_FIRST**ADAM_STEP)
    second_hat = second_new / (1.0 - BETA_SECOND**ADAM_STEP)
    param_new = param - rate * (first_hat / (jnp.sqrt(second_hat) + ADAM_EPS) + decay * param)
    return (second_new, param_new)


ALL = ("dp", "mp")


def shards(
    tokens, cotangent, routes, starts, attn_param, attn_first, attn_second, ffn_param, ffn_first, ffn_second, rates
):
    local_rows, width = tokens.shape
    place = lax.axis_index("mp")
    devices = lax.axis_size("mp")
    groups = lax.axis_size("dp")
    block = local_rows // 2

    attn_b = attn_param.astype(BF16)
    pad = jnp.zeros((attn_b.shape[0], 2 * LANES - (AC - 2 * SPAN)), BF16)
    front = jnp.concatenate([attn_b[:, :SPAN], attn_b[:, 2 * SPAN :], pad], 1)
    front_full = lax.all_gather(front, ALL, axis=0, tiled=True)
    wo_full = lax.all_gather(attn_b[:, SPAN : 2 * SPAN], ALL, axis=0, tiled=True)
    ffn_all = lax.all_gather(ffn_param.astype(BF16), ALL, axis=0, tiled=False)
    _, depth, cols = ffn_param.shape
    ffn_all = ffn_all.reshape(groups, devices, 2, depth, cols).transpose(2, 0, 3, 1, 4)
    ffn_all = ffn_all.reshape(2, groups * depth, devices * cols)

    x = deal(tokens, place)
    dy = deal(cotangent, place)
    marks = deal(jnp.concatenate([routes, starts[:, None]], 1), place)
    routes_x = marks[:, :TOPK]
    tile = 128
    tiles = local_rows // tile
    index = jnp.arange(tiles, dtype=jnp.int32)
    low = index < tiles // 2
    here = jnp.where(low, place * block + index * tile, (2 * devices - 1 - place) * block + (index - tiles // 2) * tile)
    lower = jnp.where(low, marks[0, TOPK], marks[block, TOPK])
    where = jnp.stack([here.astype(jnp.int32), lower.astype(jnp.int32)])

    h, q, kv, gates = pre_call(x, routes_x, front_full)
    kv_all = lax.all_gather(kv, "mp", axis=0, tiled=True).reshape(2 * devices, block, LANES)
    o, logs = attend_call(where, q, kv_all, tile)
    tail = front_full[:, SPAN + LANES :]
    out, dmid, do, deltas, dlogits, g1, g2, go, gain2 = middle_call(
        x, dy, o, gates, routes_x, tail, wo_full, ffn_all[0], ffn_all[1]
    )
    layer_out = gather_back(out, place)
    dh, gq, dkv = attend_back_call(where, q, do, logs, deltas, routes_x, h, dlogits, kv_all, front_full, tile)
    dkv = lax.psum_scatter(dkv.reshape(devices * local_rows, LANES), "mp", scatter_dimension=0, tiled=True)
    grad, gk = post_call(x, h, dmid, dh, dkv, dlogits, gain2, front_full[:, SPAN:])
    input_grad = gather_back(grad, place).astype(F32)

    ffn_local = jnp.stack([g1, g2]).reshape(2, groups, depth, devices, cols).transpose(1, 3, 0, 2, 4)
    ffn_local = ffn_local.reshape(groups * devices * 2 * depth, cols)
    ffn_raw = lax.psum_scatter(ffn_local, ALL, scatter_dimension=0, tiled=True).astype(F32).reshape(2, depth, cols)
    go_raw = lax.psum_scatter(go, ALL, scatter_dimension=0, tiled=True).astype(F32)
    gq_raw = lax.psum_scatter(jnp.concatenate([gq, gk], 1), ALL, scatter_dimension=0, tiled=True).astype(F32)
    attn_raw = jnp.concatenate([gq_raw[:, :SPAN], go_raw, gq_raw[:, SPAN : SPAN + AC - 2 * SPAN]], 1)

    squares = jnp.sum(attn_raw * attn_raw) + jnp.sum(ffn_raw * ffn_raw)
    grad_norm = jnp.sqrt(lax.psum(squares, ALL))
    factor = jnp.minimum(1.0, CLIP_NORM / grad_norm)
    attn_grad = attn_raw * factor
    ffn_grad = ffn_raw * factor
    attn_second_new, attn_new = adam_step(
        attn_param, attn_first, attn_second, attn_grad, rate_columns(rates)[None, :], decay_columns()[None, :]
    )
    ffn_rates = jnp.stack([rates[5], rates[6]])[:, None, None]
    ffn_second_new, ffn_new = adam_step(ffn_param, ffn_first, ffn_second, ffn_grad, ffn_rates, WEIGHT_DECAY)
    return (
        layer_out,
        input_grad,
        attn_grad,
        attn_second_new,
        attn_new,
        ffn_grad,
        ffn_second_new,
        ffn_new,
        grad_norm,
        attn_grad[:, AC - 2 :],
    )


def solution(mesh):
    by_row = P(ALL, None)
    by_ffn = P(None, "dp", "mp")
    return jax.shard_map(
        shards,
        mesh=mesh,
        in_specs=(by_row, by_row, by_row, P(ALL), by_row, by_row, by_row, by_ffn, by_ffn, by_ffn, P()),
        out_specs=(by_row, by_row, by_row, by_row, by_row, by_ffn, by_ffn, by_ffn, P(), by_row),
        check_vma=False,
    )
```

```python
import functools
import math

import jax
import jax.numpy as jnp
from jax import lax
from jax.experimental import pallas as pl
from jax.experimental.pallas import tpu as pltpu
from jax.sharding import PartitionSpec as P

HD = 64
E = 24
TOPK = 8
ADAM_STEP = 7
AC = 3226
SPAN = E * HD
PAIRS = E // 2
LANES = 128

NORM_EPS = 1e-05
MASKED = -1e30
CLIP_NORM = 0.1
BETA_FIRST = 0.9
BETA_SECOND = 0.95
ADAM_EPS = 1e-08
WEIGHT_DECAY = 0.1

SCALE = HD ** (-0.5)
LOG2E = math.log2(math.e)
SAFE_SCORE = 40.0
SAFE_VALUE = 1e15
VMEM = 58 << 20

F32 = jnp.float32
BF16 = jnp.bfloat16


def dot(left, right):
    return jnp.dot(left, right, preferred_element_type=F32)


def dot_last(left, right):
    return lax.dot_general(left, right, (((1,), (1,)), ((), ())), preferred_element_type=F32)


def turned(values):
    return values.astype(F32).T.astype(values.dtype)


def standardize(values):
    centred = values - jnp.mean(values, -1, keepdims=True)
    factor = lax.rsqrt(jnp.mean(centred * centred, -1, keepdims=True) + NORM_EPS)
    return (centred * factor, factor)


def norm_back(grad_normal, normal, factor):
    return factor * (
        grad_normal
        - jnp.mean(grad_normal, -1, keepdims=True)
        - normal * jnp.mean(grad_normal * normal, -1, keepdims=True)
    )


def lane_index(rows):
    return lax.broadcasted_iota(jnp.int32, (rows, LANES), 1)


def column(values, index, rows):
    return jnp.broadcast_to(values[:, index : index + 1], (rows, LANES))


def pick_pairs(table, chosen):
    picked = jnp.zeros(chosen.shape, F32)
    for pair in range(PAIRS):
        picked = jnp.where(chosen == 2 * pair, table[:, pair * LANES : (pair + 1) * LANES], picked)
    return picked


def gains_of(tail):
    return tail.astype(F32).T


def flat_of(index):
    x, y, z = index // 8, index // 4 % 2, index % 4
    return ((z * 2 + y) * 2 + x) * 2


def pre_kernel(me_ref, x_ref, routes_ref, near_ref, far_ref, h_ref, q_ref, kv_ref, gate_ref, w_ref, sems):
    rows = x_ref.shape[0]
    pieces, piece, _ = near_ref.shape

    @pl.when(pl.program_id(0) == 0)
    def _():
        copies = []
        for core, part in enumerate((near_ref, far_ref)):
            for index in range(pieces):
                owner = me_ref[0] ^ (flat_of(index) + core)
                first = pl.multiple_of(owner * piece, piece)
                copies.append(
                    pltpu.make_async_copy(
                        part.at[index], w_ref.at[pl.ds(first, piece), :], sems.at[core * pieces + index]
                    )
                )
        for copy in copies:
            copy.start()
        for copy in copies:
            copy.wait()

    gain = gains_of(w_ref[:, SPAN + LANES :])[E : E + 1]
    normal, _ = standardize(x_ref[...].astype(F32))
    h = (normal * gain).astype(BF16)
    h_ref[...] = h
    proj = dot(h, w_ref[...])
    kv_ref[...] = proj[:, SPAN : SPAN + LANES].astype(BF16)
    logits = proj[:, SPAN + LANES :]
    routes = routes_ref[...]
    lane = lane_index(rows)
    half = (lane >= HD).astype(jnp.int32)
    chosen = jnp.zeros((rows, LANES), jnp.bool_)
    for slot in range(TOPK):
        route = column(routes, slot, rows)
        q_ref[slot] = pick_pairs(proj, route - half).astype(BF16)
        chosen = chosen | (lane == route)
    peak = jnp.max(jnp.where(chosen, logits, MASKED), -1, keepdims=True)
    expo = jnp.where(chosen, jnp.exp(jnp.where(chosen, logits - peak, 0.0)), 0.0)
    dense = expo / jnp.sum(expo, -1, keepdims=True)
    gates = jnp.zeros((rows, LANES), F32)
    for slot in range(TOPK):
        hit = jnp.where(lane == column(routes, slot, rows), dense, 0.0)
        gates = jnp.where(lane == slot, jnp.sum(hit, -1, keepdims=True), gates)
    gate_ref[...] = gates


def pre_call(me, x, routes, near, far, tile=256):
    rows, width = x.shape
    pieces, piece, cols = near.shape
    by_row = lambda count: pl.BlockSpec((tile, count), lambda i, s: (i, 0))
    return pl.pallas_call(
        pre_kernel,
        grid_spec=pltpu.PrefetchScalarGridSpec(
            num_scalar_prefetch=1,
            grid=(rows // tile,),
            in_specs=[
                by_row(width),
                by_row(TOPK),
                pl.BlockSpec(memory_space=pl.ANY),
                pl.BlockSpec(memory_space=pl.ANY),
            ],
            out_specs=[
                by_row(width),
                pl.BlockSpec((TOPK, tile, LANES), lambda i, s: (0, i, 0)),
                by_row(LANES),
                by_row(LANES),
                pl.BlockSpec((width, cols), lambda i, s: (0, 0)),
            ],
            scratch_shapes=[pltpu.SemaphoreType.DMA((2 * pieces,))],
        ),
        out_shape=[
            jax.ShapeDtypeStruct((rows, width), BF16),
            jax.ShapeDtypeStruct((TOPK, rows, LANES), BF16),
            jax.ShapeDtypeStruct((rows, LANES), BF16),
            jax.ShapeDtypeStruct((rows, LANES), F32),
            jax.ShapeDtypeStruct((width, cols), BF16),
        ],
        compiler_params=pltpu.CompilerParams(vmem_limit_bytes=VMEM),
        cost_estimate=pl.CostEstimate(
            flops=2 * rows * width * cols, bytes_accessed=8 * rows * width + 2 * width * cols, transcendentals=0
        ),
        name="project",
    )(me, x, routes, near, far)


def spread_keyval(device, kv_ref, key_ref, value_ref):
    devices, _, block, _ = kv_ref.shape
    low_half = lane_index(block) < HD
    for index in range(devices):
        for high in range(2):
            rows = kv_ref[index, high].astype(F32)
            rolled = pltpu.roll(rows, HD, 1)
            span = block_of(device ^ index, high, devices, block)
            key_ref[span, :] = jnp.where(low_half, rows, rolled).astype(BF16)
            value_ref[span, :] = jnp.where(low_half, rolled, rows).astype(BF16)


def block_of(device, high, devices, block):
    place = 2 * devices - 1 - device if high else device
    return pl.ds(pl.multiple_of(place * block, block), block)


def attend_kernel(place_ref, q_ref, kv_ref, o_ref, log_ref, key_ref, plain_ref, value_ref, acc_ref, peak_ref, bound_ref):
    step = pl.program_id(0)
    slots, tile, _ = q_ref.shape
    rows = slots * tile
    width = 512

    @pl.when(step == 0)
    def _():
        spread_keyval(place_ref[2, 0], kv_ref, key_ref, plain_ref)
        value_ref[:, :LANES] = plain_ref[...]
        value_ref[:, LANES:] = jnp.ones((value_ref.shape[0], LANES), BF16)
        keys = key_ref[...].astype(F32)
        bound_ref[0] = jnp.max(jnp.sum(keys * keys, -1, keepdims=True)) * 0.5
        bound_ref[1] = jnp.max(jnp.abs(plain_ref[...].astype(F32)))

    here = place_ref[0, step]
    lower = place_ref[1, step]
    q = q_ref[...].reshape(rows, LANES)
    qf = q.astype(F32)
    longest = jnp.max(jnp.sum(qf * qf, -1, keepdims=True))
    plain = (longest * bound_ref[0] <= (SAFE_SCORE / SCALE) ** 2) & (bound_ref[1] <= SAFE_VALUE)
    full = (here - lower) // width
    last = pl.multiple_of(lower + full * width, width)
    token = lax.broadcasted_iota(jnp.int32, (tile, width), 0) + here
    allowed = (lax.broadcasted_iota(jnp.int32, (tile, width), 1) + last) <= token
    allowed = jnp.broadcast_to(allowed[None], (slots, tile, width)).reshape(rows, width)

    @pl.when(plain)
    def _():
        expo = jnp.exp2(dot_last(q, key_ref[pl.ds(last, width), :]) * (SCALE * LOG2E))
        expo = jnp.where(allowed, expo, 0.0).astype(BF16)
        acc_ref[...] = dot(expo, value_ref[pl.ds(last, width), :])

        def body(index, carry):
            span = pl.ds(pl.multiple_of(lower + index * width, width), width)
            expo = jnp.exp2(dot_last(q, key_ref[span, :]) * (SCALE * LOG2E)).astype(BF16)
            acc_ref[...] += dot(expo, value_ref[span, :])
            return carry

        lax.fori_loop(0, full, body, 0)
        peak_ref[...] = jnp.zeros_like(peak_ref)

    @pl.when(jnp.logical_not(plain))
    def _():
        def scaled(span):
            return dot_last(q, key_ref[span, :]) * (SCALE * LOG2E)

        scores = jnp.where(allowed, scaled(pl.ds(last, width)), MASKED)
        peak = jnp.max(scores, -1, keepdims=True)
        peak_ref[...] = jnp.broadcast_to(peak, (rows, LANES))
        acc_ref[...] = dot(jnp.exp2(scores - peak).astype(BF16), value_ref[pl.ds(last, width), :])

        def body(index, carry):
            span = pl.ds(pl.multiple_of(lower + index * width, width), width)
            scores = scaled(span)
            before = peak_ref[:, :1]
            peak = jnp.maximum(before, jnp.max(scores, -1, keepdims=True))
            peak_ref[...] = jnp.broadcast_to(peak, (rows, LANES))
            expo = jnp.exp2(scores - peak).astype(BF16)
            acc_ref[...] = acc_ref[...] * jnp.exp2(before - peak) + dot(expo, value_ref[span, :])
            return carry

        lax.fori_loop(0, full, body, 0)

    total = acc_ref[:, LANES:]
    o_ref[...] = (acc_ref[:, :LANES] / total).reshape(slots, tile, LANES)
    logs = (peak_ref[...] + jnp.log2(total)).reshape(slots, tile, LANES)
    lane = lane_index(tile)
    packed = jnp.zeros((tile, LANES), F32)
    for slot in range(slots):
        packed = jnp.where(lane == slot, logs[slot], packed)
    log_ref[...] = packed


def attend_call(place, q, kv, tile=128):
    slots, rows, _ = q.shape
    count = kv.shape[0] * kv.shape[1] * kv.shape[2]
    return pl.pallas_call(
        attend_kernel,
        grid_spec=pltpu.PrefetchScalarGridSpec(
            num_scalar_prefetch=1,
            grid=(rows // tile,),
            in_specs=[
                pl.BlockSpec((slots, tile, LANES), lambda i, s: (0, i, 0)),
                pl.BlockSpec(kv.shape, lambda i, s: (0, 0, 0, 0)),
            ],
            out_specs=[
                pl.BlockSpec((slots, tile, LANES), lambda i, s: (0, i, 0)),
                pl.BlockSpec((tile, LANES), lambda i, s: (i, 0)),
                pl.BlockSpec((count, LANES), lambda i, s: (0, 0)),
                pl.BlockSpec((count, LANES), lambda i, s: (0, 0)),
            ],
            scratch_shapes=[
                pltpu.VMEM((count, 2 * LANES), BF16),
                pltpu.VMEM((slots * tile, 2 * LANES), F32),
                pltpu.VMEM((slots * tile, LANES), F32),
                pltpu.SMEM((2,), F32),
            ],
        ),
        out_shape=[
            jax.ShapeDtypeStruct((slots, rows, LANES), F32),
            jax.ShapeDtypeStruct((rows, LANES), F32),
            jax.ShapeDtypeStruct((count, LANES), BF16),
            jax.ShapeDtypeStruct((count, LANES), BF16),
        ],
        compiler_params=pltpu.CompilerParams(vmem_limit_bytes=VMEM),
        cost_estimate=pl.CostEstimate(
            flops=8 * slots * rows * count * LANES, bytes_accessed=8 * slots * rows * LANES, transcendentals=0
        ),
        name="attend",
    )(place, q, kv)


def attend_back_kernel(first, final, groups, *refs):
    refs = list(refs)
    take = lambda count: [refs.pop(0) for _ in range(count)]
    place_ref, q_ref, do_ref, log_ref, delta_ref, routes_ref, dlog_ref, key_ref, value_ref, w_ref = take(10)
    if not first:
        dkey_in, dvalue_in = take(2)
    if final:
        h_ref, before_ref = take(2)
    dh_ref, all_ref = take(2)
    if final:
        outs = take(4)
    else:
        outs = take(2)
    dq_ref, dkey_ref, dvalue_ref, sems = take(4)
    step = pl.program_id(0)
    steps = pl.num_programs(0)
    slots, tile, _ = q_ref.shape
    rows = slots * tile
    width = 512

    @pl.when(step == 0)
    def _():
        if first:
            dkey_ref[...] = jnp.zeros_like(dkey_ref)
            dvalue_ref[...] = jnp.zeros_like(dvalue_ref)
        else:
            copies = [
                pltpu.make_async_copy(dkey_in, dkey_ref, sems.at[0]),
                pltpu.make_async_copy(dvalue_in, dvalue_ref, sems.at[1]),
            ]
            for copy in copies:
                copy.start()
            for copy in copies:
                copy.wait()

    here = place_ref[0, step]
    lower = place_ref[1, step]
    q = q_ref[...].reshape(rows, LANES)
    do = do_ref[...].reshape(rows, LANES)
    q_turned = turned(q)
    do_turned = turned(do)
    logs = log_ref[...]
    deltas = delta_ref[...]
    logs = jnp.concatenate([column(logs, slot, tile) for slot in range(slots)], 0)
    deltas = jnp.concatenate([column(deltas, slot, tile) for slot in range(slots)], 0)
    full = (here - lower) // width
    last = pl.multiple_of(lower + full * width, width)
    token = lax.broadcasted_iota(jnp.int32, (tile, width), 0) + here
    allowed = (lax.broadcasted_iota(jnp.int32, (tile, width), 1) + last) <= token
    allowed = jnp.broadcast_to(allowed[None], (slots, tile, width)).reshape(rows, width)

    def wide(values):
        return jnp.concatenate([values] * (width // LANES), 1)

    def one(start, masked):
        span = pl.ds(start, width)
        keys = key_ref[span, :]
        scores = dot_last(q, keys)
        probs = jnp.exp2(scores * (SCALE * LOG2E) - wide(logs))
        if masked:
            probs = jnp.where(allowed, probs, 0.0)
        dprobs = dot_last(do, value_ref[span, :])
        dscores = (probs * (dprobs - wide(deltas))).astype(BF16)
        dvalue_ref[:, span] += dot(do_turned, probs.astype(BF16))
        dkey_ref[:, span] += dot(q_turned, dscores)
        return dot(dscores, keys)

    dq_ref[...] = one(last, True)

    def body(index, carry):
        dq_ref[...] += one(pl.multiple_of(lower + index * width, width), False)
        return carry

    lax.fori_loop(0, full, body, 0)

    routes = routes_ref[...]
    half = (lane_index(tile) >= HD).astype(jnp.int32)
    chosen = [column(routes, slot, tile) - half for slot in range(slots)]
    dq = (dq_ref[...] * SCALE).reshape(slots, tile, LANES)
    mine = pl.ds(pl.multiple_of(step * tile, tile), tile)
    for pair in range(PAIRS):
        total = jnp.zeros((tile, LANES), F32)
        for slot in range(slots):
            total = jnp.where(chosen[slot] == 2 * pair, dq[slot], total)
        all_ref[mine, pair * LANES : (pair + 1) * LANES] = total.astype(BF16)
    dh_ref[0] = dot_last(all_ref[mine, :], w_ref[:, :SPAN]) + dot_last(dlog_ref[...], w_ref[:, SPAN + LANES :])

    @pl.when(step == steps - 1)
    def _():
        if not final:
            copies = [
                pltpu.make_async_copy(dkey_ref, outs[0], sems.at[0]),
                pltpu.make_async_copy(dvalue_ref, outs[1], sems.at[1]),
            ]
            for copy in copies:
                copy.start()
            for copy in copies:
                copy.wait()
            return
        kv_keep, kv_send, gq_keep, gq_send = outs
        _, _, block, _ = kv_keep.shape
        device = place_ref[2, 0]
        for index in range(4):
            target = kv_send if index % 2 else kv_keep
            for high in range(2):
                span = block_of(device ^ index, high, 4, block)
                dkeys = (dkey_ref[:HD, span] + dkey_ref[HD:, span]) * SCALE
                dvalues = dvalue_ref[:HD, span] + dvalue_ref[HD:, span]
                target[index // 2, high] = jnp.concatenate([dkeys, dvalues], 0).T.astype(BF16)
        gq = dot(turned(h_ref[...].reshape(-1, h_ref.shape[-1])), before_rows(before_ref, all_ref, tile))
        if groups == 8:
            scatter_rows(gq, gq_keep, gq_send, device % 2)
        else:
            gq_keep[...] = gq.astype(BF16)
            gq_send[...] = jnp.zeros_like(gq_send)


def before_rows(before_ref, all_ref, tile):
    rows = [before_ref[index, :tile] for index in range(before_ref.shape[0])] + [all_ref[:tile]]
    rows += [before_ref[index, tile:] for index in range(before_ref.shape[0])] + [all_ref[tile:]]
    return jnp.concatenate(rows, 0)


def scatter_rows(grad, keep, send, core):
    for x in range(2):
        for y in range(2):
            for z in range(4):
                base = (((z * 2 + y) * 2 + x) * 2) * 16
                low = grad[base : base + 16].astype(BF16)
                high = grad[base + 16 : base + 32].astype(BF16)
                keep[y, z, x] = jnp.where(core == 0, low, high)
                send[y, z, x] = jnp.where(core == 0, high, low)


def attend_back_call(piece, pieces, groups, where, q, do, logs, deltas, routes, dlogits, keys, values, weights, carried, extra):
    slots, rows, _ = q.shape
    count = keys.shape[0]
    width = weights.shape[0]
    tile = rows // (2 * pieces)
    first, final = piece == 0, piece == pieces - 1
    whole = lambda shape: pl.BlockSpec(shape, lambda i, s: (0,) * len(shape))
    anywhere = pl.BlockSpec(memory_space=pl.ANY)
    by_slot = pl.BlockSpec((slots, tile, LANES), lambda i, s: (0, piece + pieces * i, 0))
    by_row = lambda cols: pl.BlockSpec((tile, cols), lambda i, s: (piece + pieces * i, 0))
    in_specs = [
        by_slot, by_slot, by_row(LANES), by_row(LANES), by_row(TOPK), by_row(LANES),
        whole(keys.shape), whole(values.shape), whole(weights.shape),
    ]
    in_specs += [anywhere] * len(carried)
    in_specs += [whole(array.shape) for array in extra]
    out_specs = [pl.BlockSpec((1, tile, width), lambda i, s: (i, 0, 0)), whole((2 * tile, SPAN))]
    out_shape = [
        jax.ShapeDtypeStruct((2, tile, width), F32),
        jax.ShapeDtypeStruct((2 * tile, SPAN), BF16),
    ]
    if final:
        kv_shape = (2, 2, rows // 2, LANES)
        gq_shape = (2, 4, 2, 16, SPAN) if groups == 8 else (width, SPAN)
        off_shape = gq_shape if groups == 8 else (8, LANES)
        for shape in (kv_shape, kv_shape, gq_shape, off_shape):
            out_specs.append(whole(shape))
            out_shape.append(jax.ShapeDtypeStruct(shape, BF16))
    else:
        out_specs += [anywhere] * 2
        out_shape += [jax.ShapeDtypeStruct((LANES, count), F32)] * 2
    return pl.pallas_call(
        functools.partial(attend_back_kernel, first, final, groups),
        grid_spec=pltpu.PrefetchScalarGridSpec(
            num_scalar_prefetch=1,
            grid=(2,),
            in_specs=in_specs,
            out_specs=out_specs,
            scratch_shapes=[
                pltpu.VMEM((slots * tile, LANES), F32),
                pltpu.VMEM((LANES, count), F32),
                pltpu.VMEM((LANES, count), F32),
                pltpu.SemaphoreType.DMA((2,)),
            ],
        ),
        out_shape=out_shape,
        compiler_params=pltpu.CompilerParams(vmem_limit_bytes=VMEM),
        cost_estimate=pl.CostEstimate(
            flops=10 * slots * 2 * tile * count * LANES, bytes_accessed=16 * slots * tile * LANES, transcendentals=0
        ),
        name="attend_back",
    )(where, q, do, logs, deltas, routes, dlogits, keys, values, weights, *carried, *extra)


def middle_kernel(groups, *refs):
    refs = list(refs)
    take = lambda count: [refs.pop(0) for _ in range(count)]
    core_ref, x_ref, dy_ref, o_ref, gate_ref, routes_ref, tail_ref = take(7)
    if groups == 8:
        (gathered_ref,) = take(1)
    else:
        wo_ref, w1_ref, w2_ref = take(3)
    out_ref, dmid_ref, do_ref, delta_ref, dlog_ref, gain_ref = take(6)
    outs = take(4 if groups == 8 else 3)
    s1_ref, s2_ref, so_ref = take(3)
    width = x_ref.shape[1]
    if groups == 8:
        wo_in, w1_in, w2_in, sems = take(4)

        @pl.when(pl.program_id(0) == 0)
        def _():
            copies = []
            cols = gathered_ref.shape[-1]

            def copy(source, target):
                copies.append(pltpu.make_async_copy(source, target, sems.at[len(copies)]))

            for part in range(3):
                copy(
                    gathered_ref.at[:, :, pl.ds(128 + 16 * part, 16), :],
                    wo_in.at[:, :, :, pl.ds(part * cols, cols)],
                )
            for start, target in ((0, w1_in), (64, w2_in)):
                for index in range(4):
                    copy(
                        gathered_ref.at[:, index, pl.ds(start, 64), :],
                        target.at[:, :, pl.ds(index * cols, cols)],
                    )
            for one in copies:
                one.start()
            for one in copies:
                one.wait()

        wo = wo_in[...].reshape(width, SPAN)
        w1 = w1_in[...].reshape(width, -1)
        w2 = w2_in[...].reshape(width, -1)
    else:
        wo, w1, w2 = wo_ref[...], w1_ref[...], w2_ref[...]
    step = pl.program_id(0)
    tile = x_ref.shape[0]
    gain = gains_of(tail_ref[...])[E + 1 : E + 2]
    routes = routes_ref[...]
    gates = gate_ref[...]
    lane = lane_index(tile)
    half = (lane >= HD).astype(jnp.int32)
    chosen = [column(routes, slot, tile) - half for slot in range(TOPK)]
    weighted = [column(gates, slot, tile) * o_ref[slot] for slot in range(TOPK)]
    parts = []
    for pair in range(PAIRS):
        total = jnp.zeros((tile, LANES), F32)
        for slot in range(TOPK):
            total = jnp.where(chosen[slot] == 2 * pair, weighted[slot], total)
        parts.append(total.astype(BF16))
    combined = jnp.concatenate(parts, 1)
    mid = x_ref[...].astype(F32) + dot_last(combined, wo)
    normal, factor = standardize(mid)
    h2 = (normal * gain).astype(BF16)
    pre = dot(h2, w1)
    sigma = jax.nn.sigmoid(pre)
    act = (pre * sigma).astype(BF16)
    out_ref[...] = (mid + dot_last(act, w2)).astype(BF16)
    dy = dy_ref[...]
    dact = dot(dy, w2)
    dpre = (dact * (sigma * (1.0 + pre * (1.0 - sigma)))).astype(BF16)
    dh2 = dot_last(dpre, w1)
    dmid = dy.astype(F32) + norm_back(dh2 * gain, normal, factor)
    dmid_ref[...] = dmid
    dmid_b = dmid.astype(BF16)
    dcomb = dot(dmid_b, wo)
    p1 = dot(turned(h2), dpre)
    p2 = dot(turned(dy), act)
    po = dot(turned(dmid_b), combined)
    pg = jnp.sum(dh2 * normal, 0, keepdims=True)

    @pl.when(step == 0)
    def _():
        s1_ref[...] = p1
        s2_ref[...] = p2
        so_ref[...] = po
        gain_ref[...] = pg

    @pl.when(step > 0)
    def _():
        s1_ref[...] += p1
        s2_ref[...] += p2
        so_ref[...] += po
        gain_ref[...] += pg

    weighted_total = jnp.zeros((tile, 1), F32)
    gate_grads = []
    deltas = jnp.zeros((tile, LANES), F32)
    for slot in range(TOPK):
        picked = pick_pairs(dcomb, chosen[slot])
        o = o_ref[slot]
        gate = column(gates, slot, tile)
        do = (gate * picked).astype(BF16)
        do_ref[slot] = do
        deltas = jnp.where(lane == slot, jnp.sum(o * do.astype(F32), -1, keepdims=True), deltas)
        gate_grad = jnp.sum(o * picked, -1, keepdims=True)
        gate_grads.append(gate_grad)
        weighted_total = weighted_total + gates[:, slot : slot + 1] * gate_grad
    delta_ref[...] = deltas
    dlogits = jnp.zeros((tile, LANES), F32)
    for slot in range(TOPK):
        dsel = gates[:, slot : slot + 1] * (gate_grads[slot] - weighted_total)
        dlogits = jnp.where(lane == column(routes, slot, tile), dsel, dlogits)
    dlog_ref[...] = dlogits.astype(BF16)

    @pl.when(step == pl.num_programs(0) - 1)
    def _():
        if groups != 8:
            for target, source in zip(outs, (s1_ref, s2_ref, so_ref)):
                target[...] = source[...].astype(BF16)
            return
        a_keep, a_send, b_keep, b_send = outs
        for core, (a_low, a_high, b_low, b_high) in enumerate(
            ((a_keep, a_send, b_keep, b_send), (a_send, a_keep, b_send, b_keep))
        ):

            @pl.when(core_ref[0] == core)
            def _(pairs=((a_low, b_low), (a_high, b_high))):
                for owner in range(32):
                    z, y, x, c = owner // 8, owner // 4 % 2, owner // 2 % 2, owner % 2
                    a, b = pairs[c]
                    up = slice((owner // 4) * 64, (owner // 4) * 64 + 64)
                    across = slice((owner % 4) * 512, (owner % 4) * 512 + 512)
                    mine = slice(owner * 16, owner * 16 + 16)
                    a[x, y, z, :64] = s1_ref[up, across].astype(BF16)
                    b[y, x, z, :64] = s2_ref[up, across].astype(BF16)
                    a[x, y, z, 64:80] = so_ref[mine, :512].astype(BF16)
                    a[x, y, z, 80:] = so_ref[mine, 512:1024].astype(BF16)
                    b[y, x, z, 64:] = so_ref[mine, 1024:].astype(BF16)


def middle_call(groups, core, x, dy, o, gates, routes, tail, weights, tile=256):
    rows, width = x.shape
    hidden = 2048
    whole = lambda shape: pl.BlockSpec(shape, lambda i, s: (0,) * len(shape))
    by_slot = pl.BlockSpec((TOPK, tile, LANES), lambda i, s: (0, i, 0))
    by_row = lambda cols: pl.BlockSpec((tile, cols), lambda i, s: (i, 0))
    scratch = [
        pltpu.VMEM((width, hidden), F32),
        pltpu.VMEM((width, hidden), F32),
        pltpu.VMEM((width, SPAN), F32),
    ]
    if groups == 8:
        weight_specs = [pl.BlockSpec(memory_space=pl.ANY)]
        grads = [(2, 2, 4, 96, 512), (2, 2, 4, 96, 512), (2, 2, 4, 80, 512), (2, 2, 4, 80, 512)]
        scratch += [
            pltpu.VMEM((8, 4, 16, SPAN), BF16),
            pltpu.VMEM((8, 64, hidden), BF16),
            pltpu.VMEM((8, 64, hidden), BF16),
            pltpu.SemaphoreType.DMA((11,)),
        ]
    else:
        weight_specs = [whole(array.shape) for array in weights]
        grads = [(width, hidden), (width, hidden), (width, SPAN)]
    return pl.pallas_call(
        functools.partial(middle_kernel, groups),
        grid_spec=pltpu.PrefetchScalarGridSpec(
            num_scalar_prefetch=1,
            grid=(rows // tile,),
            in_specs=[
                by_row(width), by_row(width), by_slot, by_row(LANES), by_row(TOPK), whole(tail.shape), *weight_specs,
            ],
            out_specs=[
                by_row(width), by_row(width), by_slot, by_row(LANES), by_row(LANES), whole((1, width)),
                *[whole(shape) for shape in grads],
            ],
            scratch_shapes=scratch,
        ),
        out_shape=[
            jax.ShapeDtypeStruct((rows, width), BF16),
            jax.ShapeDtypeStruct((rows, width), F32),
            jax.ShapeDtypeStruct((TOPK, rows, LANES), BF16),
            jax.ShapeDtypeStruct((rows, LANES), F32),
            jax.ShapeDtypeStruct((rows, LANES), BF16),
            jax.ShapeDtypeStruct((1, width), F32),
            *[jax.ShapeDtypeStruct(shape, BF16) for shape in grads],
        ],
        compiler_params=pltpu.CompilerParams(vmem_limit_bytes=VMEM),
        cost_estimate=pl.CostEstimate(
            flops=2 * rows * width * (6 * hidden + 3 * SPAN), bytes_accessed=16 * rows * width, transcendentals=0
        ),
        name="middle",
    )(core, x, dy, o, gates, routes, tail, *weights)


def post_kernel(x_ref, h_ref, dmid_ref, keep_ref, recv_ref, dlog_ref, gain2_ref, w_ref, *refs):
    *dh_refs, grad_ref, gk_ref = refs
    gain = gains_of(w_ref[:, LANES:])[E : E + 1]
    normal, factor = standardize(x_ref[...].astype(F32))
    dkv = (keep_ref[...].astype(F32) + recv_ref[...].astype(F32)).astype(BF16)
    dh = jnp.concatenate([ref[0] for ref in dh_refs] + [ref[1] for ref in dh_refs], 0)
    dh = dh + dot_last(dkv, w_ref[:, :LANES])
    grad_ref[...] = (dmid_ref[...] + norm_back(dh * gain, normal, factor)).astype(grad_ref.dtype)
    gain1 = jnp.sum(dh * normal, 0, keepdims=True)
    width = gain1.shape[1]
    row = lax.broadcasted_iota(jnp.int32, (LANES, width), 0)
    gains = jnp.where(row == E, gain1, jnp.where(row == E + 1, gain2_ref[...], 0.0))
    h_turned = turned(h_ref[...])
    gk_ref[:, :LANES] = dot(h_turned, dkv).astype(BF16)
    gk_ref[:, LANES:] = (dot(h_turned, dlog_ref[...]) + gains.T).astype(BF16)


def post_call(x, h, dmid, keep, recv, dlogits, gain2, weights, parts):
    rows, width = x.shape
    return pl.pallas_call(
        post_kernel,
        out_shape=[
            jax.ShapeDtypeStruct((rows, width), BF16),
            jax.ShapeDtypeStruct((width, 2 * LANES), BF16),
        ],
        compiler_params=pltpu.CompilerParams(vmem_limit_bytes=VMEM),
        cost_estimate=pl.CostEstimate(
            flops=6 * rows * width * LANES, bytes_accessed=16 * rows * width, transcendentals=0
        ),
        name="finish",
    )(x, h, dmid, keep, recv, dlogits, gain2, weights, *parts)


RING = ((0, 1), (1, 2), (2, 3), (3, 0))
SWAP = ((1, 3), (3, 1))


def deal(rows, place):
    half = rows.shape[0] // 2
    outer = (place == 0) | (place == 3)
    first = lax.dynamic_slice_in_dim(rows, jnp.where(outer, half, 0), half, 0)
    second = lax.dynamic_slice_in_dim(rows, jnp.where(place == 1, half, 0), half, 0)
    ring = lax.ppermute(first, "mp", RING)
    swap = lax.ppermute(second, "mp", SWAP)
    low = jnp.where(place == 0, rows[:half], jnp.where(place == 3, swap, ring))
    high = jnp.where(place == 2, rows[half:], jnp.where(place == 1, swap, ring))
    return jnp.concatenate([low, high], 0)


def gather_back(rows, place):
    half = rows.shape[0] // 2
    outer = (place == 0) | (place == 3)
    first = lax.dynamic_slice_in_dim(rows, jnp.where(outer, half, 0), half, 0)
    second = lax.dynamic_slice_in_dim(rows, jnp.where(place == 1, half, 0), half, 0)
    ring = lax.ppermute(first, "mp", tuple((b, a) for a, b in RING))
    swap = lax.ppermute(second, "mp", SWAP)
    top = jnp.where(place == 0, rows[:half], jnp.where(place == 3, swap, ring))
    bottom = jnp.where(place == 2, rows[half:], jnp.where(place == 1, swap, ring))
    return jnp.concatenate([top, bottom], 0)


OTHER_CORE = ((0, 1), (1, 0), (2, 3), (3, 2))
OTHER_X = ((0, 2), (2, 0), (1, 3), (3, 1))


def swap_core(values):
    return lax.ppermute(values, "mp", OTHER_CORE)


def swap_x(values):
    return lax.ppermute(values, "mp", OTHER_X)


def swap_y(values):
    return lax.ppermute(values, "dp", tuple((i, i ^ 1) for i in range(8)))


def swap_z(values, turn):
    return lax.ppermute(values, "dp", tuple((i, i ^ (2 * turn)) for i in range(8)))


def at(values, index):
    return lax.dynamic_index_in_dim(values, index, 0, keepdims=False)


def added(left, right):
    return (left.astype(F32) + right.astype(F32)).astype(BF16)


def gather_chips(shard):
    along = jnp.stack([shard] + [swap_z(shard, turn) for turn in (1, 2, 3)])
    along = jnp.stack([along, swap_y(along)])
    along = jnp.stack([along, swap_x(along)])
    along = along.reshape(16, *shard.shape)
    return along, swap_core(along)


def tied(first, second):
    return lax.optimization_barrier((first, second))


def rate_columns(rates):
    return jnp.concatenate(
        [
            jnp.full((SPAN,), rates[0]),
            jnp.full((SPAN,), rates[1]),
            jnp.full((2 * HD,), rates[2]),
            jnp.full((E,), rates[3]),
            jnp.full((2,), rates[4]),
        ]
    )


def decay_columns():
    return jnp.concatenate([jnp.full((AC - 2,), WEIGHT_DECAY, F32), jnp.zeros((2,), F32)])


def adam_step(param, first, second, grad, rate, decay):
    first_new = BETA_FIRST * first + (1.0 - BETA_FIRST) * grad
    second_new = BETA_SECOND * second + (1.0 - BETA_SECOND) * grad * grad
    first_hat = first_new / (1.0 - BETA_FIRST**ADAM_STEP)
    second_hat = second_new / (1.0 - BETA_SECOND**ADAM_STEP)
    param_new = param - rate * (first_hat / (jnp.sqrt(second_hat) + ADAM_EPS) + decay * param)
    return (second_new, param_new)


ALL = ("dp", "mp")


def shards(
    tokens, cotangent, routes, starts, attn_param, attn_first, attn_second, ffn_param, ffn_first, ffn_second, rates
):
    local_rows, width = tokens.shape
    place = lax.axis_index("mp")
    devices = lax.axis_size("mp")
    groups = lax.axis_size("dp")
    block = local_rows // 2

    manual = groups == 8
    _, depth, cols = ffn_param.shape
    attn_b = attn_param.astype(BF16)
    ffn_b = ffn_param.astype(BF16)
    pad = jnp.zeros((attn_b.shape[0], 2 * LANES - (AC - 2 * SPAN)), BF16)
    front = jnp.concatenate([attn_b[:, :SPAN], attn_b[:, 2 * SPAN :], pad], 1)
    wo = attn_b[:, SPAN : 2 * SPAN]
    if manual:
        flat = lax.axis_index("dp") * devices + place
        chunk = jnp.concatenate([ffn_b.reshape(2 * depth, cols)] + [wo[:, i * cols : (i + 1) * cols] for i in range(3)], 0)
        weights = [lax.all_gather(chunk, ALL, axis=0, tiled=False).reshape(groups, devices, *chunk.shape)]
        near, far = gather_chips(front)
    else:
        flat = jnp.zeros((), jnp.int32)
        front_all = lax.all_gather(front, ALL, axis=0, tiled=True).reshape(4, 2, 2, 2, 16, -1)
        front_all = front_all.transpose(3, 2, 1, 0, 4, 5).reshape(2, 16, 16, -1)
        near, far = front_all[0], front_all[1]
        wo_full = lax.all_gather(wo, ALL, axis=0, tiled=True)
        ffn_all = lax.all_gather(ffn_b, ALL, axis=0, tiled=False)
        ffn_all = ffn_all.reshape(groups, devices, 2, depth, cols).transpose(2, 0, 3, 1, 4)
        ffn_all = ffn_all.reshape(2, groups * depth, devices * cols)
        weights = [wo_full, ffn_all[0], ffn_all[1]]

    side = jnp.concatenate([routes, starts[:, None] // block], 1).astype(BF16)
    side = jnp.pad(side, ((0, 0), (0, LANES - TOPK - 1)))
    x = deal(jnp.concatenate([tokens, side], 1), place)
    marks = x[:, width : width + TOPK + 1].astype(jnp.int32)
    x = x[:, :width]
    routes_x = marks[:, :TOPK]
    dy = deal(cotangent, place)
    tile = 128
    tiles = local_rows // tile
    pieces = tiles // 2
    index = jnp.arange(tiles, dtype=jnp.int32)
    low = index < pieces
    here = jnp.where(low, place * block + index * tile, (2 * devices - 1 - place) * block + (index - pieces) * tile)
    lower = jnp.where(low, marks[0, TOPK], marks[block, TOPK]) * block
    where = jnp.stack([here, lower, jnp.full((tiles,), place)]).astype(jnp.int32)

    h, q, kv, gates, front_full = pre_call(flat.reshape(1).astype(jnp.int32), x, routes_x, near, far)
    kv = kv.reshape(2, block, LANES)
    kv_x = swap_x(kv)
    kv_all = jnp.stack([kv, swap_core(kv), kv_x, swap_core(kv_x)])
    o, logs, keys, values = attend_call(where, q, kv_all, tile)
    tail = front_full[:, SPAN + LANES :]
    core = (place % 2).reshape(1).astype(jnp.int32)
    out, dmid, do, deltas, dlogits, gain2, *grads = middle_call(
        groups, core, x, dy, o, gates, routes_x, tail, weights
    )
    layer_out = gather_back(out, place)

    def back(piece, carried, extra=()):
        where_now = where[:, jnp.array([piece, piece + pieces])]
        return attend_back_call(
            piece, pieces, groups, where_now, q, do, logs, deltas, routes_x, dlogits, keys, values, front_full,
            carried, extra,
        )

    my_x, my_y, my_z = place // 2, lax.axis_index("dp") % 2, lax.axis_index("dp") // 2
    dh_parts, all_parts, carried = [], [], ()
    if manual:
        a_keep, a_send, b_keep, b_send = grads
        moving = (swap_core(a_send), swap_core(b_send))
    for piece in range(pieces - 1):
        dh_part, all_part, *carried = back(piece, carried)
        dh_parts.append(dh_part)
        all_parts.append(all_part)
        if not manual:
            continue
        carried, moving = tied(carried, moving)
        a_in, b_in = moving
        if piece == 0:
            a_now = (a_keep, a_in)
            b_now = (b_keep, b_in)
            turn_a, turn_b, swap_a, swap_b = my_x, my_y, swap_x, swap_y
        elif piece == 1:
            a_now = (a_keep, a_in)
            b_now = (b_keep, b_in)
            turn_a, turn_b, swap_a, swap_b = my_y, my_x, swap_y, swap_x
        if piece < 2:
            a_send = added(at(a_now[0], 1 - turn_a), at(a_now[1], 1 - turn_a))
            b_send = added(at(b_now[0], 1 - turn_b), at(b_now[1], 1 - turn_b))
            a_keep = added(at(a_now[0], turn_a), at(a_now[1], turn_a))
            b_keep = added(at(b_now[0], turn_b), at(b_now[1], turn_b))
            (a_send, b_send, a_keep, b_keep), carried = tied((a_send, b_send, a_keep, b_keep), carried)
            moving = (swap_a(a_send), swap_b(b_send))
        else:
            both = jnp.concatenate([added(a_keep, a_in), added(b_keep, b_in)], 1)
            both, carried = tied(both, carried)
            moving = [swap_z(at(both, my_z ^ turn), turn) for turn in (1, 2, 3)]
            chunk_keep = at(both, my_z)
    dh_part, all_part, kv_keep, kv_send, gq_keep, gq_send = back(
        pieces - 1, carried, (h, jnp.stack(all_parts))
    )
    dh_parts.append(dh_part)
    kv_in = swap_core(kv_send)
    kv_out = added(kv_keep[1], kv_in[1])
    kv_keep = added(kv_keep[0], kv_in[0]).reshape(local_rows, LANES)
    kv_recv = swap_x(kv_out).reshape(local_rows, LANES)
    if manual:
        gq_in = swap_core(gq_send)
        gq_send = added(at(gq_keep, 1 - my_y), at(gq_in, 1 - my_y))
        gq_keep = added(at(gq_keep, my_y), at(gq_in, my_y))
        gq = added(gq_keep, swap_y(gq_send))
        gq_in = [swap_z(at(gq, my_z ^ turn), turn) for turn in (1, 2, 3)]
        gq = sum((part.astype(F32) for part in gq_in), at(gq, my_z).astype(F32)).astype(BF16)
        gq_raw = at(gq, my_x).astype(F32) + swap_x(at(gq, 1 - my_x)).astype(F32)
    grad, gk = post_call(x, h, dmid, kv_keep, kv_recv, dlogits, gain2, front_full[:, SPAN:], dh_parts)
    input_grad = gather_back(grad, place).astype(F32)

    if manual:
        gk = lax.all_to_all(gk.reshape(groups * devices, -1, 2 * LANES), ALL, 0, 0, tiled=True)
        gk_raw = jnp.sum(gk.astype(F32), 0)
        chunk_raw = sum((part.astype(F32) for part in moving), chunk_keep.astype(F32))
        rows = depth
        ffn_raw = jnp.stack([chunk_raw[:rows], chunk_raw[rows + 32 : 2 * rows + 32]])
        go_raw = jnp.concatenate(
            [chunk_raw[rows : rows + 16], chunk_raw[rows + 16 : rows + 32], chunk_raw[2 * rows + 32 :]], 1
        )
    else:
        g1, g2, go = grads
        ffn_local = jnp.stack([g1, g2]).reshape(2, groups, depth, devices, cols).transpose(1, 3, 0, 2, 4)
        ffn_local = ffn_local.reshape(groups * devices * 2 * depth, cols)
        ffn_raw = lax.psum_scatter(ffn_local, ALL, scatter_dimension=0, tiled=True).astype(F32)
        ffn_raw = ffn_raw.reshape(2, depth, cols)
        go_raw = lax.psum_scatter(go, ALL, scatter_dimension=0, tiled=True).astype(F32)
        gq_raw = lax.psum_scatter(gq_keep, ALL, scatter_dimension=0, tiled=True).astype(F32)
        gk_raw = lax.psum_scatter(gk, ALL, scatter_dimension=0, tiled=True).astype(F32)
    attn_raw = jnp.concatenate([gq_raw, go_raw, gk_raw[:, : AC - 2 * SPAN]], 1)

    squares = jnp.sum(attn_raw * attn_raw) + jnp.sum(ffn_raw * ffn_raw)
    if manual:
        squares = jnp.broadcast_to(squares, (groups * devices, 8, LANES))
        squares = jnp.sum(lax.all_to_all(squares, ALL, 0, 0, tiled=True), 0)[0, 0]
    else:
        squares = lax.psum(squares, ALL)
    grad_norm = jnp.sqrt(squares)
    factor = jnp.minimum(1.0, CLIP_NORM / grad_norm)
    attn_grad = attn_raw * factor
    ffn_grad = ffn_raw * factor
    attn_second_new, attn_new = adam_step(
        attn_param, attn_first, attn_second, attn_grad, rate_columns(rates)[None, :], decay_columns()[None, :]
    )
    ffn_rates = jnp.stack([rates[5], rates[6]])[:, None, None]
    ffn_second_new, ffn_new = adam_step(ffn_param, ffn_first, ffn_second, ffn_grad, ffn_rates, WEIGHT_DECAY)
    return (
        layer_out,
        input_grad,
        attn_grad,
        attn_second_new,
        attn_new,
        ffn_grad,
        ffn_second_new,
        ffn_new,
        grad_norm,
        attn_grad[:, AC - 2 :],
    )


def solution(mesh):
    by_row = P(ALL, None)
    by_ffn = P(None, "dp", "mp")
    return jax.shard_map(
        shards,
        mesh=mesh,
        in_specs=(by_row, by_row, by_row, P(ALL), by_row, by_row, by_row, by_ffn, by_ffn, by_ffn, P()),
        out_specs=(by_row, by_row, by_row, by_row, by_row, by_ffn, by_ffn, by_ffn, P(), by_row),
        check_vma=False,
    )
```

```python
import functools
import math

import jax
import jax.numpy as jnp
from jax import lax
from jax.experimental import pallas as pl
from jax.experimental.pallas import tpu as pltpu
from jax.sharding import PartitionSpec as P

HD = 64
E = 24
TOPK = 8
ADAM_STEP = 7
AC = 3226
SPAN = E * HD
PAIRS = E // 2
LANES = 128

NORM_EPS = 1e-05
MASKED = -1e30
CLIP_NORM = 0.1
BETA_FIRST = 0.9
BETA_SECOND = 0.95
ADAM_EPS = 1e-08
WEIGHT_DECAY = 0.1

SCALE = HD ** (-0.5)
LOG2E = math.log2(math.e)
SAFE_SCORE = 40.0
SAFE_VALUE = 1e15
VMEM = 58 << 20

F32 = jnp.float32
BF16 = jnp.bfloat16


def dot(left, right):
    return jnp.dot(left, right, preferred_element_type=F32)


def dot_last(left, right):
    return lax.dot_general(left, right, (((1,), (1,)), ((), ())), preferred_element_type=F32)


def dot_first(left, right):
    return lax.dot_general(left, right, (((0,), (0,)), ((), ())), preferred_element_type=F32)


def turned(values):
    return values.astype(F32).T.astype(values.dtype)


def standardize(values):
    centred = values - jnp.mean(values, -1, keepdims=True)
    factor = lax.rsqrt(jnp.mean(centred * centred, -1, keepdims=True) + NORM_EPS)
    return (centred * factor, factor)


def norm_back(grad_normal, normal, factor):
    return factor * (
        grad_normal
        - jnp.mean(grad_normal, -1, keepdims=True)
        - normal * jnp.mean(grad_normal * normal, -1, keepdims=True)
    )


def lane_index(rows):
    return lax.broadcasted_iota(jnp.int32, (rows, LANES), 1)


def column(values, index, rows):
    return jnp.broadcast_to(values[:, index : index + 1], (rows, LANES))


def pick_pairs(table, chosen):
    picked = jnp.zeros(chosen.shape, table.dtype)
    for pair in range(PAIRS):
        picked = jnp.where(chosen == 2 * pair, table[:, pair * LANES : (pair + 1) * LANES], picked)
    return picked


def place_pairs(parts, chosen):
    columns = []
    for pair in range(PAIRS):
        total = jnp.zeros(chosen[0].shape, parts[0].dtype)
        for part, choice in zip(parts, chosen):
            total = jnp.where(choice == 2 * pair, part, total)
        columns.append(total)
    return jnp.concatenate(columns, 1)


def choices(routes, rows, dtype):
    half = (lane_index(rows) >= HD).astype(jnp.int32)
    return [(column(routes, slot, rows) - half).astype(F32).astype(dtype) for slot in range(TOPK)]


def gains_of(tail):
    return tail.astype(F32).T


def flat_of(index):
    x, y, z = index // 8, index // 4 % 2, index % 4
    return ((z * 2 + y) * 2 + x) * 2


def embed_kernel(x_ref, routes_ref, w_ref, h_ref, kv_ref, gate_ref):
    rows = x_ref.shape[0]
    gain = gains_of(w_ref[:, LANES:])[E : E + 1]
    normal, _ = standardize(x_ref[...].astype(F32))
    h = (normal * gain).astype(BF16)
    h_ref[...] = h
    proj = dot(h, w_ref[...])
    kv_ref[...] = proj[:, :LANES].astype(BF16)
    logits = proj[:, LANES:]
    routes = routes_ref[...]
    lane = lane_index(rows)
    columns = [column(routes, slot, rows) for slot in range(TOPK)]
    chosen = jnp.zeros((rows, LANES), jnp.bool_)
    for route in columns:
        chosen = chosen | (lane == route)
    peak = jnp.max(jnp.where(chosen, logits, MASKED), -1, keepdims=True)
    expo = jnp.where(chosen, jnp.exp(jnp.where(chosen, logits - peak, 0.0)), 0.0)
    dense = expo / jnp.sum(expo, -1, keepdims=True)
    gates = jnp.zeros((rows, LANES), F32)
    for slot, route in enumerate(columns):
        hit = jnp.where(lane == route, dense, 0.0)
        gates = jnp.where(lane == slot, jnp.sum(hit, -1, keepdims=True), gates)
    gate_ref[...] = gates


def embed_call(x, routes, weights, tile=256):
    rows, width = x.shape
    by_row = lambda count: pl.BlockSpec((tile, count), lambda i: (i, 0))
    return pl.pallas_call(
        embed_kernel,
        grid=(rows // tile,),
        in_specs=[by_row(width), by_row(TOPK), pl.BlockSpec(weights.shape, lambda i: (0, 0))],
        out_specs=[by_row(width), by_row(LANES), by_row(LANES)],
        out_shape=[
            jax.ShapeDtypeStruct((rows, width), BF16),
            jax.ShapeDtypeStruct((rows, LANES), BF16),
            jax.ShapeDtypeStruct((rows, LANES), F32),
        ],
        compiler_params=pltpu.CompilerParams(vmem_limit_bytes=VMEM),
        cost_estimate=pl.CostEstimate(
            flops=4 * rows * width * LANES, bytes_accessed=8 * rows * width, transcendentals=0
        ),
        name="embed",
    )(x, routes, weights)


def query_kernel(me_ref, h_ref, routes_ref, near_ref, far_ref, q_ref, w_ref, sems):
    rows = h_ref.shape[0]
    pieces, piece, _ = near_ref.shape

    @pl.when(pl.program_id(0) == 0)
    def _():
        copies = []
        for core, part in enumerate((near_ref, far_ref)):
            for index in range(pieces):
                owner = me_ref[0] ^ (flat_of(index) + core)
                first = pl.multiple_of(owner * piece, piece)
                copies.append(
                    pltpu.make_async_copy(
                        part.at[index], w_ref.at[pl.ds(first, piece), :], sems.at[core * pieces + index]
                    )
                )
        for copy in copies:
            copy.start()
        for copy in copies:
            copy.wait()

    table = dot(h_ref[...], w_ref[...]).astype(BF16)
    for slot, choice in enumerate(choices(routes_ref[...], rows, BF16)):
        q_ref[slot] = pick_pairs(table, choice)


def query_call(me, h, routes, near, far, tile=256):
    rows, width = h.shape
    pieces, piece, cols = near.shape
    by_row = lambda count: pl.BlockSpec((tile, count), lambda i, s: (i, 0))
    return pl.pallas_call(
        query_kernel,
        grid_spec=pltpu.PrefetchScalarGridSpec(
            num_scalar_prefetch=1,
            grid=(rows // tile,),
            in_specs=[
                by_row(width),
                by_row(TOPK),
                pl.BlockSpec(memory_space=pl.ANY),
                pl.BlockSpec(memory_space=pl.ANY),
            ],
            out_specs=[
                pl.BlockSpec((TOPK, tile, LANES), lambda i, s: (0, i, 0)),
                pl.BlockSpec((width, cols), lambda i, s: (0, 0)),
            ],
            scratch_shapes=[pltpu.SemaphoreType.DMA((2 * pieces,))],
        ),
        out_shape=[
            jax.ShapeDtypeStruct((TOPK, rows, LANES), BF16),
            jax.ShapeDtypeStruct((width, cols), BF16),
        ],
        compiler_params=pltpu.CompilerParams(vmem_limit_bytes=VMEM),
        cost_estimate=pl.CostEstimate(
            flops=2 * rows * width * cols, bytes_accessed=8 * rows * width + 2 * width * cols, transcendentals=0
        ),
        name="query",
    )(me, h, routes, near, far)


def spread_keyval(device, kv_refs, key_ref, value_ref):
    devices = len(kv_refs)
    _, block, _ = kv_refs[0].shape
    low_half = lane_index(block) < HD
    for index in range(devices):
        for high in range(2):
            rows = kv_refs[index][high].astype(F32)
            rolled = pltpu.roll(rows, HD, 1)
            span = block_of(device ^ index, high, devices, block)
            key_ref[span, :] = jnp.where(low_half, rows, rolled).astype(BF16)
            value_ref[span, :] = jnp.where(low_half, rolled, rows).astype(BF16)


def block_of(device, high, devices, block):
    place = 2 * devices - 1 - device if high else device
    return pl.ds(pl.multiple_of(place * block, block), block)


def attend_kernel(place_ref, q_ref, *refs):
    *kv_refs, o_ref, log_ref, key_ref, plain_ref, value_ref, acc_ref, peak_ref, bound_ref = refs
    step = pl.program_id(0)
    slots, tile, _ = q_ref.shape
    rows = slots * tile
    width = 512

    @pl.when(step == 0)
    def _():
        spread_keyval(place_ref[2, 0], kv_refs, key_ref, plain_ref)
        value_ref[:, :LANES] = plain_ref[...]
        value_ref[:, LANES:] = jnp.ones((value_ref.shape[0], LANES), BF16)
        keys = key_ref[...].astype(F32)
        bound_ref[0] = jnp.max(jnp.sum(keys * keys, -1, keepdims=True)) * 0.5
        bound_ref[1] = jnp.max(jnp.abs(plain_ref[...].astype(F32)))

    here = place_ref[0, step]
    lower = pl.multiple_of(place_ref[1, step], width)
    q = q_ref[...].reshape(rows, LANES)
    qf = q.astype(F32)
    longest = jnp.max(jnp.sum(qf * qf, -1, keepdims=True))
    plain = (longest * bound_ref[0] <= (SAFE_SCORE / SCALE) ** 2) & (bound_ref[1] <= SAFE_VALUE)
    full = (here - lower) // width
    last = pl.multiple_of(lower + full * width, width)
    token = lax.broadcasted_iota(jnp.int32, (tile, width), 0) + here
    allowed = (lax.broadcasted_iota(jnp.int32, (tile, width), 1) + last) <= token
    allowed = jnp.broadcast_to(allowed[None], (slots, tile, width)).reshape(rows, width)

    def finish(out, logs):
        o_ref[...] = out.reshape(slots, tile, LANES)
        logs = logs.reshape(slots, tile, LANES)
        lane = lane_index(tile)
        packed = jnp.zeros((tile, LANES), F32)
        for slot in range(slots):
            packed = jnp.where(lane == slot, logs[slot], packed)
        log_ref[...] = packed

    pairs = full // 2

    @pl.when(plain)
    def _():
        for count in (1, 2):

            @pl.when(full % 2 == count - 1)
            def _(count=count):
                span = pl.ds(pl.multiple_of(lower + pairs * 2 * width, width), count * width)
                expo = jnp.exp2(dot_last(q, key_ref[span, :]) * (SCALE * LOG2E))
                edge = jnp.where(allowed, expo[:, (count - 1) * width :], 0.0).astype(BF16)
                expo = jnp.concatenate([expo[:, :width].astype(BF16), edge], 1) if count > 1 else edge
                acc_ref[...] = dot(expo, value_ref[span, :])

        def body(index, carry):
            span = pl.ds(pl.multiple_of(lower + index * 2 * width, width), 2 * width)
            expo = jnp.exp2(dot_last(q, key_ref[span, :]) * (SCALE * LOG2E)).astype(BF16)
            acc_ref[...] += dot(expo, value_ref[span, :])
            return carry

        lax.fori_loop(0, pairs, body, 0)
        total = acc_ref[:, LANES:]
        finish(acc_ref[:, :LANES] / total, jnp.log2(total))

    @pl.when(jnp.logical_not(plain))
    def _():
        def scaled(span):
            return dot_last(q, key_ref[span, :]) * (SCALE * LOG2E)

        scores = jnp.where(allowed, scaled(pl.ds(last, width)), MASKED)
        peak = jnp.max(scores, -1, keepdims=True)
        peak_ref[...] = jnp.broadcast_to(peak, (rows, LANES))
        acc_ref[...] = dot(jnp.exp2(scores - peak).astype(BF16), value_ref[pl.ds(last, width), :])

        def body(index, carry):
            span = pl.ds(pl.multiple_of(lower + index * width, width), width)
            scores = scaled(span)
            before = peak_ref[:, :1]
            peak = jnp.maximum(before, jnp.max(scores, -1, keepdims=True))
            peak_ref[...] = jnp.broadcast_to(peak, (rows, LANES))
            expo = jnp.exp2(scores - peak).astype(BF16)
            acc_ref[...] = acc_ref[...] * jnp.exp2(before - peak) + dot(expo, value_ref[span, :])
            return carry

        lax.fori_loop(0, full, body, 0)
        total = acc_ref[:, LANES:]
        finish(acc_ref[:, :LANES] / total, peak_ref[...] + jnp.log2(total))


def attend_call(place, q, kv, tile=128):
    slots, rows, _ = q.shape
    count = len(kv) * kv[0].shape[0] * kv[0].shape[1]
    return pl.pallas_call(
        attend_kernel,
        grid_spec=pltpu.PrefetchScalarGridSpec(
            num_scalar_prefetch=1,
            grid=(rows // tile,),
            in_specs=[
                pl.BlockSpec((slots, tile, LANES), lambda i, s: (0, i, 0)),
                *[pl.BlockSpec(part.shape, lambda i, s: (0, 0, 0)) for part in kv],
            ],
            out_specs=[
                pl.BlockSpec((slots, tile, LANES), lambda i, s: (0, i, 0)),
                pl.BlockSpec((tile, LANES), lambda i, s: (i, 0)),
                pl.BlockSpec((count, LANES), lambda i, s: (0, 0)),
                pl.BlockSpec((count, LANES), lambda i, s: (0, 0)),
            ],
            scratch_shapes=[
                pltpu.VMEM((count, 2 * LANES), BF16),
                pltpu.VMEM((slots * tile, 2 * LANES), F32),
                pltpu.VMEM((slots * tile, LANES), F32),
                pltpu.SMEM((2,), F32),
            ],
        ),
        out_shape=[
            jax.ShapeDtypeStruct((slots, rows, LANES), F32),
            jax.ShapeDtypeStruct((rows, LANES), F32),
            jax.ShapeDtypeStruct((count, LANES), BF16),
            jax.ShapeDtypeStruct((count, LANES), BF16),
        ],
        compiler_params=pltpu.CompilerParams(vmem_limit_bytes=VMEM),
        cost_estimate=pl.CostEstimate(
            flops=8 * slots * rows * count * LANES, bytes_accessed=8 * slots * rows * LANES, transcendentals=0
        ),
        name="attend",
    )(place, q, *kv)


def attend_back_kernel(piece, pieces, groups, *refs):
    first, final = piece == 0, piece == pieces - 1
    refs = list(refs)
    take = lambda count: [refs.pop(0) for _ in range(count)]
    place_ref, q_ref, do_ref, log_ref, delta_ref, routes_ref, key_ref, value_ref = take(8)
    if not first:
        (sums_in,) = take(1)
    if final:
        (h_ref,) = take(1)
        before_refs = take(pieces - 1)
    (all_ref,) = take(1)
    outs = take(4 if final else 1)
    dq_ref, dkey_ref, dvalue_ref, sems = take(4)
    step = pl.program_id(0)
    steps = pl.num_programs(0)
    slots, tile, _ = q_ref.shape
    rows = slots * tile
    width = 512

    @pl.when(step == 0)
    def _():
        dkey_ref[...] = jnp.zeros_like(dkey_ref)
        dvalue_ref[...] = jnp.zeros_like(dvalue_ref)
        if not first:
            copies = [
                pltpu.make_async_copy(sums_in.at[0], dkey_ref.at[pl.ds(0, HD), :], sems.at[0]),
                pltpu.make_async_copy(sums_in.at[1], dvalue_ref.at[pl.ds(0, HD), :], sems.at[1]),
            ]
            for copy in copies:
                copy.start()
            for copy in copies:
                copy.wait()

    here = place_ref[0, piece + pieces * step]
    lower = place_ref[1, piece + pieces * step]
    q = q_ref[...].reshape(rows, LANES)
    do = do_ref[...].reshape(rows, LANES)
    q_turned = turned(q)
    do_turned = turned(do)
    logs = log_ref[...]
    deltas = delta_ref[...]
    logs = jnp.concatenate([column(logs, slot, tile) for slot in range(slots)], 0)
    deltas = jnp.concatenate([column(deltas, slot, tile) for slot in range(slots)], 0)
    full = (here - lower) // width
    last = pl.multiple_of(lower + full * width, width)
    token = lax.broadcasted_iota(jnp.int32, (tile, width), 0) + here
    allowed = (lax.broadcasted_iota(jnp.int32, (tile, width), 1) + last) <= token
    allowed = jnp.broadcast_to(allowed[None], (slots, tile, width)).reshape(rows, width)

    def wide(values):
        return jnp.concatenate([values] * (width // LANES), 1)

    def one(start, masked):
        span = pl.ds(start, width)
        keys = key_ref[span, :]
        scores = dot_last(q, keys)
        probs = jnp.exp2(scores * (SCALE * LOG2E) - wide(logs))
        if masked:
            probs = jnp.where(allowed, probs, 0.0)
        dprobs = dot_last(do, value_ref[span, :])
        dscores = (probs * (dprobs - wide(deltas))).astype(BF16)
        dvalue_ref[:, span] += dot(do_turned, probs.astype(BF16))
        dkey_ref[:, span] += dot(q_turned, dscores)
        return dot(dscores, keys)

    dq_ref[...] = one(last, True)

    def body(index, carry):
        dq_ref[...] += one(pl.multiple_of(lower + index * width, width), False)
        return carry

    lax.fori_loop(0, full, body, 0)

    dq = (dq_ref[...] * SCALE).astype(BF16).reshape(slots, tile, LANES)
    mine = pl.ds(pl.multiple_of(step * tile, tile), tile)
    all_ref[mine, :] = place_pairs([dq[slot] for slot in range(slots)], choices(routes_ref[...], tile, BF16))

    @pl.when(step == steps - 1)
    def _():
        if not final:
            dkey_ref[:HD] += dkey_ref[HD:]
            dvalue_ref[:HD] += dvalue_ref[HD:]
            copies = [
                pltpu.make_async_copy(dkey_ref.at[pl.ds(0, HD), :], outs[0].at[0], sems.at[0]),
                pltpu.make_async_copy(dvalue_ref.at[pl.ds(0, HD), :], outs[0].at[1], sems.at[1]),
            ]
            for copy in copies:
                copy.start()
            for copy in copies:
                copy.wait()
            return
        kv_keep, kv_send, gq_keep, gq_send = outs
        _, _, block, _ = kv_keep.shape
        device = place_ref[2, 0]
        for index in range(4):
            target = kv_send if index % 2 else kv_keep
            for high in range(2):
                span = block_of(device ^ index, high, 4, block)
                dkeys = (dkey_ref[:HD, span] + dkey_ref[HD:, span]) * SCALE
                dvalues = dvalue_ref[:HD, span] + dvalue_ref[HD:, span]
                target[index // 2, high] = jnp.concatenate([dkeys, dvalues], 0).T.astype(BF16)
        gq = dot(turned(h_ref[...]), in_rows([*before_refs, all_ref], tile))
        if groups == 8:
            scatter_rows(gq, gq_keep, gq_send, device % 2)
        else:
            gq_keep[...] = gq.astype(BF16)
            gq_send[...] = jnp.zeros_like(gq_send)


def in_rows(parts, tile):
    return jnp.concatenate([part[:tile] for part in parts] + [part[tile:] for part in parts], 0)


def scatter_rows(grad, keep, send, core):
    for x in range(2):
        for y in range(2):
            for z in range(4):
                base = (((z * 2 + y) * 2 + x) * 2) * 16
                low = grad[base : base + 16].astype(BF16)
                high = grad[base + 16 : base + 32].astype(BF16)
                keep[y, z, x] = jnp.where(core == 0, low, high)
                send[y, z, x] = jnp.where(core == 0, high, low)


def attend_back_call(piece, pieces, groups, where, q, do, logs, deltas, routes, keys, values, carried, h, before):
    slots, rows, _ = q.shape
    count = keys.shape[0]
    width = h.shape[1]
    tile = rows // (2 * pieces)
    final = piece == pieces - 1
    whole = lambda shape: pl.BlockSpec(shape, lambda i, s: (0,) * len(shape))
    anywhere = pl.BlockSpec(memory_space=pl.ANY)
    by_slot = pl.BlockSpec((slots, tile, LANES), lambda i, s: (0, piece + pieces * i, 0))
    by_row = lambda cols: pl.BlockSpec((tile, cols), lambda i, s: (piece + pieces * i, 0))
    in_specs = [
        by_slot, by_slot, by_row(LANES), by_row(LANES), by_row(TOPK), whole(keys.shape), whole(values.shape),
    ]
    in_specs += [anywhere] * len(carried)
    extra = [h, *before] if final else []
    in_specs += [whole(array.shape) for array in extra]
    out_specs = [whole((2 * tile, SPAN))]
    out_shape = [jax.ShapeDtypeStruct((2 * tile, SPAN), BF16)]
    if final:
        kv_shape = (2, 2, rows // 2, LANES)
        gq_shape = (2, 4, 2, 16, SPAN) if groups == 8 else (width, SPAN)
        off_shape = gq_shape if groups == 8 else (8, LANES)
        for shape in (kv_shape, kv_shape, gq_shape, off_shape):
            out_specs.append(whole(shape))
            out_shape.append(jax.ShapeDtypeStruct(shape, BF16))
    else:
        out_specs.append(anywhere)
        out_shape.append(jax.ShapeDtypeStruct((2, HD, count), F32))
    return pl.pallas_call(
        functools.partial(attend_back_kernel, piece, pieces, groups),
        grid_spec=pltpu.PrefetchScalarGridSpec(
            num_scalar_prefetch=1,
            grid=(2,),
            in_specs=in_specs,
            out_specs=out_specs,
            scratch_shapes=[
                pltpu.VMEM((slots * tile, LANES), F32),
                pltpu.VMEM((LANES, count), F32),
                pltpu.VMEM((LANES, count), F32),
                pltpu.SemaphoreType.DMA((2,)),
            ],
        ),
        out_shape=out_shape,
        compiler_params=pltpu.CompilerParams(vmem_limit_bytes=VMEM),
        cost_estimate=pl.CostEstimate(
            flops=10 * slots * 2 * tile * count * LANES, bytes_accessed=16 * slots * tile * LANES, transcendentals=0
        ),
        name="attend_back",
    )(where, q, do, logs, deltas, routes, keys, values, *carried, *extra)


def query_back_kernel(dlog_ref, wq_ref, wr_ref, *refs):
    *all_refs, dh_ref = refs
    rows = in_rows(all_refs, all_refs[0].shape[0] // 2)
    dh_ref[...] = dot_last(rows, wq_ref[...]) + dot_last(dlog_ref[...], wr_ref[...])


def query_back_call(dlogits, wq, wk, parts):
    rows = dlogits.shape[0]
    width = wq.shape[0]
    cols = lambda size, index: pl.BlockSpec((width, size), lambda i: (0, index))
    whole = lambda shape: pl.BlockSpec(shape, lambda i: (0,) * len(shape))
    return pl.pallas_call(
        query_back_kernel,
        grid=(1,),
        in_specs=[
            whole(dlogits.shape), cols(SPAN, 0), cols(LANES, 1), *[whole(part.shape) for part in parts],
        ],
        out_specs=whole((rows, width)),
        out_shape=jax.ShapeDtypeStruct((rows, width), F32),
        compiler_params=pltpu.CompilerParams(vmem_limit_bytes=VMEM),
        cost_estimate=pl.CostEstimate(
            flops=2 * rows * width * (SPAN + LANES), bytes_accessed=4 * rows * (SPAN + width), transcendentals=0
        ),
        name="query_back",
    )(dlogits, wq, wk, *parts)


def middle_kernel(groups, *refs):
    refs = list(refs)
    take = lambda count: [refs.pop(0) for _ in range(count)]
    core_ref, x_hbm, dy_hbm, o_hbm, gate_ref, routes_ref, tail_ref = take(7)
    weights_in = take(8 if groups == 8 else 3)
    out_hbm, dmid_hbm, do_hbm, delta_ref, dlog_ref, gain_ref = take(6)
    outs_hbm = take(4 if groups == 8 else 3)
    x_ref, dy_ref, o_ref, comb_ref, mid_ref, normal_ref, acc_ref, dh_ref, dcomb_ref, out_ref, do_ref = take(11)
    wo_in, w1_in, w2_in = take(3)
    in_sems, out_sems = take(2)
    outs = refs
    rows, width = x_ref.shape
    part = 256
    cols = 512
    count = [0]

    def copy(source, target):
        count[0] += 1
        return pltpu.make_async_copy(source, target, in_sems.at[count[0] - 1])

    slot_copies = [copy(o_hbm.at[slot], o_ref.at[slot]) for slot in range(TOPK)]
    x_copy, dy_copy = copy(x_hbm, x_ref), copy(dy_hbm, dy_ref)
    if groups == 8:
        flat = core_ref[0]
        my_x, my_y, core = flat // 2 % 2, flat // 4 % 2, flat % 2
        wo_copies, w1_copies, w2_copies = [], [], []
        for index in range(8):
            other_core, other = index // 4, index % 4
            for y_turn in range(2):
                y = my_y ^ y_turn
                part_a = weights_in[4 * other_core + (other // 2)]
                x = my_x ^ (other // 2)
                mp = 2 * x + (core ^ other_core)
                across = pl.ds(pl.multiple_of(mp * cols, cols), cols)
                if other % 2 == 0:
                    wo_copies.append(copy(part_a.at[y_turn, :, 4:6], wo_in.at[:, y, mp, 0:2]))
                    w1_copies.append(copy(part_a.at[y_turn, :, 0:4], w1_in.at[:, y, :, :, across]))
                else:
                    part_b = weights_in[4 * other_core + 2 + y_turn]
                    x_turn = other // 2
                    wo_copies.append(copy(part_b.at[x_turn, :, 4:5], wo_in.at[:, y, mp, 2:3]))
                    w2_copies.append(copy(part_b.at[x_turn, :, 0:4], w2_in.at[:, y, :, :, across]))
    else:
        wo_copies, w1_copies, w2_copies = [
            [copy(source, target)] for source, target in zip(weights_in, (wo_in, w1_in, w2_in))
        ]
    for one in (*slot_copies, *wo_copies, x_copy, *w1_copies, dy_copy, *w2_copies):
        one.start()
    view = lambda ref: ref[...].reshape(width, -1)
    third = lambda ref, index: ref[:, :, :, index].reshape(width, cols)

    gain = gains_of(tail_ref[...])[E + 1 : E + 2]
    for one in slot_copies:
        one.wait()

    def combine(index, carry):
        mine = pl.ds(pl.multiple_of(index * part, part), part)
        gates = gate_ref[mine, :]
        weighted = [(column(gates, slot, part) * o_ref[slot, mine, :]).astype(BF16) for slot in range(TOPK)]
        comb_ref[mine, :] = place_pairs(weighted, choices(routes_ref[mine, :], part, BF16))
        return carry

    lax.fori_loop(0, rows // part, combine, 0)
    for one in (*wo_copies, x_copy):
        one.wait()
    mid = x_ref[...].astype(F32)
    if groups == 8:
        for index in range(3):
            mid = mid + dot_last(comb_ref[:, index * cols : (index + 1) * cols], third(wo_in, index))
    else:
        mid = mid + dot_last(comb_ref[...], wo_in[...])
    mid_ref[...] = mid
    normal, factor = standardize(mid)
    normal_ref[...] = normal
    h2 = (normal * gain).astype(BF16)
    for one in (*w1_copies, dy_copy, *w2_copies):
        one.wait()
    dy = dy_ref[...]
    w1, w2 = view(w1_in), view(w2_in)

    for index in range(w1.shape[1] // cols):
        span = slice(index * cols, (index + 1) * cols)
        up, down = w1[:, span], w2[:, span]
        pre = dot(h2, up)
        dact = dot(dy, down)
        sigma = jax.nn.sigmoid(pre)
        act = (pre * sigma).astype(BF16)
        dpre = (dact * (sigma * (1.0 + pre * (1.0 - sigma)))).astype(BF16)
        branch = dot_last(act, down)
        dh2 = dot_last(dpre, up)
        if index == 0:
            acc_ref[...] = branch
            dh_ref[...] = dh2
        else:
            acc_ref[...] += branch
            dh_ref[...] += dh2
        g1 = dot_first(h2, dpre).astype(BF16)
        g2 = dot_first(dy, act).astype(BF16)
        if groups != 8:
            outs[0][:, span] = g1
            outs[1][:, span] = g2
            continue
        for mine, (a, b) in ((True, (outs[0], outs[2])), (False, (outs[1], outs[3]))):

            @pl.when((core_ref[0] % 2 == index % 2) == mine)
            def _(a=a, b=b, g1=g1, g2=g2, x=index // 2):
                for owner in range(8):
                    piece = slice(owner * 64, owner * 64 + 64)
                    a[x, owner % 2, owner // 2, :64] = g1[piece]
                    b[owner % 2, x, owner // 2, :64] = g2[piece]

    out_ref[...] = (mid_ref[...] + acc_ref[...]).astype(BF16)
    out_copy = pltpu.make_async_copy(out_ref, out_hbm, out_sems.at[0])
    out_copy.start()
    dh2 = dh_ref[...]
    normal = normal_ref[...]
    gain_ref[...] = jnp.sum(dh2 * normal, 0, keepdims=True)
    dmid = dy.astype(F32) + norm_back(dh2 * gain, normal, factor)
    mid_ref[...] = dmid
    dmid_copy = pltpu.make_async_copy(mid_ref, dmid_hbm, out_sems.at[1])
    dmid_copy.start()
    dmid_b = dmid.astype(BF16)
    if groups == 8:
        for index in range(3):
            span = slice(index * cols, (index + 1) * cols)
            dcomb_ref[:, span] = dot(dmid_b, third(wo_in, index)).astype(BF16)
    else:
        dcomb_ref[...] = dot(dmid_b, wo_in[...]).astype(BF16)
    go = dot_first(dmid_b, comb_ref[...]).astype(BF16)
    if groups == 8:
        for core in range(2):

            @pl.when(core_ref[0] % 2 == core)
            def _(pairs=((outs[0], outs[2]), (outs[1], outs[3])), core=core):
                for owner in range(32):
                    z, y, x, c = owner // 8, owner // 4 % 2, owner // 2 % 2, owner % 2
                    a, b = pairs[c ^ core]
                    mine = slice(owner * 16, owner * 16 + 16)
                    a[x, y, z, 64:80] = go[mine, :512]
                    a[x, y, z, 80:] = go[mine, 512:1024]
                    b[y, x, z, 64:] = go[mine, 1024:]
    else:
        outs[2][...] = go

    grad_copies = [
        pltpu.make_async_copy(source, target, out_sems.at[3 + index])
        for index, (source, target) in enumerate(zip(outs, outs_hbm))
    ]
    for one in grad_copies:
        one.start()

    def spread(index, carry):
        mine = pl.ds(pl.multiple_of(index * part, part), part)
        gates = gate_ref[mine, :]
        routes = routes_ref[mine, :]
        lane = lane_index(part)
        dcomb = dcomb_ref[mine, :]
        gate_grads = jnp.zeros((part, LANES), F32)
        for slot, choice in enumerate(choices(routes, part, BF16)):
            picked = pick_pairs(dcomb, choice).astype(F32)
            do_ref[slot, mine, :] = (column(gates, slot, part) * picked).astype(BF16)
            total = jnp.sum(o_ref[slot, mine, :] * picked, -1, keepdims=True)
            gate_grads = jnp.where(lane == slot, total, gate_grads)
        weighted = gates * gate_grads
        delta_ref[mine, :] = weighted
        dsel = weighted - gates * jnp.sum(weighted, -1, keepdims=True)
        dlogits = jnp.zeros((part, LANES), F32)
        for slot in range(TOPK):
            dlogits = jnp.where(lane == column(routes, slot, part), column(dsel, slot, part), dlogits)
        dlog_ref[mine, :] = dlogits.astype(BF16)
        return carry

    lax.fori_loop(0, rows // part, spread, 0)
    do_copy = pltpu.make_async_copy(do_ref, do_hbm, out_sems.at[2])
    do_copy.start()
    for one in (out_copy, dmid_copy, do_copy, *grad_copies):
        one.wait()


def middle_call(groups, core, x, dy, o, gates, routes, front, weights):
    rows, width = x.shape
    hidden = 2048
    whole = lambda shape: pl.BlockSpec(shape, lambda i, s: (0,) * len(shape))
    anywhere = pl.BlockSpec(memory_space=pl.ANY)
    if groups == 8:
        grads = [(2, 2, 4, 96, 512), (2, 2, 4, 96, 512), (2, 2, 4, 80, 512), (2, 2, 4, 80, 512)]
        held = [(4, 2, 4, 3, 16, 512), (4, 2, 4, 16, hidden), (4, 2, 4, 16, hidden)]
    else:
        grads = [(width, hidden), (width, hidden), (width, SPAN)]
        held = [(width, SPAN), (width, hidden), (width, hidden)]
    return pl.pallas_call(
        functools.partial(middle_kernel, groups),
        grid_spec=pltpu.PrefetchScalarGridSpec(
            num_scalar_prefetch=1,
            grid=(1,),
            in_specs=[
                anywhere, anywhere, anywhere, whole(gates.shape), whole(routes.shape),
                pl.BlockSpec((width, LANES), lambda i, s: (0, 1)), *[anywhere] * len(weights),
            ],
            out_specs=[
                anywhere, anywhere, anywhere, whole((rows, LANES)), whole((rows, LANES)), whole((1, width)),
                *[anywhere] * len(grads),
            ],
            scratch_shapes=[
                pltpu.VMEM((rows, width), BF16),
                pltpu.VMEM((rows, width), BF16),
                pltpu.VMEM((TOPK, rows, LANES), F32),
                pltpu.VMEM((rows, SPAN), BF16),
                pltpu.VMEM((rows, width), F32),
                pltpu.VMEM((rows, width), F32),
                pltpu.VMEM((rows, width), F32),
                pltpu.VMEM((rows, width), F32),
                pltpu.VMEM((rows, SPAN), BF16),
                pltpu.VMEM((rows, width), BF16),
                pltpu.VMEM((TOPK, rows, LANES), BF16),
                *[pltpu.VMEM(shape, BF16) for shape in held],
                pltpu.SemaphoreType.DMA((42,)),
                pltpu.SemaphoreType.DMA((7,)),
                *[pltpu.VMEM(shape, BF16) for shape in grads],
            ],
        ),
        out_shape=[
            jax.ShapeDtypeStruct((rows, width), BF16),
            jax.ShapeDtypeStruct((rows, width), F32),
            jax.ShapeDtypeStruct((TOPK, rows, LANES), BF16),
            jax.ShapeDtypeStruct((rows, LANES), F32),
            jax.ShapeDtypeStruct((rows, LANES), BF16),
            jax.ShapeDtypeStruct((1, width), F32),
            *[jax.ShapeDtypeStruct(shape, BF16) for shape in grads],
        ],
        compiler_params=pltpu.CompilerParams(vmem_limit_bytes=VMEM),
        cost_estimate=pl.CostEstimate(
            flops=2 * rows * width * (6 * hidden + 3 * SPAN), bytes_accessed=16 * rows * width, transcendentals=0
        ),
        name="middle",
    )(core, x, dy, o, gates, routes, front, *weights)


def post_kernel(x_ref, h_ref, dmid_ref, dh_ref, keep_ref, recv_ref, dlog_ref, gain2_ref, w_ref, grad_ref, gk_ref, sum_ref):
    step = pl.program_id(0)
    gain = gains_of(w_ref[:, LANES:])[E : E + 1]
    normal, factor = standardize(x_ref[...].astype(F32))
    dkv = (keep_ref[...].astype(F32) + recv_ref[...].astype(F32)).astype(BF16)
    dh = dh_ref[...] + dot_last(dkv, w_ref[:, :LANES])
    grad_ref[...] = (dmid_ref[...] + norm_back(dh * gain, normal, factor)).astype(grad_ref.dtype)
    gain1 = jnp.sum(dh * normal, 0, keepdims=True)
    width = gain1.shape[1]
    row = lax.broadcasted_iota(jnp.int32, (LANES, width), 0)
    gain2 = jnp.where(step == 0, gain2_ref[...], 0.0)
    gains = jnp.where(row == E, gain1, jnp.where(row == E + 1, gain2, 0.0))
    h_turned = turned(h_ref[...])
    keyval = dot(h_turned, dkv)
    router = dot(h_turned, dlog_ref[...]) + gains.T

    @pl.when(step == 0)
    def _():
        sum_ref[:, :LANES] = keyval
        sum_ref[:, LANES:] = router

    @pl.when(step > 0)
    def _():
        sum_ref[:, :LANES] += keyval
        sum_ref[:, LANES:] += router

    @pl.when(step == pl.num_programs(0) - 1)
    def _():
        gk_ref[...] = sum_ref[...].astype(BF16)


def post_call(x, h, dmid, dh, keep, recv, dlogits, gain2, weights, tile=256):
    rows, width = x.shape
    by_row = lambda cols: pl.BlockSpec((tile, cols), lambda i: (i, 0))
    return pl.pallas_call(
        post_kernel,
        grid=(rows // tile,),
        in_specs=[
            by_row(width), by_row(width), by_row(width), by_row(width), by_row(LANES), by_row(LANES), by_row(LANES),
            pl.BlockSpec((1, width), lambda i: (0, 0)),
            pl.BlockSpec((width, 2 * LANES), lambda i: (0, 0)),
        ],
        out_specs=[by_row(width), pl.BlockSpec((width, 2 * LANES), lambda i: (0, 0))],
        out_shape=[
            jax.ShapeDtypeStruct((rows, width), BF16),
            jax.ShapeDtypeStruct((width, 2 * LANES), BF16),
        ],
        scratch_shapes=[pltpu.VMEM((width, 2 * LANES), F32)],
        compiler_params=pltpu.CompilerParams(vmem_limit_bytes=VMEM),
        cost_estimate=pl.CostEstimate(
            flops=6 * rows * width * LANES, bytes_accessed=16 * rows * width, transcendentals=0
        ),
        name="finish",
    )(x, h, dmid, dh, keep, recv, dlogits, gain2, weights)


RING = ((0, 1), (1, 2), (2, 3), (3, 0))
SWAP = ((1, 3), (3, 1))


def halves(rows, place):
    half = rows.shape[0] // 2
    outer = (place == 0) | (place == 3)
    first = lax.dynamic_slice_in_dim(rows, jnp.where(outer, half, 0), half, 0)
    second = lax.dynamic_slice_in_dim(rows, jnp.where(place == 1, half, 0), half, 0)
    return first, second


def deal(rows, sent, place):
    half = rows.shape[0] // 2
    ring = lax.ppermute(sent[0], "mp", RING)
    swap = lax.ppermute(sent[1], "mp", SWAP)
    low = jnp.where(place == 0, rows[:half], jnp.where(place == 3, swap, ring))
    high = jnp.where(place == 2, rows[half:], jnp.where(place == 1, swap, ring))
    return jnp.concatenate([low, high], 0)


def gather_back(rows, place):
    half = rows.shape[0] // 2
    first, second = halves(rows, place)
    ring = lax.ppermute(first, "mp", tuple((b, a) for a, b in RING))
    swap = lax.ppermute(second, "mp", SWAP)
    top = jnp.where(place == 0, rows[:half], jnp.where(place == 3, swap, ring))
    bottom = jnp.where(place == 2, rows[half:], jnp.where(place == 1, swap, ring))
    return jnp.concatenate([top, bottom], 0)


OTHER_CORE = ((0, 1), (1, 0), (2, 3), (3, 2))
OTHER_X = ((0, 2), (2, 0), (1, 3), (3, 1))


def swap_core(values):
    return lax.ppermute(values, "mp", OTHER_CORE)


def swap_x(values):
    return lax.ppermute(values, "mp", OTHER_X)


def swap_y(values):
    return lax.ppermute(values, "dp", tuple((i, i ^ 1) for i in range(8)))


def swap_z(values, turn):
    return lax.ppermute(values, "dp", tuple((i, i ^ (2 * turn)) for i in range(8)))


def at(values, index):
    return lax.dynamic_index_in_dim(values, index, 0, keepdims=False)


def added(left, right):
    return (left.astype(F32) + right.astype(F32)).astype(BF16)


def gather_z(shard, my_z):
    turns = [shard] + [swap_z(shard, turn) for turn in (1, 2, 3)]
    rows = []
    for z in range(4):
        row = turns[3]
        for turn in (2, 1, 0):
            row = jnp.where(my_z == z ^ turn, turns[turn], row)
        rows.append(row)
    return jnp.stack(rows)


def after(values, others):
    return lax.optimization_barrier((values, others))[0]


def tied(first, second):
    return lax.optimization_barrier((first, second))


def adam_step(param, first, second, grad, rate, decay):
    first_new = BETA_FIRST * first + (1.0 - BETA_FIRST) * grad
    second_new = BETA_SECOND * second + (1.0 - BETA_SECOND) * grad * grad
    first_hat = first_new / (1.0 - BETA_FIRST**ADAM_STEP)
    second_hat = second_new / (1.0 - BETA_SECOND**ADAM_STEP)
    param_new = param - rate * (first_hat / (jnp.sqrt(second_hat) + ADAM_EPS) + decay * param)
    return (second_new, param_new)


def update_kernel(
    rates_ref, squares_ref, gq_ref, go_ref, gk_ref, ffn_ref,
    ap_ref, am_ref, av_ref, fp_ref, fm_ref, fv_ref,
    ag_ref, avn_ref, apn_ref, fg_ref, fvn_ref, fpn_ref, norm_ref, gain_ref,
):
    norm = jnp.sqrt(jnp.sum(squares_ref[...], 0)[:1, :1])
    norm_ref[...] = norm
    factor = jnp.minimum(1.0, CLIP_NORM / norm)
    tail = AC - 2 * SPAN
    for source, span, rate in (
        (gq_ref, slice(0, SPAN), rates_ref[0]),
        (go_ref, slice(SPAN, 2 * SPAN), rates_ref[1]),
        (gk_ref, slice(2 * SPAN, AC), None),
    ):
        decay = WEIGHT_DECAY
        grad = source[...] * factor
        if rate is None:
            grad = grad[:, :tail]
            place = lax.broadcasted_iota(jnp.int32, (1, tail), 1)
            rate = jnp.where(
                place < 2 * HD, rates_ref[2], jnp.where(place < 2 * HD + E, rates_ref[3], rates_ref[4])
            )
            decay = jnp.where(place < 2 * HD + E, WEIGHT_DECAY, 0.0)
            gain_ref[...] = grad[:, tail - 2 :]
        ag_ref[:, span] = grad
        avn_ref[:, span], apn_ref[:, span] = adam_step(
            ap_ref[:, span], am_ref[:, span], av_ref[:, span], grad, rate, decay
        )
    for index in range(2):
        grad = ffn_ref[index] * factor
        fg_ref[index] = grad
        fvn_ref[index], fpn_ref[index] = adam_step(
            fp_ref[index], fm_ref[index], fv_ref[index], grad, rates_ref[5 + index], WEIGHT_DECAY
        )


def update_call(rates, squares, gq, go, gk, ffn, attn, ffn_state):
    rows = gq.shape[0]
    attn_shape = jax.ShapeDtypeStruct(attn[0].shape, F32)
    ffn_shape = jax.ShapeDtypeStruct(ffn.shape, F32)
    whole = pl.BlockSpec(memory_space=pltpu.VMEM)
    return pl.pallas_call(
        update_kernel,
        in_specs=[pl.BlockSpec(memory_space=pltpu.SMEM)] + [whole] * 11,
        out_specs=[whole] * 8,
        out_shape=[
            attn_shape, attn_shape, attn_shape, ffn_shape, ffn_shape, ffn_shape,
            jax.ShapeDtypeStruct((1, 1), F32), jax.ShapeDtypeStruct((rows, 2), F32),
        ],
        compiler_params=pltpu.CompilerParams(vmem_limit_bytes=VMEM),
        name="update",
    )(rates, squares, gq, go, gk, ffn, *attn, *ffn_state)


ALL = ("dp", "mp")


def shards(
    tokens, cotangent, routes, starts, attn_param, attn_first, attn_second, ffn_param, ffn_first, ffn_second, rates
):
    local_rows, width = tokens.shape
    place = lax.axis_index("mp")
    devices = lax.axis_size("mp")
    groups = lax.axis_size("dp")
    block = local_rows // 2
    manual = groups == 8
    _, depth, cols = ffn_param.shape
    my_x, my_y, my_z = place // 2, lax.axis_index("dp") % 2, lax.axis_index("dp") // 2
    flat = (lax.axis_index("dp") * devices + place).astype(jnp.int32)

    side = jnp.concatenate([routes, starts[:, None] // block], 1).astype(BF16)
    side = jnp.pad(side, ((0, 0), (0, LANES - TOPK - 1)))
    mine = jnp.concatenate([tokens, side], 1)
    sent = halves(mine, place)
    x = deal(mine, sent, place)

    attn_b = attn_param.astype(BF16)
    ffn_b = ffn_param.astype(BF16)
    pad = jnp.zeros((attn_b.shape[0], 2 * LANES - (AC - 2 * SPAN)), BF16)
    wk = jnp.concatenate([attn_b[:, 2 * SPAN :], pad], 1)
    wq = attn_b[:, :SPAN]
    wo = attn_b[:, SPAN : 2 * SPAN]
    if manual:
        wk, wq = after((wk, wq), sent)
        wk = lax.all_to_all(jnp.broadcast_to(wk, (groups * devices, *wk.shape)), ALL, 0, 0, tiled=True)
        wk = wk.reshape(-1, 2 * LANES)
        along = jnp.stack([wq] + [swap_z(wq, turn) for turn in (1, 2, 3)])
        ffn_b, wo = after((ffn_b, wo), along)
        along = jnp.stack([along, swap_y(along)])
        along = after(along, x)
        near = jnp.stack([along, swap_x(along)]).reshape(16, *wq.shape)
        far = swap_core(near)
        chunk = [ffn_b[0].reshape(-1, 16, cols), wo[None, :, :cols], wo[None, :, cols : 2 * cols]]
        chunk += [ffn_b[1].reshape(-1, 16, cols), wo[None, :, 2 * cols :]]
        chunk = gather_z(jnp.concatenate(chunk, 0), my_z)
    else:
        wk = lax.all_gather(wk, ALL, axis=0, tiled=True)
        wq_all = lax.all_gather(wq, ALL, axis=0, tiled=True).reshape(4, 2, 2, 2, 16, -1)
        wq_all = wq_all.transpose(3, 2, 1, 0, 4, 5).reshape(2, 16, 16, -1)
        near, far = wq_all[0], wq_all[1]
        wo_full = lax.all_gather(wo, ALL, axis=0, tiled=True)
        ffn_all = lax.all_gather(ffn_b, ALL, axis=0, tiled=False)
        ffn_all = ffn_all.reshape(groups, devices, 2, depth, cols).transpose(2, 0, 3, 1, 4)
        ffn_all = ffn_all.reshape(2, groups * depth, devices * cols)
        weights = [wo_full, ffn_all[0], ffn_all[1]]

    marks = x[:, width : width + TOPK + 1].astype(jnp.int32)
    x = x[:, :width]
    routes_x = marks[:, :TOPK]
    tile = 128
    tiles = local_rows // tile
    pieces = tiles // 2
    index = jnp.arange(tiles, dtype=jnp.int32)
    low = index < pieces
    here = jnp.where(low, place * block + index * tile, (2 * devices - 1 - place) * block + (index - pieces) * tile)
    lower = jnp.where(low, marks[0, TOPK], marks[block, TOPK]) * block
    where = jnp.stack([here, lower, jnp.full((tiles,), place)]).astype(jnp.int32)

    h, kv, gates = embed_call(x, routes_x, wk)
    kv = kv.reshape(2, block, LANES)
    kv_x = swap_x(kv)
    me = flat.reshape(1) if manual else jnp.zeros((1,), jnp.int32)
    q, wq_full = query_call(me, h, routes_x, near, far)
    if manual:
        a_own = chunk[:, :6]
        b_own = after(chunk[:, 6:], kv_x)
        a_own = jnp.stack([a_own, swap_y(a_own)])
        b_own = jnp.stack([b_own, swap_x(b_own)])
        a_far, b_far = swap_x(a_own), swap_y(b_own)
        weights = [a_own, a_far, b_own, b_far]
        weights += [swap_core(part) for part in weights]
        q = after(q, (a_own, b_own))
    cotangent = after(cotangent, kv_x)
    dy = deal(cotangent, halves(cotangent, place), place)
    o, logs, keys, values = attend_call(where, q, [kv, swap_core(kv), kv_x, swap_core(kv_x)], tile)
    out, dmid, do, deltas, dlogits, gain2, *grads = middle_call(
        groups, flat.reshape(1), x, dy, o, gates, routes_x, wk, weights
    )
    layer_out = gather_back(out, place)

    def back(piece, carried, before):
        return attend_back_call(
            piece, pieces, groups, where, q, do, logs, deltas, routes_x, keys, values, carried, h, before
        )

    all_parts, carried = [], ()
    if manual:
        a_keep, a_send, b_keep, b_send = grads
        moving = (swap_core(a_send), swap_core(b_send))
    for piece in range(pieces - 1):
        all_part, *carried = back(piece, carried, all_parts)
        all_parts.append(all_part)
        if not manual:
            continue
        carried, moving = tied(carried, moving)
        a_in, b_in = moving
        if piece == 0:
            a_now = (a_keep, a_in)
            b_now = (b_keep, b_in)
            turn_a, turn_b, swap_a, swap_b = my_x, my_y, swap_x, swap_y
        elif piece == 1:
            a_now = (a_keep, a_in)
            b_now = (b_keep, b_in)
            turn_a, turn_b, swap_a, swap_b = my_y, my_x, swap_y, swap_x
        if piece < 2:
            a_send = added(at(a_now[0], 1 - turn_a), at(a_now[1], 1 - turn_a))
            b_send = added(at(b_now[0], 1 - turn_b), at(b_now[1], 1 - turn_b))
            a_keep = added(at(a_now[0], turn_a), at(a_now[1], turn_a))
            b_keep = added(at(b_now[0], turn_b), at(b_now[1], turn_b))
            (a_send, b_send, a_keep, b_keep), carried = tied((a_send, b_send, a_keep, b_keep), carried)
            moving = (swap_a(a_send), swap_b(b_send))
        else:
            both = jnp.concatenate([added(a_keep, a_in), added(b_keep, b_in)], 1)
            both, carried = tied(both, carried)
            moving = [swap_z(at(both, my_z ^ turn), turn) for turn in (1, 2, 3)]
            chunk_keep = at(both, my_z)
    all_part, kv_keep, kv_send, gq_keep, gq_send = back(pieces - 1, carried, all_parts)
    all_parts.append(all_part)
    kv_in = swap_core(kv_send)
    kv_out = added(kv_keep[1], kv_in[1])
    kv_keep = added(kv_keep[0], kv_in[0]).reshape(local_rows, LANES)
    kv_recv = swap_x(kv_out).reshape(local_rows, LANES)
    dh = query_back_call(dlogits, wq_full, wk, after(all_parts, (kv_out, kv_keep)))
    if manual:
        gq_in = swap_core(gq_send)
        gq_send = added(at(gq_keep, 1 - my_y), at(gq_in, 1 - my_y))
        gq_keep = added(at(gq_keep, my_y), at(gq_in, my_y))
        gq_y = added(gq_keep, swap_y(gq_send))
        gq = after(gq_y, dh)
        gq_in = [swap_z(at(gq, my_z ^ turn), turn) for turn in (1, 2, 3)]
        gq = sum((part.astype(F32) for part in gq_in), at(gq, my_z).astype(F32)).astype(BF16)
        gq_raw = at(gq, my_x).astype(F32) + swap_x(at(gq, 1 - my_x)).astype(F32)
    grad, gk = post_call(x, h, dmid, dh, kv_keep, kv_recv, dlogits, gain2, wk)
    if manual:
        gk = after(gk, gq_y)
        grad = after(grad, gq)
    input_grad = gather_back(grad, place).astype(F32)

    if manual:
        gk = lax.all_to_all(gk.reshape(groups * devices, -1, 2 * LANES), ALL, 0, 0, tiled=True)
        gk_raw = jnp.sum(gk.astype(F32), 0)
        chunk_raw = sum((part.astype(F32) for part in moving), chunk_keep.astype(F32))
        rows = depth
        ffn_raw = jnp.stack([chunk_raw[:rows], chunk_raw[rows + 32 : 2 * rows + 32]])
        go_raw = jnp.concatenate(
            [chunk_raw[rows : rows + 16], chunk_raw[rows + 16 : rows + 32], chunk_raw[2 * rows + 32 :]], 1
        )
    else:
        g1, g2, go = grads
        ffn_local = jnp.stack([g1, g2]).reshape(2, groups, depth, devices, cols).transpose(1, 3, 0, 2, 4)
        ffn_local = ffn_local.reshape(groups * devices * 2 * depth, cols)
        ffn_raw = lax.psum_scatter(ffn_local, ALL, scatter_dimension=0, tiled=True).astype(F32)
        ffn_raw = ffn_raw.reshape(2, depth, cols)
        go_raw = lax.psum_scatter(go, ALL, scatter_dimension=0, tiled=True).astype(F32)
        gq_raw = lax.psum_scatter(gq_keep, ALL, scatter_dimension=0, tiled=True).astype(F32)
        gk_raw = lax.psum_scatter(gk, ALL, scatter_dimension=0, tiled=True).astype(F32)
    squares = sum(jnp.sum(part * part) for part in (gq_raw, go_raw, gk_raw, ffn_raw))
    if manual:
        squares = jnp.broadcast_to(squares, (groups * devices, 8, LANES))
        squares = lax.all_to_all(squares, ALL, 0, 0, tiled=True)
    else:
        squares = jnp.broadcast_to(lax.psum(squares, ALL), (1, 8, LANES))
    attn_grad, attn_second_new, attn_new, ffn_grad, ffn_second_new, ffn_new, grad_norm, gain_grad = update_call(
        rates, squares, gq_raw, go_raw, gk_raw, ffn_raw,
        (attn_param, attn_first, attn_second), (ffn_param, ffn_first, ffn_second),
    )
    return (
        layer_out,
        input_grad,
        attn_grad,
        attn_second_new,
        attn_new,
        ffn_grad,
        ffn_second_new,
        ffn_new,
        grad_norm.reshape(()),
        gain_grad,
    )


def solution(mesh):
    by_row = P(ALL, None)
    by_ffn = P(None, "dp", "mp")
    return jax.shard_map(
        shards,
        mesh=mesh,
        in_specs=(by_row, by_row, by_row, P(ALL), by_row, by_row, by_row, by_ffn, by_ffn, by_ffn, P()),
        out_specs=(by_row, by_row, by_row, by_row, by_row, by_ffn, by_ffn, by_ffn, P(), by_row),
        check_vma=False,
    )
```

```python
import functools
import math

import jax
import jax.numpy as jnp
from jax import lax
from jax.experimental import pallas as pl
from jax.experimental.pallas import tpu as pltpu
from jax.sharding import PartitionSpec as P

HD = 64
E = 24
TOPK = 8
ADAM_STEP = 7
AC = 3226
SPAN = E * HD
PAIRS = E // 2
LANES = 128

NORM_EPS = 1e-05
MASKED = -1e30
CLIP_NORM = 0.1
BETA_FIRST = 0.9
BETA_SECOND = 0.95
ADAM_EPS = 1e-08
WEIGHT_DECAY = 0.1

SCALE = HD ** (-0.5)
LOG2E = math.log2(math.e)
SAFE_SCORE = 40.0
SAFE_VALUE = 1e15
VMEM = 58 << 20

F32 = jnp.float32
BF16 = jnp.bfloat16


def dot(left, right):
    return jnp.dot(left, right, preferred_element_type=F32)


def dot_last(left, right):
    return lax.dot_general(left, right, (((1,), (1,)), ((), ())), preferred_element_type=F32)


def dot_first(left, right):
    return lax.dot_general(left, right, (((0,), (0,)), ((), ())), preferred_element_type=F32)


def turned(values):
    return values.astype(F32).T.astype(values.dtype)


def standardize(values):
    centred = values - jnp.mean(values, -1, keepdims=True)
    factor = lax.rsqrt(jnp.mean(centred * centred, -1, keepdims=True) + NORM_EPS)
    return (centred * factor, factor)


def norm_back(grad_normal, normal, factor):
    return factor * (
        grad_normal
        - jnp.mean(grad_normal, -1, keepdims=True)
        - normal * jnp.mean(grad_normal * normal, -1, keepdims=True)
    )


def lane_index(rows):
    return lax.broadcasted_iota(jnp.int32, (rows, LANES), 1)


def column(values, index, rows):
    return jnp.broadcast_to(values[:, index : index + 1], (rows, LANES))


def pick_pairs(table, chosen):
    picked = jnp.zeros(chosen.shape, table.dtype)
    for pair in range(PAIRS):
        picked = jnp.where(chosen == 2 * pair, table[:, pair * LANES : (pair + 1) * LANES], picked)
    return picked


def place_pairs(parts, chosen):
    columns = []
    for pair in range(PAIRS):
        total = jnp.zeros(chosen[0].shape, parts[0].dtype)
        for part, choice in zip(parts, chosen):
            total = jnp.where(choice == 2 * pair, part, total)
        columns.append(total)
    return jnp.concatenate(columns, 1)


def choices(routes, rows, dtype):
    half = (lane_index(rows) >= HD).astype(jnp.int32)
    return [(column(routes, slot, rows) - half).astype(F32).astype(dtype) for slot in range(TOPK)]


def gains_of(tail):
    return tail.astype(F32).T


def flat_of(index):
    x, y, z = index // 8, index // 4 % 2, index % 4
    return ((z * 2 + y) * 2 + x) * 2


def embed_kernel(x_ref, routes_ref, w_ref, h_ref, kv_ref, gate_ref):
    rows = x_ref.shape[0]
    gain = gains_of(w_ref[:, LANES:])[E : E + 1]
    normal, _ = standardize(x_ref[...].astype(F32))
    h = (normal * gain).astype(BF16)
    h_ref[...] = h
    proj = dot(h, w_ref[...])
    kv_ref[...] = proj[:, :LANES].astype(BF16)
    logits = proj[:, LANES:]
    routes = routes_ref[...]
    lane = lane_index(rows)
    columns = [column(routes, slot, rows) for slot in range(TOPK)]
    chosen = jnp.zeros((rows, LANES), jnp.bool_)
    for route in columns:
        chosen = chosen | (lane == route)
    peak = jnp.max(jnp.where(chosen, logits, MASKED), -1, keepdims=True)
    expo = jnp.where(chosen, jnp.exp(jnp.where(chosen, logits - peak, 0.0)), 0.0)
    dense = expo / jnp.sum(expo, -1, keepdims=True)
    gates = jnp.zeros((rows, LANES), F32)
    for slot, route in enumerate(columns):
        hit = jnp.where(lane == route, dense, 0.0)
        gates = jnp.where(lane == slot, jnp.sum(hit, -1, keepdims=True), gates)
    gate_ref[...] = gates


def embed_call(x, routes, weights, tile=256):
    rows, width = x.shape
    by_row = lambda count: pl.BlockSpec((tile, count), lambda i: (i, 0))
    return pl.pallas_call(
        embed_kernel,
        grid=(rows // tile,),
        in_specs=[by_row(width), by_row(TOPK), pl.BlockSpec(weights.shape, lambda i: (0, 0))],
        out_specs=[by_row(width), by_row(LANES), by_row(LANES)],
        out_shape=[
            jax.ShapeDtypeStruct((rows, width), BF16),
            jax.ShapeDtypeStruct((rows, LANES), BF16),
            jax.ShapeDtypeStruct((rows, LANES), F32),
        ],
        compiler_params=pltpu.CompilerParams(vmem_limit_bytes=12 << 20),
        cost_estimate=pl.CostEstimate(
            flops=4 * rows * width * LANES, bytes_accessed=8 * rows * width, transcendentals=0
        ),
        name="embed",
    )(x, routes, weights)


def query_kernel(me_ref, h_ref, routes_ref, near_ref, far_ref, q_ref, w_ref, sems):
    rows = h_ref.shape[0]
    pieces, piece, _ = near_ref.shape

    @pl.when(pl.program_id(0) == 0)
    def _():
        copies = []
        for core, part in enumerate((near_ref, far_ref)):
            for index in range(pieces):
                owner = me_ref[0] ^ (flat_of(index) + core)
                first = pl.multiple_of(owner * piece, piece)
                copies.append(
                    pltpu.make_async_copy(
                        part.at[index], w_ref.at[pl.ds(first, piece), :], sems.at[core * pieces + index]
                    )
                )
        for copy in copies:
            copy.start()
        for copy in copies:
            copy.wait()

    table = dot(h_ref[...], w_ref[...]).astype(BF16)
    for slot, choice in enumerate(choices(routes_ref[...], rows, BF16)):
        q_ref[slot] = pick_pairs(table, choice)


def query_call(me, h, routes, near, far, tile=256):
    rows, width = h.shape
    pieces, piece, cols = near.shape
    by_row = lambda count: pl.BlockSpec((tile, count), lambda i, s: (i, 0))
    return pl.pallas_call(
        query_kernel,
        grid_spec=pltpu.PrefetchScalarGridSpec(
            num_scalar_prefetch=1,
            grid=(rows // tile,),
            in_specs=[
                by_row(width),
                by_row(TOPK),
                pl.BlockSpec(memory_space=pl.ANY),
                pl.BlockSpec(memory_space=pl.ANY),
            ],
            out_specs=[
                pl.BlockSpec((TOPK, tile, LANES), lambda i, s: (0, i, 0)),
                pl.BlockSpec((width, cols), lambda i, s: (0, 0)),
            ],
            scratch_shapes=[pltpu.SemaphoreType.DMA((2 * pieces,))],
        ),
        out_shape=[
            jax.ShapeDtypeStruct((TOPK, rows, LANES), BF16),
            jax.ShapeDtypeStruct((width, cols), BF16),
        ],
        compiler_params=pltpu.CompilerParams(vmem_limit_bytes=16 << 20),
        cost_estimate=pl.CostEstimate(
            flops=2 * rows * width * cols, bytes_accessed=8 * rows * width + 2 * width * cols, transcendentals=0
        ),
        name="query",
    )(me, h, routes, near, far)


def spread_keyval(device, kv_refs, key_ref, value_ref):
    devices = len(kv_refs)
    _, block, _ = kv_refs[0].shape
    low_half = lane_index(block) < HD
    for index in range(devices):
        for high in range(2):
            rows = kv_refs[index][high].astype(F32)
            rolled = pltpu.roll(rows, HD, 1)
            span = block_of(device ^ index, high, devices, block)
            key_ref[span, :] = jnp.where(low_half, rows, rolled).astype(BF16)
            value_ref[span, :] = jnp.where(low_half, rolled, rows).astype(BF16)


def block_of(device, high, devices, block):
    place = 2 * devices - 1 - device if high else device
    return pl.ds(pl.multiple_of(place * block, block), block)


def attend_kernel(place_ref, q_ref, *refs):
    *kv_refs, o_ref, log_ref, key_ref, plain_ref, value_ref, acc_ref, peak_ref, bound_ref = refs
    step = pl.program_id(0)
    slots, tile, _ = q_ref.shape
    rows = slots * tile
    width = 512

    @pl.when(step == 0)
    def _():
        spread_keyval(place_ref[2, 0], kv_refs, key_ref, plain_ref)
        value_ref[:, :LANES] = plain_ref[...]
        value_ref[:, LANES:] = jnp.ones((value_ref.shape[0], LANES), BF16)
        keys = key_ref[...].astype(F32)
        bound_ref[0] = jnp.max(jnp.sum(keys * keys, -1, keepdims=True)) * 0.5
        bound_ref[1] = jnp.max(jnp.abs(plain_ref[...].astype(F32)))

    here = place_ref[0, step]
    lower = pl.multiple_of(place_ref[1, step], width)
    q = q_ref[...].reshape(rows, LANES)
    qf = q.astype(F32)
    longest = jnp.max(jnp.sum(qf * qf, -1, keepdims=True))
    plain = (longest * bound_ref[0] <= (SAFE_SCORE / SCALE) ** 2) & (bound_ref[1] <= SAFE_VALUE)
    full = (here - lower) // width
    last = pl.multiple_of(lower + full * width, width)
    token = lax.broadcasted_iota(jnp.int32, (tile, width), 0) + here
    allowed = (lax.broadcasted_iota(jnp.int32, (tile, width), 1) + last) <= token
    allowed = jnp.broadcast_to(allowed[None], (slots, tile, width)).reshape(rows, width)

    def finish(out, logs):
        o_ref[...] = out.reshape(slots, tile, LANES)
        logs = logs.reshape(slots, tile, LANES)
        lane = lane_index(tile)
        packed = jnp.zeros((tile, LANES), F32)
        for slot in range(slots):
            packed = jnp.where(lane == slot, logs[slot], packed)
        log_ref[...] = packed

    pairs = full // 2

    @pl.when(plain)
    def _():
        for count in (1, 2):

            @pl.when(full % 2 == count - 1)
            def _(count=count):
                span = pl.ds(pl.multiple_of(lower + pairs * 2 * width, width), count * width)
                expo = jnp.exp2(dot_last(q, key_ref[span, :]) * (SCALE * LOG2E))
                edge = jnp.where(allowed, expo[:, (count - 1) * width :], 0.0).astype(BF16)
                expo = jnp.concatenate([expo[:, :width].astype(BF16), edge], 1) if count > 1 else edge
                acc_ref[...] = dot(expo, value_ref[span, :])

        def body(index, carry):
            span = pl.ds(pl.multiple_of(lower + index * 2 * width, width), 2 * width)
            expo = jnp.exp2(dot_last(q, key_ref[span, :]) * (SCALE * LOG2E)).astype(BF16)
            acc_ref[...] += dot(expo, value_ref[span, :])
            return carry

        lax.fori_loop(0, pairs, body, 0)
        total = acc_ref[:, LANES:]
        finish(acc_ref[:, :LANES] / total, jnp.log2(total))

    @pl.when(jnp.logical_not(plain))
    def _():
        def scaled(span):
            return dot_last(q, key_ref[span, :]) * (SCALE * LOG2E)

        scores = jnp.where(allowed, scaled(pl.ds(last, width)), MASKED)
        peak = jnp.max(scores, -1, keepdims=True)
        peak_ref[...] = jnp.broadcast_to(peak, (rows, LANES))
        acc_ref[...] = dot(jnp.exp2(scores - peak).astype(BF16), value_ref[pl.ds(last, width), :])

        def body(index, carry):
            span = pl.ds(pl.multiple_of(lower + index * width, width), width)
            scores = scaled(span)
            before = peak_ref[:, :1]
            peak = jnp.maximum(before, jnp.max(scores, -1, keepdims=True))
            peak_ref[...] = jnp.broadcast_to(peak, (rows, LANES))
            expo = jnp.exp2(scores - peak).astype(BF16)
            acc_ref[...] = acc_ref[...] * jnp.exp2(before - peak) + dot(expo, value_ref[span, :])
            return carry

        lax.fori_loop(0, full, body, 0)
        total = acc_ref[:, LANES:]
        finish(acc_ref[:, :LANES] / total, peak_ref[...] + jnp.log2(total))


def attend_call(place, q, kv, tile=128):
    slots, rows, _ = q.shape
    count = len(kv) * kv[0].shape[0] * kv[0].shape[1]
    return pl.pallas_call(
        attend_kernel,
        grid_spec=pltpu.PrefetchScalarGridSpec(
            num_scalar_prefetch=1,
            grid=(rows // tile,),
            in_specs=[
                pl.BlockSpec((slots, tile, LANES), lambda i, s: (0, i, 0)),
                *[pl.BlockSpec(part.shape, lambda i, s: (0, 0, 0)) for part in kv],
            ],
            out_specs=[
                pl.BlockSpec((slots, tile, LANES), lambda i, s: (0, i, 0)),
                pl.BlockSpec((tile, LANES), lambda i, s: (i, 0)),
                pl.BlockSpec((count, LANES), lambda i, s: (0, 0)),
                pl.BlockSpec((count, LANES), lambda i, s: (0, 0)),
            ],
            scratch_shapes=[
                pltpu.VMEM((count, 2 * LANES), BF16),
                pltpu.VMEM((slots * tile, 2 * LANES), F32),
                pltpu.VMEM((slots * tile, LANES), F32),
                pltpu.SMEM((2,), F32),
            ],
        ),
        out_shape=[
            jax.ShapeDtypeStruct((slots, rows, LANES), F32),
            jax.ShapeDtypeStruct((rows, LANES), F32),
            jax.ShapeDtypeStruct((count, LANES), BF16),
            jax.ShapeDtypeStruct((count, LANES), BF16),
        ],
        compiler_params=pltpu.CompilerParams(vmem_limit_bytes=24 << 20),
        cost_estimate=pl.CostEstimate(
            flops=8 * slots * rows * count * LANES, bytes_accessed=8 * slots * rows * LANES, transcendentals=0
        ),
        name="attend",
    )(place, q, *kv)


def attend_back_kernel(piece, pieces, groups, *refs):
    first, final = piece == 0, piece == pieces - 1
    refs = list(refs)
    take = lambda count: [refs.pop(0) for _ in range(count)]
    place_ref, q_ref, do_ref, log_ref, delta_ref, routes_ref, key_ref, value_ref = take(8)
    if not first:
        (sums_in,) = take(1)
    if final:
        (h_ref,) = take(1)
        before_refs = take(pieces - 1)
    (all_ref,) = take(1)
    outs = take(4 if final else 1)
    dq_ref, dkey_ref, dvalue_ref, sems = take(4)
    step = pl.program_id(0)
    steps = pl.num_programs(0)
    slots, tile, _ = q_ref.shape
    rows = slots * tile
    width = 512

    def carry_copies():
        return [
            pltpu.make_async_copy(sums_in.at[0], dkey_ref.at[pl.ds(0, HD), :], sems.at[0]),
            pltpu.make_async_copy(sums_in.at[1], dvalue_ref.at[pl.ds(0, HD), :], sems.at[1]),
        ]

    @pl.when(step == 0)
    def _():
        if first:
            dkey_ref[:HD] = jnp.zeros_like(dkey_ref[:HD])
            dvalue_ref[:HD] = jnp.zeros_like(dvalue_ref[:HD])
        else:
            for copy in carry_copies():
                copy.start()
        dkey_ref[HD:] = jnp.zeros_like(dkey_ref[HD:])
        dvalue_ref[HD:] = jnp.zeros_like(dvalue_ref[HD:])

    here = place_ref[0, piece + pieces * step]
    lower = place_ref[1, piece + pieces * step]
    q = q_ref[...].reshape(rows, LANES)
    do = do_ref[...].reshape(rows, LANES)
    logs = log_ref[...]
    deltas = delta_ref[...]
    logs = jnp.concatenate([column(logs, slot, tile) for slot in range(slots)], 0)
    deltas = jnp.concatenate([column(deltas, slot, tile) for slot in range(slots)], 0)
    full = (here - lower) // width
    last = pl.multiple_of(lower + full * width, width)
    token = lax.broadcasted_iota(jnp.int32, (tile, width), 0) + here
    allowed = (lax.broadcasted_iota(jnp.int32, (tile, width), 1) + last) <= token
    allowed = jnp.broadcast_to(allowed[None], (slots, tile, width)).reshape(rows, width)

    def wide(values):
        return jnp.concatenate([values] * (width // LANES), 1)

    if not first:

        @pl.when(step == 0)
        def _():
            for copy in carry_copies():
                copy.wait()

    def one(start, masked):
        span = pl.ds(start, width)
        keys = key_ref[span, :]
        scores = dot_last(q, keys)
        probs = jnp.exp2(scores * (SCALE * LOG2E) - wide(logs))
        if masked:
            probs = jnp.where(allowed, probs, 0.0)
        dprobs = dot_last(do, value_ref[span, :])
        dscores = (probs * (dprobs - wide(deltas))).astype(BF16)
        dvalue_ref[:, span] += dot_first(do, probs.astype(BF16))
        dkey_ref[:, span] += dot_first(q, dscores)
        return dot(dscores, keys)

    dq_ref[...] = one(last, True)

    def body(index, carry):
        dq_ref[...] += one(pl.multiple_of(lower + index * width, width), False)
        return carry

    lax.fori_loop(0, full, body, 0)

    def sum_copies():
        return [
            pltpu.make_async_copy(dkey_ref.at[pl.ds(0, HD), :], outs[0].at[0], sems.at[0]),
            pltpu.make_async_copy(dvalue_ref.at[pl.ds(0, HD), :], outs[0].at[1], sems.at[1]),
        ]

    if not final:

        @pl.when(step == steps - 1)
        def _():
            dkey_ref[:HD] += dkey_ref[HD:]
            dvalue_ref[:HD] += dvalue_ref[HD:]
            for copy in sum_copies():
                copy.start()

    dq = (dq_ref[...] * SCALE).astype(BF16).reshape(slots, tile, LANES)
    mine = pl.ds(pl.multiple_of(step * tile, tile), tile)
    all_ref[mine, :] = place_pairs([dq[slot] for slot in range(slots)], choices(routes_ref[...], tile, BF16))

    @pl.when(step == steps - 1)
    def _():
        if not final:
            for copy in sum_copies():
                copy.wait()
            return
        kv_keep, kv_send, gq_keep, gq_send = outs
        _, _, block, _ = kv_keep.shape
        device = place_ref[2, 0]
        for index in range(4):
            target = kv_send if index % 2 else kv_keep
            for high in range(2):
                span = block_of(device ^ index, high, 4, block)
                dkeys = (dkey_ref[:HD, span] + dkey_ref[HD:, span]) * SCALE
                dvalues = dvalue_ref[:HD, span] + dvalue_ref[HD:, span]
                target[index // 2, high] = jnp.concatenate([dkeys, dvalues], 0).T.astype(BF16)
        gq = dot(turned(h_ref[...]), in_rows([*before_refs, all_ref], tile))
        if groups == 8:
            scatter_rows(gq, gq_keep, gq_send, device % 2)
        else:
            gq_keep[...] = gq.astype(BF16)
            gq_send[...] = jnp.zeros_like(gq_send)


def in_rows(parts, tile):
    return jnp.concatenate([part[:tile] for part in parts] + [part[tile:] for part in parts], 0)


def scatter_rows(grad, keep, send, core):
    for x in range(2):
        for y in range(2):
            for z in range(4):
                base = (((z * 2 + y) * 2 + x) * 2) * 16
                low = grad[base : base + 16].astype(BF16)
                high = grad[base + 16 : base + 32].astype(BF16)
                keep[y, z, x] = jnp.where(core == 0, low, high)
                send[y, z, x] = jnp.where(core == 0, high, low)


def attend_back_call(piece, pieces, groups, where, q, do, logs, deltas, routes, keys, values, carried, h, before):
    slots, rows, _ = q.shape
    count = keys.shape[0]
    width = h.shape[1]
    tile = rows // (2 * pieces)
    final = piece == pieces - 1
    whole = lambda shape: pl.BlockSpec(shape, lambda i, s: (0,) * len(shape))
    anywhere = pl.BlockSpec(memory_space=pl.ANY)
    by_slot = pl.BlockSpec((slots, tile, LANES), lambda i, s: (0, piece + pieces * i, 0))
    by_row = lambda cols: pl.BlockSpec((tile, cols), lambda i, s: (piece + pieces * i, 0))
    in_specs = [
        by_slot, by_slot, by_row(LANES), by_row(LANES), by_row(TOPK), whole(keys.shape), whole(values.shape),
    ]
    in_specs += [anywhere] * len(carried)
    extra = [h, *before] if final else []
    in_specs += [whole(array.shape) for array in extra]
    out_specs = [whole((2 * tile, SPAN))]
    out_shape = [jax.ShapeDtypeStruct((2 * tile, SPAN), BF16)]
    if final:
        kv_shape = (2, 2, rows // 2, LANES)
        gq_shape = (2, 4, 2, 16, SPAN) if groups == 8 else (width, SPAN)
        off_shape = gq_shape if groups == 8 else (8, LANES)
        for shape in (kv_shape, kv_shape, gq_shape, off_shape):
            out_specs.append(whole(shape))
            out_shape.append(jax.ShapeDtypeStruct(shape, BF16))
    else:
        out_specs.append(anywhere)
        out_shape.append(jax.ShapeDtypeStruct((2, HD, count), F32))
    return pl.pallas_call(
        functools.partial(attend_back_kernel, piece, pieces, groups),
        grid_spec=pltpu.PrefetchScalarGridSpec(
            num_scalar_prefetch=1,
            grid=(2,),
            in_specs=in_specs,
            out_specs=out_specs,
            scratch_shapes=[
                pltpu.VMEM((slots * tile, LANES), F32),
                pltpu.VMEM((LANES, count), F32),
                pltpu.VMEM((LANES, count), F32),
                pltpu.SemaphoreType.DMA((2,)),
            ],
        ),
        out_shape=out_shape,
        compiler_params=pltpu.CompilerParams(vmem_limit_bytes=20 << 20),
        cost_estimate=pl.CostEstimate(
            flops=10 * slots * 2 * tile * count * LANES, bytes_accessed=16 * slots * tile * LANES, transcendentals=0
        ),
        name="attend_back",
    )(where, q, do, logs, deltas, routes, keys, values, *carried, *extra)


def query_back_kernel(dlog_ref, wq_ref, wr_ref, *refs):
    *all_refs, dh_ref = refs
    rows = in_rows(all_refs, all_refs[0].shape[0] // 2)
    dh_ref[...] = dot_last(rows, wq_ref[...]) + dot_last(dlog_ref[...], wr_ref[...])


def query_back_call(dlogits, wq, wk, parts):
    rows = dlogits.shape[0]
    width = wq.shape[0]
    cols = lambda size, index: pl.BlockSpec((width, size), lambda i: (0, index))
    whole = lambda shape: pl.BlockSpec(shape, lambda i: (0,) * len(shape))
    return pl.pallas_call(
        query_back_kernel,
        grid=(1,),
        in_specs=[
            whole(dlogits.shape), cols(SPAN, 0), cols(LANES, 1), *[whole(part.shape) for part in parts],
        ],
        out_specs=whole((rows, width)),
        out_shape=jax.ShapeDtypeStruct((rows, width), F32),
        compiler_params=pltpu.CompilerParams(vmem_limit_bytes=24 << 20),
        cost_estimate=pl.CostEstimate(
            flops=2 * rows * width * (SPAN + LANES), bytes_accessed=4 * rows * (SPAN + width), transcendentals=0
        ),
        name="query_back",
    )(dlogits, wq, wk, *parts)


def middle_kernel(groups, *refs):
    refs = list(refs)
    take = lambda count: [refs.pop(0) for _ in range(count)]
    core_ref, x_hbm, dy_hbm, o_hbm, gate_ref, routes_ref, tail_ref = take(7)
    weights_in = take(8 if groups == 8 else 3)
    out_hbm, dmid_hbm, do_hbm, delta_ref, dlog_ref, gain_ref = take(6)
    outs_hbm = take(4 if groups == 8 else 3)
    x_ref, dy_ref, o_ref, comb_ref, mid_ref, normal_ref, acc_ref, dh_ref, dcomb_ref, out_ref, do_ref = take(11)
    wo_in, w1_in, w2_in = take(3)
    in_sems, out_sems = take(2)
    outs = refs
    rows, width = x_ref.shape
    part = 256
    cols = 512
    count = [0]

    def copy(source, target):
        count[0] += 1
        return pltpu.make_async_copy(source, target, in_sems.at[count[0] - 1])

    slot_copies = [copy(o_hbm.at[slot], o_ref.at[slot]) for slot in range(TOPK)]
    x_copy, dy_copy = copy(x_hbm, x_ref), copy(dy_hbm, dy_ref)
    if groups == 8:
        flat = core_ref[0]
        my_x, my_y, core = flat // 2 % 2, flat // 4 % 2, flat % 2
        wo_copies, w1_copies, w2_copies = [], [], []
        for index in range(8):
            other_core, other = index // 4, index % 4
            for y_turn in range(2):
                y = my_y ^ y_turn
                part_a = weights_in[4 * other_core + (other // 2)]
                x = my_x ^ (other // 2)
                mp = 2 * x + (core ^ other_core)
                across = pl.ds(pl.multiple_of(mp * cols, cols), cols)
                if other % 2 == 0:
                    wo_copies.append(copy(part_a.at[y_turn, :, 4:6], wo_in.at[:, y, mp, 0:2]))
                    w1_copies.append(copy(part_a.at[y_turn, :, 0:4], w1_in.at[:, y, :, :, across]))
                else:
                    part_b = weights_in[4 * other_core + 2 + y_turn]
                    x_turn = other // 2
                    wo_copies.append(copy(part_b.at[x_turn, :, 4:5], wo_in.at[:, y, mp, 2:3]))
                    w2_copies.append(copy(part_b.at[x_turn, :, 0:4], w2_in.at[:, y, :, :, across]))
    else:
        wo_copies, w1_copies, w2_copies = [
            [copy(source, target)] for source, target in zip(weights_in, (wo_in, w1_in, w2_in))
        ]
    for one in (*slot_copies, *wo_copies, x_copy, *w1_copies, dy_copy, *w2_copies):
        one.start()
    view = lambda ref: ref[...].reshape(width, -1)
    third = lambda ref, index: ref[:, :, :, index].reshape(width, cols)

    gain = gains_of(tail_ref[...])[E + 1 : E + 2]
    for one in slot_copies:
        one.wait()

    def combine(index, carry):
        mine = pl.ds(pl.multiple_of(index * part, part), part)
        gates = gate_ref[mine, :]
        weighted = [(column(gates, slot, part) * o_ref[slot, mine, :]).astype(BF16) for slot in range(TOPK)]
        comb_ref[mine, :] = place_pairs(weighted, choices(routes_ref[mine, :], part, BF16))
        return carry

    lax.fori_loop(0, rows // part, combine, 0)
    for one in (*wo_copies, x_copy):
        one.wait()
    mid = x_ref[...].astype(F32)
    if groups == 8:
        for index in range(3):
            mid = mid + dot_last(comb_ref[:, index * cols : (index + 1) * cols], third(wo_in, index))
    else:
        mid = mid + dot_last(comb_ref[...], wo_in[...])
    mid_ref[...] = mid
    normal, factor = standardize(mid)
    normal_ref[...] = normal
    h2 = (normal * gain).astype(BF16)
    for one in (*w1_copies, dy_copy, *w2_copies):
        one.wait()
    dy = dy_ref[...]
    w1, w2 = view(w1_in), view(w2_in)

    for index in range(w1.shape[1] // cols):
        span = slice(index * cols, (index + 1) * cols)
        up, down = w1[:, span], w2[:, span]
        pre = dot(h2, up)
        dact = dot(dy, down)
        sigma = jax.nn.sigmoid(pre)
        act = (pre * sigma).astype(BF16)
        dpre = (dact * (sigma * (1.0 + pre * (1.0 - sigma)))).astype(BF16)
        branch = dot_last(act, down)
        dh2 = dot_last(dpre, up)
        if index == 0:
            acc_ref[...] = branch
            dh_ref[...] = dh2
        else:
            acc_ref[...] += branch
            dh_ref[...] += dh2
        g1 = dot_first(h2, dpre).astype(BF16)
        g2 = dot_first(dy, act).astype(BF16)
        if groups != 8:
            outs[0][:, span] = g1
            outs[1][:, span] = g2
            continue
        for mine, (a, b) in ((True, (outs[0], outs[2])), (False, (outs[1], outs[3]))):

            @pl.when((core_ref[0] % 2 == index % 2) == mine)
            def _(a=a, b=b, g1=g1, g2=g2, x=index // 2):
                for owner in range(8):
                    piece = slice(owner * 64, owner * 64 + 64)
                    a[x, owner % 2, owner // 2, :64] = g1[piece]
                    b[owner % 2, x, owner // 2, :64] = g2[piece]

    out_ref[...] = (mid_ref[...] + acc_ref[...]).astype(BF16)
    out_copy = pltpu.make_async_copy(out_ref, out_hbm, out_sems.at[0])
    out_copy.start()
    dh2 = dh_ref[...]
    normal = normal_ref[...]
    gain_ref[...] = jnp.sum(dh2 * normal, 0, keepdims=True)
    dmid = dy.astype(F32) + norm_back(dh2 * gain, normal, factor)
    mid_ref[...] = dmid
    dmid_copy = pltpu.make_async_copy(mid_ref, dmid_hbm, out_sems.at[1])
    dmid_copy.start()
    dmid_b = dmid.astype(BF16)
    if groups == 8:
        for index in range(3):
            span = slice(index * cols, (index + 1) * cols)
            dcomb_ref[:, span] = dot(dmid_b, third(wo_in, index)).astype(BF16)
    else:
        dcomb_ref[...] = dot(dmid_b, wo_in[...]).astype(BF16)
    go = dot_first(dmid_b, comb_ref[...]).astype(BF16)
    if groups == 8:
        for core in range(2):

            @pl.when(core_ref[0] % 2 == core)
            def _(pairs=((outs[0], outs[2]), (outs[1], outs[3])), core=core):
                for owner in range(32):
                    z, y, x, c = owner // 8, owner // 4 % 2, owner // 2 % 2, owner % 2
                    a, b = pairs[c ^ core]
                    mine = slice(owner * 16, owner * 16 + 16)
                    a[x, y, z, 64:80] = go[mine, :512]
                    a[x, y, z, 80:] = go[mine, 512:1024]
                    b[y, x, z, 64:] = go[mine, 1024:]
    else:
        outs[2][...] = go

    grad_copies = [
        pltpu.make_async_copy(source, target, out_sems.at[3 + index])
        for index, (source, target) in enumerate(zip(outs, outs_hbm))
    ]
    for one in grad_copies:
        one.start()

    def spread(index, carry):
        mine = pl.ds(pl.multiple_of(index * part, part), part)
        gates = gate_ref[mine, :]
        routes = routes_ref[mine, :]
        lane = lane_index(part)
        dcomb = dcomb_ref[mine, :]
        gate_grads = jnp.zeros((part, LANES), F32)
        for slot, choice in enumerate(choices(routes, part, BF16)):
            picked = pick_pairs(dcomb, choice).astype(F32)
            do_ref[slot, mine, :] = (column(gates, slot, part) * picked).astype(BF16)
            total = jnp.sum(o_ref[slot, mine, :] * picked, -1, keepdims=True)
            gate_grads = jnp.where(lane == slot, total, gate_grads)
        weighted = gates * gate_grads
        delta_ref[mine, :] = weighted
        dsel = weighted - gates * jnp.sum(weighted, -1, keepdims=True)
        dlogits = jnp.zeros((part, LANES), F32)
        for slot in range(TOPK):
            dlogits = jnp.where(lane == column(routes, slot, part), column(dsel, slot, part), dlogits)
        dlog_ref[mine, :] = dlogits.astype(BF16)
        return carry

    lax.fori_loop(0, rows // part, spread, 0)
    do_copy = pltpu.make_async_copy(do_ref, do_hbm, out_sems.at[2])
    do_copy.start()
    for one in (out_copy, dmid_copy, do_copy, *grad_copies):
        one.wait()


def middle_call(groups, core, x, dy, o, gates, routes, front, weights):
    rows, width = x.shape
    hidden = 2048
    whole = lambda shape: pl.BlockSpec(shape, lambda i, s: (0,) * len(shape))
    anywhere = pl.BlockSpec(memory_space=pl.ANY)
    if groups == 8:
        grads = [(2, 2, 4, 96, 512), (2, 2, 4, 96, 512), (2, 2, 4, 80, 512), (2, 2, 4, 80, 512)]
        held = [(4, 2, 4, 3, 16, 512), (4, 2, 4, 16, hidden), (4, 2, 4, 16, hidden)]
    else:
        grads = [(width, hidden), (width, hidden), (width, SPAN)]
        held = [(width, SPAN), (width, hidden), (width, hidden)]
    return pl.pallas_call(
        functools.partial(middle_kernel, groups),
        grid_spec=pltpu.PrefetchScalarGridSpec(
            num_scalar_prefetch=1,
            grid=(1,),
            in_specs=[
                anywhere, anywhere, anywhere, whole(gates.shape), whole(routes.shape),
                pl.BlockSpec((width, LANES), lambda i, s: (0, 1)), *[anywhere] * len(weights),
            ],
            out_specs=[
                anywhere, anywhere, anywhere, whole((rows, LANES)), whole((rows, LANES)), whole((1, width)),
                *[anywhere] * len(grads),
            ],
            scratch_shapes=[
                pltpu.VMEM((rows, width), BF16),
                pltpu.VMEM((rows, width), BF16),
                pltpu.VMEM((TOPK, rows, LANES), F32),
                pltpu.VMEM((rows, SPAN), BF16),
                pltpu.VMEM((rows, width), F32),
                pltpu.VMEM((rows, width), F32),
                pltpu.VMEM((rows, width), F32),
                pltpu.VMEM((rows, width), F32),
                pltpu.VMEM((rows, SPAN), BF16),
                pltpu.VMEM((rows, width), BF16),
                pltpu.VMEM((TOPK, rows, LANES), BF16),
                *[pltpu.VMEM(shape, BF16) for shape in held],
                pltpu.SemaphoreType.DMA((42,)),
                pltpu.SemaphoreType.DMA((7,)),
                *[pltpu.VMEM(shape, BF16) for shape in grads],
            ],
        ),
        out_shape=[
            jax.ShapeDtypeStruct((rows, width), BF16),
            jax.ShapeDtypeStruct((rows, width), F32),
            jax.ShapeDtypeStruct((TOPK, rows, LANES), BF16),
            jax.ShapeDtypeStruct((rows, LANES), F32),
            jax.ShapeDtypeStruct((rows, LANES), BF16),
            jax.ShapeDtypeStruct((1, width), F32),
            *[jax.ShapeDtypeStruct(shape, BF16) for shape in grads],
        ],
        compiler_params=pltpu.CompilerParams(vmem_limit_bytes=48 << 20),
        cost_estimate=pl.CostEstimate(
            flops=2 * rows * width * (6 * hidden + 3 * SPAN), bytes_accessed=16 * rows * width, transcendentals=0
        ),
        name="middle",
    )(core, x, dy, o, gates, routes, front, *weights)


def post_kernel(x_ref, h_ref, dmid_ref, dh_ref, keep_ref, recv_ref, dlog_ref, gain2_ref, w_ref, grad_ref, gk_ref, sum_ref):
    step = pl.program_id(0)
    gain = gains_of(w_ref[:, LANES:])[E : E + 1]
    normal, factor = standardize(x_ref[...].astype(F32))
    dkv = (keep_ref[...].astype(F32) + recv_ref[...].astype(F32)).astype(BF16)
    dh = dh_ref[...] + dot_last(dkv, w_ref[:, :LANES])
    grad_ref[...] = (dmid_ref[...] + norm_back(dh * gain, normal, factor)).astype(grad_ref.dtype)
    gain1 = jnp.sum(dh * normal, 0, keepdims=True)
    width = gain1.shape[1]
    row = lax.broadcasted_iota(jnp.int32, (LANES, width), 0)
    gain2 = jnp.where(step == 0, gain2_ref[...], 0.0)
    gains = jnp.where(row == E, gain1, jnp.where(row == E + 1, gain2, 0.0))
    h_turned = turned(h_ref[...])
    keyval = dot(h_turned, dkv)
    router = dot(h_turned, dlog_ref[...]) + gains.T

    @pl.when(step == 0)
    def _():
        sum_ref[:, :LANES] = keyval
        sum_ref[:, LANES:] = router

    @pl.when(step > 0)
    def _():
        sum_ref[:, :LANES] += keyval
        sum_ref[:, LANES:] += router

    @pl.when(step == pl.num_programs(0) - 1)
    def _():
        gk_ref[...] = sum_ref[...].astype(BF16)


def post_call(x, h, dmid, dh, keep, recv, dlogits, gain2, weights, tile=256):
    rows, width = x.shape
    by_row = lambda cols: pl.BlockSpec((tile, cols), lambda i: (i, 0))
    return pl.pallas_call(
        post_kernel,
        grid=(rows // tile,),
        in_specs=[
            by_row(width), by_row(width), by_row(width), by_row(width), by_row(LANES), by_row(LANES), by_row(LANES),
            pl.BlockSpec((1, width), lambda i: (0, 0)),
            pl.BlockSpec((width, 2 * LANES), lambda i: (0, 0)),
        ],
        out_specs=[by_row(width), pl.BlockSpec((width, 2 * LANES), lambda i: (0, 0))],
        out_shape=[
            jax.ShapeDtypeStruct((rows, width), BF16),
            jax.ShapeDtypeStruct((width, 2 * LANES), BF16),
        ],
        scratch_shapes=[pltpu.VMEM((width, 2 * LANES), F32)],
        compiler_params=pltpu.CompilerParams(vmem_limit_bytes=16 << 20),
        cost_estimate=pl.CostEstimate(
            flops=6 * rows * width * LANES, bytes_accessed=16 * rows * width, transcendentals=0
        ),
        name="finish",
    )(x, h, dmid, dh, keep, recv, dlogits, gain2, weights)


RING = ((0, 1), (1, 2), (2, 3), (3, 0))
SWAP = ((1, 3), (3, 1))


def halves(rows, place):
    half = rows.shape[0] // 2
    outer = (place == 0) | (place == 3)
    first = lax.dynamic_slice_in_dim(rows, jnp.where(outer, half, 0), half, 0)
    second = lax.dynamic_slice_in_dim(rows, jnp.where(place == 1, half, 0), half, 0)
    return first, second


def deal(rows, sent, place, ready=None):
    half = rows.shape[0] // 2
    ring = lax.ppermute(sent[0], "mp", RING)
    swap = lax.ppermute(sent[1], "mp", SWAP)
    if ready is not None:
        ring, swap = after((ring, swap), ready)
    low = jnp.where(place == 0, rows[:half], jnp.where(place == 3, swap, ring))
    high = jnp.where(place == 2, rows[half:], jnp.where(place == 1, swap, ring))
    return jnp.concatenate([low, high], 0)


def gather_back(rows, place):
    half = rows.shape[0] // 2
    first, second = halves(rows, place)
    ring = lax.ppermute(first, "mp", tuple((b, a) for a, b in RING))
    swap = lax.ppermute(second, "mp", SWAP)
    top = jnp.where(place == 0, rows[:half], jnp.where(place == 3, swap, ring))
    bottom = jnp.where(place == 2, rows[half:], jnp.where(place == 1, swap, ring))
    return jnp.concatenate([top, bottom], 0)


OTHER_CORE = ((0, 1), (1, 0), (2, 3), (3, 2))
OTHER_X = ((0, 2), (2, 0), (1, 3), (3, 1))


def swap_core(values):
    return lax.ppermute(values, "mp", OTHER_CORE)


def swap_x(values):
    return lax.ppermute(values, "mp", OTHER_X)


def swap_y(values):
    return lax.ppermute(values, "dp", tuple((i, i ^ 1) for i in range(8)))


def swap_z(values, turn):
    return lax.ppermute(values, "dp", tuple((i, i ^ (2 * turn)) for i in range(8)))


def at(values, index):
    return lax.dynamic_index_in_dim(values, index, 0, keepdims=False)


def added(left, right):
    return (left.astype(F32) + right.astype(F32)).astype(BF16)


def gather_z(shard, my_z):
    turns = [shard] + [swap_z(shard, turn) for turn in (1, 2, 3)]
    rows = []
    for z in range(4):
        row = turns[3]
        for turn in (2, 1, 0):
            row = jnp.where(my_z == z ^ turn, turns[turn], row)
        rows.append(row)
    return jnp.stack(rows)


def after(values, others):
    return lax.optimization_barrier((values, others))[0]


def tied(first, second):
    return lax.optimization_barrier((first, second))


def adam_step(param, first, second, grad, rate, decay):
    first_new = BETA_FIRST * first + (1.0 - BETA_FIRST) * grad
    second_new = BETA_SECOND * second + (1.0 - BETA_SECOND) * grad * grad
    first_hat = first_new / (1.0 - BETA_FIRST**ADAM_STEP)
    second_hat = second_new / (1.0 - BETA_SECOND**ADAM_STEP)
    param_new = param - rate * (first_hat / (jnp.sqrt(second_hat) + ADAM_EPS) + decay * param)
    return (second_new, param_new)


def update_kernel(
    rates_ref, squares_ref, gq_ref, go_ref, gk_ref, ffn_ref,
    ap_ref, am_ref, av_ref, fp_ref, fm_ref, fv_ref,
    ag_ref, avn_ref, apn_ref, fg_ref, fvn_ref, fpn_ref, norm_ref, gain_ref,
):
    norm = jnp.sqrt(jnp.sum(squares_ref[...], 0)[:1, :1])
    norm_ref[...] = norm
    factor = jnp.minimum(1.0, CLIP_NORM / norm)
    tail = AC - 2 * SPAN
    for source, span, rate in (
        (gq_ref, slice(0, SPAN), rates_ref[0]),
        (go_ref, slice(SPAN, 2 * SPAN), rates_ref[1]),
        (gk_ref, slice(2 * SPAN, AC), None),
    ):
        decay = WEIGHT_DECAY
        grad = source[...] * factor
        if rate is None:
            grad = grad[:, :tail]
            place = lax.broadcasted_iota(jnp.int32, (1, tail), 1)
            rate = jnp.where(
                place < 2 * HD, rates_ref[2], jnp.where(place < 2 * HD + E, rates_ref[3], rates_ref[4])
            )
            decay = jnp.where(place < 2 * HD + E, WEIGHT_DECAY, 0.0)
            gain_ref[...] = grad[:, tail - 2 :]
        ag_ref[:, span] = grad
        avn_ref[:, span], apn_ref[:, span] = adam_step(
            ap_ref[:, span], am_ref[:, span], av_ref[:, span], grad, rate, decay
        )
    for index in range(2):
        grad = ffn_ref[index] * factor
        fg_ref[index] = grad
        fvn_ref[index], fpn_ref[index] = adam_step(
            fp_ref[index], fm_ref[index], fv_ref[index], grad, rates_ref[5 + index], WEIGHT_DECAY
        )


def update_call(rates, squares, gq, go, gk, ffn, attn, ffn_state):
    rows = gq.shape[0]
    attn_shape = jax.ShapeDtypeStruct(attn[0].shape, F32)
    ffn_shape = jax.ShapeDtypeStruct(ffn.shape, F32)
    whole = pl.BlockSpec(memory_space=pltpu.VMEM)
    return pl.pallas_call(
        update_kernel,
        in_specs=[pl.BlockSpec(memory_space=pltpu.SMEM)] + [whole] * 11,
        out_specs=[whole] * 8,
        out_shape=[
            attn_shape, attn_shape, attn_shape, ffn_shape, ffn_shape, ffn_shape,
            jax.ShapeDtypeStruct((1, 1), F32), jax.ShapeDtypeStruct((rows, 2), F32),
        ],
        compiler_params=pltpu.CompilerParams(vmem_limit_bytes=24 << 20),
        name="update",
    )(rates, squares, gq, go, gk, ffn, *attn, *ffn_state)


ALL = ("dp", "mp")


def shards(
    tokens, cotangent, routes, starts, attn_param, attn_first, attn_second, ffn_param, ffn_first, ffn_second, rates
):
    local_rows, width = tokens.shape
    place = lax.axis_index("mp")
    devices = lax.axis_size("mp")
    groups = lax.axis_size("dp")
    block = local_rows // 2
    manual = groups == 8
    _, depth, cols = ffn_param.shape
    my_x, my_y, my_z = place // 2, lax.axis_index("dp") % 2, lax.axis_index("dp") // 2
    flat = (lax.axis_index("dp") * devices + place).astype(jnp.int32)

    side = jnp.concatenate([routes, starts[:, None] // block], 1).astype(BF16)
    side = jnp.pad(side, ((0, 0), (0, LANES - TOPK - 1)))
    mine = jnp.concatenate([tokens, side], 1)
    sent = halves(mine, place)
    x = deal(mine, sent, place)

    attn_b = attn_param.astype(BF16)
    ffn_b = ffn_param.astype(BF16)
    pad = jnp.zeros((attn_b.shape[0], 2 * LANES - (AC - 2 * SPAN)), BF16)
    wk = jnp.concatenate([attn_b[:, 2 * SPAN :], pad], 1)
    wq = attn_b[:, :SPAN]
    wo = attn_b[:, SPAN : 2 * SPAN]
    if manual:
        wk, wq = after((wk, wq), sent)
        wk = lax.all_to_all(jnp.broadcast_to(wk, (groups * devices, *wk.shape)), ALL, 0, 0, tiled=True)
        wk = wk.reshape(-1, 2 * LANES)
        along = jnp.stack([wq] + [swap_z(wq, turn) for turn in (1, 2, 3)])
        ffn_b, wo = after((ffn_b, wo), along)
        along = after(along, x)
        along = jnp.stack([along, swap_y(along)])
        near = jnp.stack([along, swap_x(along)]).reshape(16, *wq.shape)
        far = swap_core(near)
        chunk = [ffn_b[0].reshape(-1, 16, cols), wo[None, :, :cols], wo[None, :, cols : 2 * cols]]
        chunk += [ffn_b[1].reshape(-1, 16, cols), wo[None, :, 2 * cols :]]
        chunk = gather_z(jnp.concatenate(chunk, 0), my_z)
    else:
        wk = lax.all_gather(wk, ALL, axis=0, tiled=True)
        wq_all = lax.all_gather(wq, ALL, axis=0, tiled=True).reshape(4, 2, 2, 2, 16, -1)
        wq_all = wq_all.transpose(3, 2, 1, 0, 4, 5).reshape(2, 16, 16, -1)
        near, far = wq_all[0], wq_all[1]
        wo_full = lax.all_gather(wo, ALL, axis=0, tiled=True)
        ffn_all = lax.all_gather(ffn_b, ALL, axis=0, tiled=False)
        ffn_all = ffn_all.reshape(groups, devices, 2, depth, cols).transpose(2, 0, 3, 1, 4)
        ffn_all = ffn_all.reshape(2, groups * depth, devices * cols)
        weights = [wo_full, ffn_all[0], ffn_all[1]]

    marks = x[:, width : width + TOPK + 1].astype(jnp.int32)
    x = x[:, :width]
    routes_x = marks[:, :TOPK]
    tile = 128
    tiles = local_rows // tile
    pieces = tiles // 2
    index = jnp.arange(tiles, dtype=jnp.int32)
    low = index < pieces
    here = jnp.where(low, place * block + index * tile, (2 * devices - 1 - place) * block + (index - pieces) * tile)
    lower = jnp.where(low, marks[0, TOPK], marks[block, TOPK]) * block
    where = jnp.stack([here, lower, jnp.full((tiles,), place)]).astype(jnp.int32)

    h, kv, gates = embed_call(x, routes_x, wk)
    kv = kv.reshape(2, block, LANES)
    kv_x = swap_x(kv)
    me = flat.reshape(1) if manual else jnp.zeros((1,), jnp.int32)
    if manual:
        chunk = after(chunk, kv)
        a_own = chunk[:, :6]
        b_own = chunk[:, 6:]
        a_own = jnp.stack([a_own, swap_y(a_own)])
        b_own = jnp.stack([b_own, swap_x(b_own)])
        a_far, b_far = swap_x(a_own), swap_y(b_own)
        weights = [a_own, a_far, b_own, b_far]
        near, far = after((near, far), (a_own, b_own))
    q, wq_full = query_call(me, h, routes_x, near, far)
    o, logs, keys, values = attend_call(where, q, [kv, swap_core(kv), kv_x, swap_core(kv_x)], tile)
    if manual:
        own = [swap_core(a_own), swap_core(b_own)]
        a_far, b_far = after((a_far, b_far), logs)
        weights += [own[0], swap_core(a_far), own[1], swap_core(b_far)]
        cotangent = after(cotangent, (q, own))
    else:
        cotangent = after(cotangent, q)
    dy = deal(cotangent, halves(cotangent, place), place, logs)
    out, dmid, do, deltas, dlogits, gain2, *grads = middle_call(
        groups, flat.reshape(1), x, dy, o, gates, routes_x, wk, weights
    )
    layer_out = gather_back(out, place)

    def back(piece, carried, before):
        return attend_back_call(
            piece, pieces, groups, where, q, do, logs, deltas, routes_x, keys, values, carried, h, before
        )

    all_parts, carried = [], ()
    if manual:
        a_keep, a_send, b_keep, b_send = grads
        moving = (swap_core(a_send), swap_core(b_send))
    for piece in range(pieces - 1):
        all_part, *carried = back(piece, carried, all_parts)
        all_parts.append(all_part)
        if not manual:
            continue
        carried, moving = tied(carried, moving)
        a_in, b_in = moving
        if piece == 0:
            a_now = (a_keep, a_in)
            b_now = (b_keep, b_in)
            turn_a, turn_b, swap_a, swap_b = my_x, my_y, swap_x, swap_y
        elif piece == 1:
            a_now = (a_keep, a_in)
            b_now = (b_keep, b_in)
            turn_a, turn_b, swap_a, swap_b = my_y, my_x, swap_y, swap_x
        if piece < 2:
            a_send = added(at(a_now[0], 1 - turn_a), at(a_now[1], 1 - turn_a))
            b_send = added(at(b_now[0], 1 - turn_b), at(b_now[1], 1 - turn_b))
            a_keep = added(at(a_now[0], turn_a), at(a_now[1], turn_a))
            b_keep = added(at(b_now[0], turn_b), at(b_now[1], turn_b))
            (a_send, b_send, a_keep, b_keep), carried = tied((a_send, b_send, a_keep, b_keep), carried)
            moving = (swap_a(a_send), swap_b(b_send))
        else:
            both = jnp.concatenate([added(a_keep, a_in), added(b_keep, b_in)], 1)
            both, carried = tied(both, carried)
            moving = [swap_z(at(both, my_z ^ turn), turn) for turn in (1, 2, 3)]
            chunk_keep = at(both, my_z)
    all_part, kv_keep, kv_send, gq_keep, gq_send = back(pieces - 1, carried, all_parts)
    all_parts.append(all_part)
    kv_in = swap_core(kv_send)
    kv_out = added(kv_keep[1], kv_in[1])
    kv_keep = added(kv_keep[0], kv_in[0]).reshape(local_rows, LANES)
    kv_recv = swap_x(kv_out).reshape(local_rows, LANES)
    dh = query_back_call(dlogits, wq_full, wk, after(all_parts, (kv_out, kv_keep)))
    if manual:
        gq_in = swap_core(gq_send)
        gq_send = added(at(gq_keep, 1 - my_y), at(gq_in, 1 - my_y))
        gq_keep = added(at(gq_keep, my_y), at(gq_in, my_y))
        gq_y = added(gq_keep, swap_y(gq_send))
        gq = after(gq_y, dh)
        gq_in = [swap_z(at(gq, my_z ^ turn), turn) for turn in (1, 2, 3)]
        gq = sum((part.astype(F32) for part in gq_in), at(gq, my_z).astype(F32)).astype(BF16)
        gq_raw = at(gq, my_x).astype(F32) + swap_x(at(gq, 1 - my_x)).astype(F32)
    grad, gk = post_call(x, h, dmid, dh, kv_keep, kv_recv, dlogits, gain2, wk)
    if manual:
        gk = after(gk, gq)
        grad = after(grad, gq)
    input_grad = gather_back(grad, place).astype(F32)

    if manual:
        gk = lax.all_to_all(gk.reshape(groups * devices, -1, 2 * LANES), ALL, 0, 0, tiled=True)
        gk_raw = jnp.sum(gk.astype(F32), 0)
        chunk_raw = sum((part.astype(F32) for part in moving), chunk_keep.astype(F32))
        rows = depth
        ffn_raw = jnp.stack([chunk_raw[:rows], chunk_raw[rows + 32 : 2 * rows + 32]])
        go_raw = jnp.concatenate(
            [chunk_raw[rows : rows + 16], chunk_raw[rows + 16 : rows + 32], chunk_raw[2 * rows + 32 :]], 1
        )
    else:
        g1, g2, go = grads
        ffn_local = jnp.stack([g1, g2]).reshape(2, groups, depth, devices, cols).transpose(1, 3, 0, 2, 4)
        ffn_local = ffn_local.reshape(groups * devices * 2 * depth, cols)
        ffn_raw = lax.psum_scatter(ffn_local, ALL, scatter_dimension=0, tiled=True).astype(F32)
        ffn_raw = ffn_raw.reshape(2, depth, cols)
        go_raw = lax.psum_scatter(go, ALL, scatter_dimension=0, tiled=True).astype(F32)
        gq_raw = lax.psum_scatter(gq_keep, ALL, scatter_dimension=0, tiled=True).astype(F32)
        gk_raw = lax.psum_scatter(gk, ALL, scatter_dimension=0, tiled=True).astype(F32)
    squares = sum(jnp.sum(part * part) for part in (gq_raw, go_raw, gk_raw, ffn_raw))
    if manual:
        squares = jnp.broadcast_to(squares, (groups * devices, 8, LANES))
        squares = lax.all_to_all(squares, ALL, 0, 0, tiled=True)
    else:
        squares = jnp.broadcast_to(lax.psum(squares, ALL), (1, 8, LANES))
    attn_grad, attn_second_new, attn_new, ffn_grad, ffn_second_new, ffn_new, grad_norm, gain_grad = update_call(
        rates, squares, gq_raw, go_raw, gk_raw, ffn_raw,
        (attn_param, attn_first, attn_second), (ffn_param, ffn_first, ffn_second),
    )
    return (
        layer_out,
        input_grad,
        attn_grad,
        attn_second_new,
        attn_new,
        ffn_grad,
        ffn_second_new,
        ffn_new,
        grad_norm.reshape(()),
        gain_grad,
    )


def solution(mesh):
    by_row = P(ALL, None)
    by_ffn = P(None, "dp", "mp")
    return jax.shard_map(
        shards,
        mesh=mesh,
        in_specs=(by_row, by_row, by_row, P(ALL), by_row, by_row, by_row, by_ffn, by_ffn, by_ffn, P()),
        out_specs=(by_row, by_row, by_row, by_row, by_row, by_ffn, by_ffn, by_ffn, P(), by_row),
        check_vma=False,
    )
```

```python
import functools
import math

import jax
import jax.numpy as jnp
from jax import lax
from jax.experimental import pallas as pl
from jax.experimental.pallas import tpu as pltpu
from jax.sharding import PartitionSpec as P

HD = 64
E = 24
TOPK = 8
ADAM_STEP = 7
AC = 3226
SPAN = E * HD
PAIRS = E // 2
LANES = 128

NORM_EPS = 1e-05
MASKED = -1e30
CLIP_NORM = 0.1
BETA_FIRST = 0.9
BETA_SECOND = 0.95
ADAM_EPS = 1e-08
WEIGHT_DECAY = 0.1

SCALE = HD ** (-0.5)
LOG2E = math.log2(math.e)
SAFE_SCORE = 40.0
SAFE_VALUE = 1e15
VMEM = 58 << 20

F32 = jnp.float32
BF16 = jnp.bfloat16


def dot(left, right):
    return jnp.dot(left, right, preferred_element_type=F32)


def dot_last(left, right):
    return lax.dot_general(left, right, (((1,), (1,)), ((), ())), preferred_element_type=F32)


def dot_first(left, right):
    return lax.dot_general(left, right, (((0,), (0,)), ((), ())), preferred_element_type=F32)


def turned(values):
    return values.astype(F32).T.astype(values.dtype)


def standardize(values):
    centred = values - jnp.mean(values, -1, keepdims=True)
    factor = lax.rsqrt(jnp.mean(centred * centred, -1, keepdims=True) + NORM_EPS)
    return (centred * factor, factor)


def norm_back(grad_normal, normal, factor):
    return factor * (
        grad_normal
        - jnp.mean(grad_normal, -1, keepdims=True)
        - normal * jnp.mean(grad_normal * normal, -1, keepdims=True)
    )


def lane_index(rows):
    return lax.broadcasted_iota(jnp.int32, (rows, LANES), 1)


def column(values, index, rows):
    return jnp.broadcast_to(values[:, index : index + 1], (rows, LANES))


def pick_pairs(table, chosen):
    picked = jnp.zeros(chosen.shape, table.dtype)
    for pair in range(PAIRS):
        picked = jnp.where(chosen == 2 * pair, table[:, pair * LANES : (pair + 1) * LANES], picked)
    return picked


def place_pairs(parts, chosen):
    columns = []
    for pair in range(PAIRS):
        total = jnp.zeros(chosen[0].shape, parts[0].dtype)
        for part, choice in zip(parts, chosen):
            total = jnp.where(choice == 2 * pair, part, total)
        columns.append(total)
    return jnp.concatenate(columns, 1)


def choices(routes, rows, dtype):
    half = (lane_index(rows) >= HD).astype(jnp.int32)
    return [(column(routes, slot, rows) - half).astype(F32).astype(dtype) for slot in range(TOPK)]


def gains_of(tail):
    return tail.astype(F32).T


def flat_of(index):
    x, y, z = index // 8, index // 4 % 2, index % 4
    return ((z * 2 + y) * 2 + x) * 2


def embed_kernel(x_ref, routes_ref, w_ref, h_ref, kv_ref, gate_ref):
    rows = x_ref.shape[0]
    gain = gains_of(w_ref[:, LANES:])[E : E + 1]
    normal, _ = standardize(x_ref[...].astype(F32))
    h = (normal * gain).astype(BF16)
    h_ref[...] = h
    proj = dot(h, w_ref[...])
    kv_ref[...] = proj[:, :LANES].astype(BF16)
    logits = proj[:, LANES:]
    routes = routes_ref[...]
    lane = lane_index(rows)
    columns = [column(routes, slot, rows) for slot in range(TOPK)]
    chosen = jnp.zeros((rows, LANES), jnp.bool_)
    for route in columns:
        chosen = chosen | (lane == route)
    peak = jnp.max(jnp.where(chosen, logits, MASKED), -1, keepdims=True)
    expo = jnp.where(chosen, jnp.exp(jnp.where(chosen, logits - peak, 0.0)), 0.0)
    dense = expo / jnp.sum(expo, -1, keepdims=True)
    gates = jnp.zeros((rows, LANES), F32)
    for slot, route in enumerate(columns):
        hit = jnp.where(lane == route, dense, 0.0)
        gates = jnp.where(lane == slot, jnp.sum(hit, -1, keepdims=True), gates)
    gate_ref[...] = gates


def embed_call(x, routes, weights, tile=256):
    rows, width = x.shape
    by_row = lambda count: pl.BlockSpec((tile, count), lambda i: (i, 0))
    return pl.pallas_call(
        embed_kernel,
        grid=(rows // tile,),
        in_specs=[by_row(width), by_row(TOPK), pl.BlockSpec(weights.shape, lambda i: (0, 0))],
        out_specs=[by_row(width), by_row(LANES), by_row(LANES)],
        out_shape=[
            jax.ShapeDtypeStruct((rows, width), BF16),
            jax.ShapeDtypeStruct((rows, LANES), BF16),
            jax.ShapeDtypeStruct((rows, LANES), F32),
        ],
        compiler_params=pltpu.CompilerParams(vmem_limit_bytes=12 << 20),
        cost_estimate=pl.CostEstimate(
            flops=4 * rows * width * LANES, bytes_accessed=8 * rows * width, transcendentals=0
        ),
        name="embed",
    )(x, routes, weights)


def query_kernel(me_ref, h_ref, routes_ref, near_ref, far_ref, q_ref, w_ref, sems):
    rows = h_ref.shape[0]
    pieces, piece, _ = near_ref.shape

    @pl.when(pl.program_id(0) == 0)
    def _():
        copies = []
        for core, part in enumerate((near_ref, far_ref)):
            for index in range(pieces):
                owner = me_ref[0] ^ (flat_of(index) + core)
                first = pl.multiple_of(owner * piece, piece)
                copies.append(
                    pltpu.make_async_copy(
                        part.at[index], w_ref.at[pl.ds(first, piece), :], sems.at[core * pieces + index]
                    )
                )
        for copy in copies:
            copy.start()
        for copy in copies:
            copy.wait()

    table = dot(h_ref[...], w_ref[...]).astype(BF16)
    for slot, choice in enumerate(choices(routes_ref[...], rows, BF16)):
        q_ref[slot] = pick_pairs(table, choice)


def query_call(me, h, routes, near, far, tile=256):
    rows, width = h.shape
    pieces, piece, cols = near.shape
    by_row = lambda count: pl.BlockSpec((tile, count), lambda i, s: (i, 0))
    return pl.pallas_call(
        query_kernel,
        grid_spec=pltpu.PrefetchScalarGridSpec(
            num_scalar_prefetch=1,
            grid=(rows // tile,),
            in_specs=[
                by_row(width),
                by_row(TOPK),
                pl.BlockSpec(memory_space=pl.ANY),
                pl.BlockSpec(memory_space=pl.ANY),
            ],
            out_specs=[
                pl.BlockSpec((TOPK, tile, LANES), lambda i, s: (0, i, 0)),
                pl.BlockSpec((width, cols), lambda i, s: (0, 0)),
            ],
            scratch_shapes=[pltpu.SemaphoreType.DMA((2 * pieces,))],
        ),
        out_shape=[
            jax.ShapeDtypeStruct((TOPK, rows, LANES), BF16),
            jax.ShapeDtypeStruct((width, cols), BF16),
        ],
        compiler_params=pltpu.CompilerParams(vmem_limit_bytes=16 << 20),
        cost_estimate=pl.CostEstimate(
            flops=2 * rows * width * cols, bytes_accessed=8 * rows * width + 2 * width * cols, transcendentals=0
        ),
        name="query",
    )(me, h, routes, near, far)


def spread_keyval(device, kv_refs, key_ref, value_ref):
    devices = len(kv_refs)
    _, block, _ = kv_refs[0].shape
    low_half = lane_index(block) < HD
    for index in range(devices):
        for high in range(2):
            rows = kv_refs[index][high].astype(F32)
            rolled = pltpu.roll(rows, HD, 1)
            span = block_of(device ^ index, high, devices, block)
            key_ref[span, :] = jnp.where(low_half, rows, rolled).astype(BF16)
            value_ref[span, :] = jnp.where(low_half, rolled, rows).astype(BF16)


def block_of(device, high, devices, block):
    place = 2 * devices - 1 - device if high else device
    return pl.ds(pl.multiple_of(place * block, block), block)


def attend_kernel(place_ref, q_ref, *refs):
    *kv_refs, o_ref, log_ref, key_ref, plain_ref, value_ref, acc_ref, peak_ref, bound_ref = refs
    step = pl.program_id(0)
    slots, tile, _ = q_ref.shape
    rows = slots * tile
    width = 512

    @pl.when(step == 0)
    def _():
        spread_keyval(place_ref[2, 0], kv_refs, key_ref, plain_ref)
        value_ref[:, :LANES] = plain_ref[...]
        value_ref[:, LANES:] = jnp.ones((value_ref.shape[0], LANES), BF16)
        keys = key_ref[...].astype(F32)
        bound_ref[0] = jnp.max(jnp.sum(keys * keys, -1, keepdims=True)) * 0.5
        bound_ref[1] = jnp.max(jnp.abs(plain_ref[...].astype(F32)))

    here = place_ref[0, step]
    lower = pl.multiple_of(place_ref[1, step], width)
    q = q_ref[...].reshape(rows, LANES)
    qf = q.astype(F32)
    longest = jnp.max(jnp.sum(qf * qf, -1, keepdims=True))
    plain = (longest * bound_ref[0] <= (SAFE_SCORE / SCALE) ** 2) & (bound_ref[1] <= SAFE_VALUE)
    full = (here - lower) // width
    last = pl.multiple_of(lower + full * width, width)
    token = lax.broadcasted_iota(jnp.int32, (tile, width), 0) + here
    allowed = (lax.broadcasted_iota(jnp.int32, (tile, width), 1) + last) <= token
    allowed = jnp.broadcast_to(allowed[None], (slots, tile, width)).reshape(rows, width)

    def finish(out, logs):
        o_ref[...] = out.reshape(slots, tile, LANES)
        logs = logs.reshape(slots, tile, LANES)
        lane = lane_index(tile)
        packed = jnp.zeros((tile, LANES), F32)
        for slot in range(slots):
            packed = jnp.where(lane == slot, logs[slot], packed)
        log_ref[...] = packed

    pairs = full // 2

    @pl.when(plain)
    def _():
        for count, edge_width in ((0, width // 2), (0, width), (1, width // 2), (1, width)):

            @pl.when((full % 2 == count) & ((here - last >= width // 2) == (edge_width == width)))
            def _(count=count, edge_width=edge_width):
                inner = count * width
                span = pl.ds(pl.multiple_of(lower + pairs * 2 * width, width), inner + edge_width)
                expo = jnp.exp2(dot_last(q, key_ref[span, :]) * (SCALE * LOG2E))
                edge = jnp.where(allowed[:, :edge_width], expo[:, inner:], 0.0).astype(BF16)
                expo = jnp.concatenate([expo[:, :inner].astype(BF16), edge], 1) if count else edge
                acc_ref[...] = dot(expo, value_ref[span, :])

        def body(index, carry):
            span = pl.ds(pl.multiple_of(lower + index * 2 * width, width), 2 * width)
            expo = jnp.exp2(dot_last(q, key_ref[span, :]) * (SCALE * LOG2E)).astype(BF16)
            acc_ref[...] += dot(expo, value_ref[span, :])
            return carry

        lax.fori_loop(0, pairs, body, 0)
        total = acc_ref[:, LANES:]
        finish(acc_ref[:, :LANES] / total, jnp.log2(total))

    @pl.when(jnp.logical_not(plain))
    def _():
        def scaled(span):
            return dot_last(q, key_ref[span, :]) * (SCALE * LOG2E)

        scores = jnp.where(allowed, scaled(pl.ds(last, width)), MASKED)
        peak = jnp.max(scores, -1, keepdims=True)
        peak_ref[...] = jnp.broadcast_to(peak, (rows, LANES))
        acc_ref[...] = dot(jnp.exp2(scores - peak).astype(BF16), value_ref[pl.ds(last, width), :])

        def body(index, carry):
            span = pl.ds(pl.multiple_of(lower + index * width, width), width)
            scores = scaled(span)
            before = peak_ref[:, :1]
            peak = jnp.maximum(before, jnp.max(scores, -1, keepdims=True))
            peak_ref[...] = jnp.broadcast_to(peak, (rows, LANES))
            expo = jnp.exp2(scores - peak).astype(BF16)
            acc_ref[...] = acc_ref[...] * jnp.exp2(before - peak) + dot(expo, value_ref[span, :])
            return carry

        lax.fori_loop(0, full, body, 0)
        total = acc_ref[:, LANES:]
        finish(acc_ref[:, :LANES] / total, peak_ref[...] + jnp.log2(total))


def attend_call(place, q, kv, tile=128):
    slots, rows, _ = q.shape
    count = len(kv) * kv[0].shape[0] * kv[0].shape[1]
    return pl.pallas_call(
        attend_kernel,
        grid_spec=pltpu.PrefetchScalarGridSpec(
            num_scalar_prefetch=1,
            grid=(rows // tile,),
            in_specs=[
                pl.BlockSpec((slots, tile, LANES), lambda i, s: (0, i, 0)),
                *[pl.BlockSpec(part.shape, lambda i, s: (0, 0, 0)) for part in kv],
            ],
            out_specs=[
                pl.BlockSpec((slots, tile, LANES), lambda i, s: (0, i, 0)),
                pl.BlockSpec((tile, LANES), lambda i, s: (i, 0)),
                pl.BlockSpec((count, LANES), lambda i, s: (0, 0)),
                pl.BlockSpec((count, LANES), lambda i, s: (0, 0)),
            ],
            scratch_shapes=[
                pltpu.VMEM((count, 2 * LANES), BF16),
                pltpu.VMEM((slots * tile, 2 * LANES), F32),
                pltpu.VMEM((slots * tile, LANES), F32),
                pltpu.SMEM((2,), F32),
            ],
        ),
        out_shape=[
            jax.ShapeDtypeStruct((slots, rows, LANES), F32),
            jax.ShapeDtypeStruct((rows, LANES), F32),
            jax.ShapeDtypeStruct((count, LANES), BF16),
            jax.ShapeDtypeStruct((count, LANES), BF16),
        ],
        compiler_params=pltpu.CompilerParams(vmem_limit_bytes=24 << 20),
        cost_estimate=pl.CostEstimate(
            flops=8 * slots * rows * count * LANES, bytes_accessed=8 * slots * rows * LANES, transcendentals=0
        ),
        name="attend",
    )(place, q, *kv)


def attend_back_kernel(first, final, tile_of, groups, before, *refs):
    refs = list(refs)
    take = lambda count: [refs.pop(0) for _ in range(count)]
    place_ref, q_ref, do_ref, log_ref, delta_ref, routes_ref, key_ref, value_ref = take(8)
    if not first:
        (sums_in,) = take(1)
    if final:
        (h_ref,) = take(1)
        before_refs = take(before)
    (all_ref,) = take(1)
    outs = take(4 if final else 1)
    dq_ref, dkey_ref, dvalue_ref, sems = take(4)
    step = pl.program_id(0)
    steps = pl.num_programs(0)
    slots, tile, _ = q_ref.shape
    rows = slots * tile
    width = 512

    def carry_copies():
        return [
            pltpu.make_async_copy(sums_in.at[0], dkey_ref.at[pl.ds(0, HD), :], sems.at[0]),
            pltpu.make_async_copy(sums_in.at[1], dvalue_ref.at[pl.ds(0, HD), :], sems.at[1]),
        ]

    @pl.when(step == 0)
    def _():
        if first:
            dkey_ref[:HD] = jnp.zeros_like(dkey_ref[:HD])
            dvalue_ref[:HD] = jnp.zeros_like(dvalue_ref[:HD])
        else:
            for copy in carry_copies():
                copy.start()
        dkey_ref[HD:] = jnp.zeros_like(dkey_ref[HD:])
        dvalue_ref[HD:] = jnp.zeros_like(dvalue_ref[HD:])

    here = place_ref[0, tile_of(step)]
    lower = place_ref[1, tile_of(step)]
    q = q_ref[...].reshape(rows, LANES)
    do = do_ref[...].reshape(rows, LANES)
    logs = log_ref[...]
    deltas = delta_ref[...]
    logs = jnp.concatenate([column(logs, slot, tile) for slot in range(slots)], 0)
    deltas = jnp.concatenate([column(deltas, slot, tile) for slot in range(slots)], 0)
    full = (here - lower) // width
    last = pl.multiple_of(lower + full * width, width)
    token = lax.broadcasted_iota(jnp.int32, (tile, width), 0) + here
    allowed = (lax.broadcasted_iota(jnp.int32, (tile, width), 1) + last) <= token
    allowed = jnp.broadcast_to(allowed[None], (slots, tile, width)).reshape(rows, width)

    if not first:

        @pl.when(step == 0)
        def _():
            for copy in carry_copies():
                copy.wait()

    def one(start, size, masked):
        wide = lambda values: jnp.concatenate([values] * (size // LANES), 1)
        span = pl.ds(start, size)
        keys = key_ref[span, :]
        scores = dot_last(q, keys)
        probs = jnp.exp2(scores * (SCALE * LOG2E) - wide(logs))
        if masked:
            probs = jnp.where(allowed[:, :size], probs, 0.0)
        dprobs = dot_last(do, value_ref[span, :])
        dscores = (probs * (dprobs - wide(deltas))).astype(BF16)
        dvalue_ref[:, span] += dot_first(do, probs.astype(BF16))
        dkey_ref[:, span] += dot_first(q, dscores)
        return dot(dscores, keys)

    for size in (width // 2, width):

        @pl.when((here - last >= width // 2) == (size == width))
        def _(size=size):
            dq_ref[...] = one(last, size, True)

    def body(index, carry):
        dq_ref[...] += one(pl.multiple_of(lower + index * width, width), width, False)
        return carry

    lax.fori_loop(0, full, body, 0)

    def sum_copies():
        return [
            pltpu.make_async_copy(dkey_ref.at[pl.ds(0, HD), :], outs[0].at[0], sems.at[0]),
            pltpu.make_async_copy(dvalue_ref.at[pl.ds(0, HD), :], outs[0].at[1], sems.at[1]),
        ]

    if not final:

        @pl.when(step == steps - 1)
        def _():
            dkey_ref[:HD] += dkey_ref[HD:]
            dvalue_ref[:HD] += dvalue_ref[HD:]
            for copy in sum_copies():
                copy.start()

    dq = (dq_ref[...] * SCALE).astype(BF16).reshape(slots, tile, LANES)
    mine = pl.ds(pl.multiple_of(step * tile, tile), tile)
    all_ref[mine, :] = place_pairs([dq[slot] for slot in range(slots)], choices(routes_ref[...], tile, BF16))

    @pl.when(step == steps - 1)
    def _():
        if not final:
            for copy in sum_copies():
                copy.wait()
            return
        kv_keep, kv_send, gq_keep, gq_send = outs
        _, _, block, _ = kv_keep.shape
        device = place_ref[2, 0]
        for index in range(4):
            target = kv_send if index % 2 else kv_keep
            for high in range(2):
                span = block_of(device ^ index, high, 4, block)
                dkeys = (dkey_ref[:HD, span] + dkey_ref[HD:, span]) * SCALE
                dvalues = dvalue_ref[:HD, span] + dvalue_ref[HD:, span]
                target[index // 2, high] = jnp.concatenate([dkeys, dvalues], 0).T.astype(BF16)
        gq = dot_first(h_ref[...], in_rows([*before_refs, all_ref]))
        if groups == 8:
            scatter_rows(gq, gq_keep, gq_send, device % 2)
        else:
            gq_keep[...] = gq.astype(BF16)
            gq_send[...] = jnp.zeros_like(gq_send)


def in_rows(parts):
    half = lambda part: part.shape[0] // 2
    return jnp.concatenate([part[: half(part)] for part in parts] + [part[half(part) :] for part in parts], 0)


def scatter_rows(grad, keep, send, core):
    for x in range(2):
        for y in range(2):
            for z in range(4):
                base = (((z * 2 + y) * 2 + x) * 2) * 16
                low = grad[base : base + 16].astype(BF16)
                high = grad[base + 16 : base + 32].astype(BF16)
                keep[y, z, x] = jnp.where(core == 0, low, high)
                send[y, z, x] = jnp.where(core == 0, high, low)


def attend_back_call(start, count, tiles, groups, where, q, do, logs, deltas, routes, keys, values, carried, h, before):
    slots, rows, _ = q.shape
    length = keys.shape[0]
    width = h.shape[1]
    tile = rows // (2 * tiles)
    first, final = start == 0, start + count == tiles

    def tile_of(step):
        return jnp.where(step < count, start + step, tiles + start + step - count)

    whole = lambda shape: pl.BlockSpec(shape, lambda i, s: (0,) * len(shape))
    anywhere = pl.BlockSpec(memory_space=pl.ANY)
    by_slot = pl.BlockSpec((slots, tile, LANES), lambda i, s: (0, tile_of(i), 0))
    by_row = lambda cols: pl.BlockSpec((tile, cols), lambda i, s: (tile_of(i), 0))
    in_specs = [
        by_slot, by_slot, by_row(LANES), by_row(LANES), by_row(TOPK), whole(keys.shape), whole(values.shape),
    ]
    in_specs += [anywhere] * len(carried)
    extra = [h, *before] if final else []
    in_specs += [whole(array.shape) for array in extra]
    out_specs = [whole((2 * count * tile, SPAN))]
    out_shape = [jax.ShapeDtypeStruct((2 * count * tile, SPAN), BF16)]
    if final:
        kv_shape = (2, 2, rows // 2, LANES)
        gq_shape = (2, 4, 2, 16, SPAN) if groups == 8 else (width, SPAN)
        off_shape = gq_shape if groups == 8 else (8, LANES)
        for shape in (kv_shape, kv_shape, gq_shape, off_shape):
            out_specs.append(whole(shape))
            out_shape.append(jax.ShapeDtypeStruct(shape, BF16))
    else:
        out_specs.append(anywhere)
        out_shape.append(jax.ShapeDtypeStruct((2, HD, length), F32))
    return pl.pallas_call(
        functools.partial(attend_back_kernel, first, final, tile_of, groups, len(before)),
        grid_spec=pltpu.PrefetchScalarGridSpec(
            num_scalar_prefetch=1,
            grid=(2 * count,),
            in_specs=in_specs,
            out_specs=out_specs,
            scratch_shapes=[
                pltpu.VMEM((slots * tile, LANES), F32),
                pltpu.VMEM((LANES, length), F32),
                pltpu.VMEM((LANES, length), F32),
                pltpu.SemaphoreType.DMA((2,)),
            ],
        ),
        out_shape=out_shape,
        compiler_params=pltpu.CompilerParams(vmem_limit_bytes=20 << 20),
        cost_estimate=pl.CostEstimate(
            flops=10 * slots * 2 * count * tile * length * LANES, bytes_accessed=16 * slots * tile * LANES, transcendentals=0
        ),
        name="attend_back",
    )(where, q, do, logs, deltas, routes, keys, values, *carried, *extra)


def query_back_kernel(dlog_ref, wq_ref, wr_ref, *refs):
    *all_refs, dh_ref = refs
    rows = in_rows(all_refs)
    dh_ref[...] = dot_last(rows, wq_ref[...]) + dot_last(dlog_ref[...], wr_ref[...])


def query_back_call(dlogits, wq, wk, parts):
    rows = dlogits.shape[0]
    width = wq.shape[0]
    cols = lambda size, index: pl.BlockSpec((width, size), lambda i: (0, index))
    whole = lambda shape: pl.BlockSpec(shape, lambda i: (0,) * len(shape))
    return pl.pallas_call(
        query_back_kernel,
        grid=(1,),
        in_specs=[
            whole(dlogits.shape), cols(SPAN, 0), cols(LANES, 1), *[whole(part.shape) for part in parts],
        ],
        out_specs=whole((rows, width)),
        out_shape=jax.ShapeDtypeStruct((rows, width), F32),
        compiler_params=pltpu.CompilerParams(vmem_limit_bytes=24 << 20),
        cost_estimate=pl.CostEstimate(
            flops=2 * rows * width * (SPAN + LANES), bytes_accessed=4 * rows * (SPAN + width), transcendentals=0
        ),
        name="query_back",
    )(dlogits, wq, wk, *parts)


def middle_kernel(groups, *refs):
    refs = list(refs)
    take = lambda count: [refs.pop(0) for _ in range(count)]
    core_ref, x_hbm, dy_hbm, o_hbm, gate_ref, routes_ref, tail_ref = take(7)
    weights_in = take(8 if groups == 8 else 3)
    out_hbm, dmid_hbm, do_hbm, delta_ref, dlog_ref, gain_ref = take(6)
    outs_hbm = take(4 if groups == 8 else 3)
    x_ref, dy_ref, o_ref, comb_ref, mid_ref, normal_ref, acc_ref, dh_ref, dcomb_ref, out_ref, do_ref = take(11)
    wo_in, w1_in, w2_in = take(3)
    in_sems, out_sems = take(2)
    outs = refs
    rows, width = x_ref.shape
    part = 256
    cols = 512
    count = [0]

    def copy(source, target):
        count[0] += 1
        return pltpu.make_async_copy(source, target, in_sems.at[count[0] - 1])

    slot_copies = [copy(o_hbm.at[slot], o_ref.at[slot]) for slot in range(TOPK)]
    x_copy, dy_copy = copy(x_hbm, x_ref), copy(dy_hbm, dy_ref)
    if groups == 8:
        flat = core_ref[0]
        my_x, my_y, core = flat // 2 % 2, flat // 4 % 2, flat % 2
        wo_copies, w1_copies, w2_copies = [], [], []
        for index in range(8):
            other_core, other = index // 4, index % 4
            for y_turn in range(2):
                y = my_y ^ y_turn
                part_a = weights_in[4 * other_core + (other // 2)]
                x = my_x ^ (other // 2)
                mp = 2 * x + (core ^ other_core)
                across = pl.ds(pl.multiple_of(mp * cols, cols), cols)
                if other % 2 == 0:
                    wo_copies.append(copy(part_a.at[y_turn, :, 4:6], wo_in.at[:, y, mp, 0:2]))
                    w1_copies.append(copy(part_a.at[y_turn, :, 0:4], w1_in.at[:, y, :, :, across]))
                else:
                    part_b = weights_in[4 * other_core + 2 + y_turn]
                    x_turn = other // 2
                    wo_copies.append(copy(part_b.at[x_turn, :, 4:5], wo_in.at[:, y, mp, 2:3]))
                    w2_copies.append(copy(part_b.at[x_turn, :, 0:4], w2_in.at[:, y, :, :, across]))
    else:
        wo_copies, w1_copies, w2_copies = [
            [copy(source, target)] for source, target in zip(weights_in, (wo_in, w1_in, w2_in))
        ]
    for one in (*slot_copies, *wo_copies, x_copy, *w1_copies, dy_copy, *w2_copies):
        one.start()
    view = lambda ref: ref[...].reshape(width, -1)
    third = lambda ref, index: ref[:, :, :, index].reshape(width, cols)

    gain = gains_of(tail_ref[...])[E + 1 : E + 2]
    for one in slot_copies:
        one.wait()

    def combine(index, carry):
        mine = pl.ds(pl.multiple_of(index * part, part), part)
        gates = gate_ref[mine, :]
        weighted = [(column(gates, slot, part) * o_ref[slot, mine, :]).astype(BF16) for slot in range(TOPK)]
        comb_ref[mine, :] = place_pairs(weighted, choices(routes_ref[mine, :], part, BF16))
        return carry

    lax.fori_loop(0, rows // part, combine, 0)
    for one in (*wo_copies, x_copy):
        one.wait()
    mid = x_ref[...].astype(F32)
    if groups == 8:
        for index in range(3):
            mid = mid + dot_last(comb_ref[:, index * cols : (index + 1) * cols], third(wo_in, index))
    else:
        mid = mid + dot_last(comb_ref[...], wo_in[...])
    mid_ref[...] = mid
    normal, factor = standardize(mid)
    normal_ref[...] = normal
    h2 = (normal * gain).astype(BF16)
    for one in (*w1_copies, dy_copy, *w2_copies):
        one.wait()
    dy = dy_ref[...]
    w1, w2 = view(w1_in), view(w2_in)

    for index in range(w1.shape[1] // cols):
        span = slice(index * cols, (index + 1) * cols)
        up, down = w1[:, span], w2[:, span]
        pre = dot(h2, up)
        dact = dot(dy, down)
        sigma = jax.nn.sigmoid(pre)
        act = (pre * sigma).astype(BF16)
        dpre = (dact * (sigma * (1.0 + pre * (1.0 - sigma)))).astype(BF16)
        branch = dot_last(act, down)
        dh2 = dot_last(dpre, up)
        if index == 0:
            acc_ref[...] = branch
            dh_ref[...] = dh2
        else:
            acc_ref[...] += branch
            dh_ref[...] += dh2
        g1 = dot_first(h2, dpre).astype(BF16)
        g2 = dot_first(dy, act).astype(BF16)
        if groups != 8:
            outs[0][:, span] = g1
            outs[1][:, span] = g2
            continue
        for mine, (a, b) in ((True, (outs[0], outs[2])), (False, (outs[1], outs[3]))):

            @pl.when((core_ref[0] % 2 == index % 2) == mine)
            def _(a=a, b=b, g1=g1, g2=g2, x=index // 2):
                for owner in range(8):
                    piece = slice(owner * 64, owner * 64 + 64)
                    a[x, owner % 2, owner // 2, :64] = g1[piece]
                    b[owner % 2, x, owner // 2, :64] = g2[piece]

    out_ref[...] = (mid_ref[...] + acc_ref[...]).astype(BF16)
    out_copy = pltpu.make_async_copy(out_ref, out_hbm, out_sems.at[0])
    out_copy.start()
    dh2 = dh_ref[...]
    normal = normal_ref[...]
    gain_ref[...] = jnp.sum(dh2 * normal, 0, keepdims=True)
    dmid = dy.astype(F32) + norm_back(dh2 * gain, normal, factor)
    mid_ref[...] = dmid
    dmid_copy = pltpu.make_async_copy(mid_ref, dmid_hbm, out_sems.at[1])
    dmid_copy.start()
    dmid_b = dmid.astype(BF16)
    if groups == 8:
        for index in range(3):
            span = slice(index * cols, (index + 1) * cols)
            dcomb_ref[:, span] = dot(dmid_b, third(wo_in, index)).astype(BF16)
    else:
        dcomb_ref[...] = dot(dmid_b, wo_in[...]).astype(BF16)
    go = dot_first(dmid_b, comb_ref[...]).astype(BF16)
    if groups == 8:
        for core in range(2):

            @pl.when(core_ref[0] % 2 == core)
            def _(pairs=((outs[0], outs[2]), (outs[1], outs[3])), core=core):
                for owner in range(32):
                    z, y, x, c = owner // 8, owner // 4 % 2, owner // 2 % 2, owner % 2
                    a, b = pairs[c ^ core]
                    mine = slice(owner * 16, owner * 16 + 16)
                    a[x, y, z, 64:80] = go[mine, :512]
                    a[x, y, z, 80:] = go[mine, 512:1024]
                    b[y, x, z, 64:] = go[mine, 1024:]
    else:
        outs[2][...] = go

    grad_copies = [
        pltpu.make_async_copy(source, target, out_sems.at[3 + index])
        for index, (source, target) in enumerate(zip(outs, outs_hbm))
    ]
    for one in grad_copies:
        one.start()

    def spread(index, carry):
        mine = pl.ds(pl.multiple_of(index * part, part), part)
        gates = gate_ref[mine, :]
        routes = routes_ref[mine, :]
        lane = lane_index(part)
        dcomb = dcomb_ref[mine, :]
        gate_grads = jnp.zeros((part, LANES), F32)
        for slot, choice in enumerate(choices(routes, part, BF16)):
            picked = pick_pairs(dcomb, choice).astype(F32)
            do_ref[slot, mine, :] = (column(gates, slot, part) * picked).astype(BF16)
            total = jnp.sum(o_ref[slot, mine, :] * picked, -1, keepdims=True)
            gate_grads = jnp.where(lane == slot, total, gate_grads)
        weighted = gates * gate_grads
        delta_ref[mine, :] = weighted
        dsel = weighted - gates * jnp.sum(weighted, -1, keepdims=True)
        dlogits = jnp.zeros((part, LANES), F32)
        for slot in range(TOPK):
            dlogits = jnp.where(lane == column(routes, slot, part), column(dsel, slot, part), dlogits)
        dlog_ref[mine, :] = dlogits.astype(BF16)
        return carry

    lax.fori_loop(0, rows // part, spread, 0)
    do_copy = pltpu.make_async_copy(do_ref, do_hbm, out_sems.at[2])
    do_copy.start()
    for one in (out_copy, dmid_copy, do_copy, *grad_copies):
        one.wait()


def middle_call(groups, core, x, dy, o, gates, routes, front, weights):
    rows, width = x.shape
    hidden = 2048
    whole = lambda shape: pl.BlockSpec(shape, lambda i, s: (0,) * len(shape))
    anywhere = pl.BlockSpec(memory_space=pl.ANY)
    if groups == 8:
        grads = [(2, 2, 4, 96, 512), (2, 2, 4, 96, 512), (2, 2, 4, 80, 512), (2, 2, 4, 80, 512)]
        held = [(4, 2, 4, 3, 16, 512), (4, 2, 4, 16, hidden), (4, 2, 4, 16, hidden)]
    else:
        grads = [(width, hidden), (width, hidden), (width, SPAN)]
        held = [(width, SPAN), (width, hidden), (width, hidden)]
    return pl.pallas_call(
        functools.partial(middle_kernel, groups),
        grid_spec=pltpu.PrefetchScalarGridSpec(
            num_scalar_prefetch=1,
            grid=(1,),
            in_specs=[
                anywhere, anywhere, anywhere, whole(gates.shape), whole(routes.shape),
                pl.BlockSpec((width, LANES), lambda i, s: (0, 1)), *[anywhere] * len(weights),
            ],
            out_specs=[
                anywhere, anywhere, anywhere, whole((rows, LANES)), whole((rows, LANES)), whole((1, width)),
                *[anywhere] * len(grads),
            ],
            scratch_shapes=[
                pltpu.VMEM((rows, width), BF16),
                pltpu.VMEM((rows, width), BF16),
                pltpu.VMEM((TOPK, rows, LANES), F32),
                pltpu.VMEM((rows, SPAN), BF16),
                pltpu.VMEM((rows, width), F32),
                pltpu.VMEM((rows, width), F32),
                pltpu.VMEM((rows, width), F32),
                pltpu.VMEM((rows, width), F32),
                pltpu.VMEM((rows, SPAN), BF16),
                pltpu.VMEM((rows, width), BF16),
                pltpu.VMEM((TOPK, rows, LANES), BF16),
                *[pltpu.VMEM(shape, BF16) for shape in held],
                pltpu.SemaphoreType.DMA((42,)),
                pltpu.SemaphoreType.DMA((7,)),
                *[pltpu.VMEM(shape, BF16) for shape in grads],
            ],
        ),
        out_shape=[
            jax.ShapeDtypeStruct((rows, width), BF16),
            jax.ShapeDtypeStruct((rows, width), F32),
            jax.ShapeDtypeStruct((TOPK, rows, LANES), BF16),
            jax.ShapeDtypeStruct((rows, LANES), F32),
            jax.ShapeDtypeStruct((rows, LANES), BF16),
            jax.ShapeDtypeStruct((1, width), F32),
            *[jax.ShapeDtypeStruct(shape, BF16) for shape in grads],
        ],
        compiler_params=pltpu.CompilerParams(vmem_limit_bytes=48 << 20),
        cost_estimate=pl.CostEstimate(
            flops=2 * rows * width * (6 * hidden + 3 * SPAN), bytes_accessed=16 * rows * width, transcendentals=0
        ),
        name="middle",
    )(core, x, dy, o, gates, routes, front, *weights)


def post_kernel(x_ref, h_ref, dmid_ref, dh_ref, keep_ref, recv_ref, dlog_ref, gain2_ref, w_ref, grad_ref, gk_ref, sum_ref):
    step = pl.program_id(0)
    gain = gains_of(w_ref[:, LANES:])[E : E + 1]
    normal, factor = standardize(x_ref[...].astype(F32))
    dkv = (keep_ref[...].astype(F32) + recv_ref[...].astype(F32)).astype(BF16)
    dh = dh_ref[...] + dot_last(dkv, w_ref[:, :LANES])
    grad_ref[...] = (dmid_ref[...] + norm_back(dh * gain, normal, factor)).astype(grad_ref.dtype)
    gain1 = jnp.sum(dh * normal, 0, keepdims=True)
    width = gain1.shape[1]
    row = lax.broadcasted_iota(jnp.int32, (LANES, width), 0)
    gain2 = jnp.where(step == 0, gain2_ref[...], 0.0)
    gains = jnp.where(row == E, gain1, jnp.where(row == E + 1, gain2, 0.0))
    h_turned = turned(h_ref[...])
    keyval = dot(h_turned, dkv)
    router = dot(h_turned, dlog_ref[...]) + gains.T

    @pl.when(step == 0)
    def _():
        sum_ref[:, :LANES] = keyval
        sum_ref[:, LANES:] = router

    @pl.when(step > 0)
    def _():
        sum_ref[:, :LANES] += keyval
        sum_ref[:, LANES:] += router

    @pl.when(step == pl.num_programs(0) - 1)
    def _():
        gk_ref[...] = sum_ref[...].astype(BF16)


def post_call(x, h, dmid, dh, keep, recv, dlogits, gain2, weights, tile=256):
    rows, width = x.shape
    by_row = lambda cols: pl.BlockSpec((tile, cols), lambda i: (i, 0))
    return pl.pallas_call(
        post_kernel,
        grid=(rows // tile,),
        in_specs=[
            by_row(width), by_row(width), by_row(width), by_row(width), by_row(LANES), by_row(LANES), by_row(LANES),
            pl.BlockSpec((1, width), lambda i: (0, 0)),
            pl.BlockSpec((width, 2 * LANES), lambda i: (0, 0)),
        ],
        out_specs=[by_row(width), pl.BlockSpec((width, 2 * LANES), lambda i: (0, 0))],
        out_shape=[
            jax.ShapeDtypeStruct((rows, width), BF16),
            jax.ShapeDtypeStruct((width, 2 * LANES), BF16),
        ],
        scratch_shapes=[pltpu.VMEM((width, 2 * LANES), F32)],
        compiler_params=pltpu.CompilerParams(vmem_limit_bytes=16 << 20),
        cost_estimate=pl.CostEstimate(
            flops=6 * rows * width * LANES, bytes_accessed=16 * rows * width, transcendentals=0
        ),
        name="finish",
    )(x, h, dmid, dh, keep, recv, dlogits, gain2, weights)


RING = ((0, 1), (1, 2), (2, 3), (3, 0))
SWAP = ((1, 3), (3, 1))


def halves(rows, place):
    half = rows.shape[0] // 2
    outer = (place == 0) | (place == 3)
    first = lax.dynamic_slice_in_dim(rows, jnp.where(outer, half, 0), half, 0)
    second = lax.dynamic_slice_in_dim(rows, jnp.where(place == 1, half, 0), half, 0)
    return first, second


def deal(rows, sent, place, ready=None):
    half = rows.shape[0] // 2
    ring = lax.ppermute(sent[0], "mp", RING)
    swap = lax.ppermute(sent[1], "mp", SWAP)
    if ready is not None:
        ring, swap = after((ring, swap), ready)
    low = jnp.where(place == 0, rows[:half], jnp.where(place == 3, swap, ring))
    high = jnp.where(place == 2, rows[half:], jnp.where(place == 1, swap, ring))
    return jnp.concatenate([low, high], 0)


def send_back(rows, place):
    first, second = halves(rows, place)
    ring = lax.ppermute(first, "mp", tuple((b, a) for a, b in RING))
    return ring, lax.ppermute(second, "mp", SWAP)


def put_back(rows, returned, place):
    half = rows.shape[0] // 2
    ring, swap = returned
    top = jnp.where(place == 0, rows[:half], jnp.where(place == 3, swap, ring))
    bottom = jnp.where(place == 2, rows[half:], jnp.where(place == 1, swap, ring))
    return jnp.concatenate([top, bottom], 0)


OTHER_CORE = ((0, 1), (1, 0), (2, 3), (3, 2))
OTHER_X = ((0, 2), (2, 0), (1, 3), (3, 1))


def swap_core(values):
    return lax.ppermute(values, "mp", OTHER_CORE)


def swap_x(values):
    return lax.ppermute(values, "mp", OTHER_X)


def swap_y(values):
    return lax.ppermute(values, "dp", tuple((i, i ^ 1) for i in range(8)))


def swap_z(values, turn):
    return lax.ppermute(values, "dp", tuple((i, i ^ (2 * turn)) for i in range(8)))


def at(values, index):
    return lax.dynamic_index_in_dim(values, index, 0, keepdims=False)


def added(left, right):
    return (left.astype(F32) + right.astype(F32)).astype(BF16)


def gather_z(shard, my_z):
    turns = [shard] + [swap_z(shard, turn) for turn in (1, 2, 3)]
    rows = []
    for z in range(4):
        row = turns[3]
        for turn in (2, 1, 0):
            row = jnp.where(my_z == z ^ turn, turns[turn], row)
        rows.append(row)
    return jnp.stack(rows)


def after(values, others):
    return lax.optimization_barrier((values, others))[0]


def tied(first, second):
    return lax.optimization_barrier((first, second))


def adam_step(param, first, second, grad, rate, decay):
    first_new = BETA_FIRST * first + (1.0 - BETA_FIRST) * grad
    second_new = BETA_SECOND * second + (1.0 - BETA_SECOND) * grad * grad
    first_hat = first_new / (1.0 - BETA_FIRST**ADAM_STEP)
    second_hat = second_new / (1.0 - BETA_SECOND**ADAM_STEP)
    param_new = param - rate * (first_hat / (jnp.sqrt(second_hat) + ADAM_EPS) + decay * param)
    return (second_new, param_new)


def update_kernel(
    rates_ref, squares_ref, gq_ref, go_ref, gk_ref, ffn_ref,
    ap_ref, am_ref, av_ref, fp_ref, fm_ref, fv_ref,
    ag_ref, avn_ref, apn_ref, fg_ref, fvn_ref, fpn_ref, norm_ref, gain_ref,
):
    norm = jnp.sqrt(jnp.sum(jnp.sum(squares_ref[...], 0), keepdims=True))
    norm_ref[...] = norm
    factor = jnp.minimum(1.0, CLIP_NORM / norm)
    tail = AC - 2 * SPAN
    for source, span, rate in (
        (gq_ref, slice(0, SPAN), rates_ref[0]),
        (go_ref, slice(SPAN, 2 * SPAN), rates_ref[1]),
        (gk_ref, slice(2 * SPAN, AC), None),
    ):
        decay = WEIGHT_DECAY
        grad = source[...] * factor
        if rate is None:
            grad = grad[:, :tail]
            place = lax.broadcasted_iota(jnp.int32, (1, tail), 1)
            rate = jnp.where(
                place < 2 * HD, rates_ref[2], jnp.where(place < 2 * HD + E, rates_ref[3], rates_ref[4])
            )
            decay = jnp.where(place < 2 * HD + E, WEIGHT_DECAY, 0.0)
            gain_ref[...] = grad[:, tail - 2 :]
        ag_ref[:, span] = grad
        avn_ref[:, span], apn_ref[:, span] = adam_step(
            ap_ref[:, span], am_ref[:, span], av_ref[:, span], grad, rate, decay
        )
    for index in range(2):
        grad = ffn_ref[index] * factor
        fg_ref[index] = grad
        fvn_ref[index], fpn_ref[index] = adam_step(
            fp_ref[index], fm_ref[index], fv_ref[index], grad, rates_ref[5 + index], WEIGHT_DECAY
        )


def squares_kernel(gq_ref, go_ref, ffn_ref, gk_ref, sums_ref, gk_out_ref):
    gk = jnp.sum(gk_ref[...].astype(F32), 0)
    gk_out_ref[...] = gk
    total = jnp.zeros((8, LANES), F32)
    for part in (gq_ref[...], go_ref[...], gk, ffn_ref[...].reshape(-1, ffn_ref.shape[-1])):
        square = part * part
        for row in range(0, square.shape[0], 8):
            for col in range(0, square.shape[1], LANES):
                total = total + square[row : row + 8, col : col + LANES]
    sums_ref[...] = jnp.broadcast_to(total[None], sums_ref.shape)


def squares_call(gq, go, ffn, gk):
    return pl.pallas_call(
        squares_kernel,
        out_shape=[
            jax.ShapeDtypeStruct((gk.shape[0], 8, LANES), F32),
            jax.ShapeDtypeStruct(gk.shape[1:], F32),
        ],
        compiler_params=pltpu.CompilerParams(vmem_limit_bytes=8 << 20),
        name="squares",
    )(gq, go, ffn, gk)


def update_call(rates, squares, gq, go, gk, ffn, attn, ffn_state):
    rows = gq.shape[0]
    attn_shape = jax.ShapeDtypeStruct(attn[0].shape, F32)
    ffn_shape = jax.ShapeDtypeStruct(ffn.shape, F32)
    whole = pl.BlockSpec(memory_space=pltpu.VMEM)
    return pl.pallas_call(
        update_kernel,
        in_specs=[pl.BlockSpec(memory_space=pltpu.SMEM)] + [whole] * 11,
        out_specs=[whole] * 8,
        out_shape=[
            attn_shape, attn_shape, attn_shape, ffn_shape, ffn_shape, ffn_shape,
            jax.ShapeDtypeStruct((1, 1), F32), jax.ShapeDtypeStruct((rows, 2), F32),
        ],
        compiler_params=pltpu.CompilerParams(vmem_limit_bytes=24 << 20),
        name="update",
    )(rates, squares, gq, go, gk, ffn, *attn, *ffn_state)


ALL = ("dp", "mp")


def shards(
    tokens, cotangent, routes, starts, attn_param, attn_first, attn_second, ffn_param, ffn_first, ffn_second, rates
):
    local_rows, width = tokens.shape
    place = lax.axis_index("mp")
    devices = lax.axis_size("mp")
    groups = lax.axis_size("dp")
    block = local_rows // 2
    manual = groups == 8
    _, depth, cols = ffn_param.shape
    my_x, my_y, my_z = place // 2, lax.axis_index("dp") % 2, lax.axis_index("dp") // 2
    flat = (lax.axis_index("dp") * devices + place).astype(jnp.int32)

    marks = jnp.concatenate([routes, starts[:, None] // block], 1).astype(BF16)
    marks = jnp.pad(marks, ((0, 0), (0, 16 - TOPK - 1))).T
    dealt = [tokens[:block], marks[:, :block], tokens[block:], marks[:, block:]]
    dealt = jnp.concatenate([part.reshape(-1, width) for part in dealt], 0)
    extra = dealt.shape[0] // 2 - block
    sent = halves(dealt, place)
    dealt = deal(dealt, sent, place)
    x = jnp.concatenate([dealt[:block], dealt[block + extra : 2 * block + extra]], 0)
    marks = [dealt[block : block + extra], dealt[2 * block + extra :]]
    marks = jnp.concatenate([part.reshape(16, block) for part in marks], 1).T[:, : TOPK + 1].astype(jnp.int32)

    attn_b = attn_param.astype(BF16)
    ffn_b = ffn_param.astype(BF16)
    pad = jnp.zeros((attn_b.shape[0], 2 * LANES - (AC - 2 * SPAN)), BF16)
    wk = jnp.concatenate([attn_b[:, 2 * SPAN :], pad], 1)
    wq = attn_b[:, :SPAN]
    wo = attn_b[:, SPAN : 2 * SPAN]
    if manual:
        wk, wq = after((wk, wq), sent)
        wk = lax.all_to_all(jnp.broadcast_to(wk, (groups * devices, *wk.shape)), ALL, 0, 0, tiled=True)
        wk = wk.reshape(-1, 2 * LANES)
        along = jnp.stack([wq] + [swap_z(wq, turn) for turn in (1, 2, 3)])
        along = jnp.stack([along, swap_y(along)])
        (along, x, marks), (ffn_b, wo) = tied((along, x, marks), (ffn_b, wo))
        near = jnp.stack([along, swap_x(along)]).reshape(16, *wq.shape)
        far = swap_core(near)
        chunk = [ffn_b[0].reshape(-1, 16, cols), wo[None, :, :cols], wo[None, :, cols : 2 * cols]]
        chunk += [ffn_b[1].reshape(-1, 16, cols), wo[None, :, 2 * cols :]]
        chunk = gather_z(jnp.concatenate(chunk, 0), my_z)
    else:
        wk = lax.all_gather(wk, ALL, axis=0, tiled=True)
        wq_all = lax.all_gather(wq, ALL, axis=0, tiled=True).reshape(4, 2, 2, 2, 16, -1)
        wq_all = wq_all.transpose(3, 2, 1, 0, 4, 5).reshape(2, 16, 16, -1)
        near, far = wq_all[0], wq_all[1]
        wo_full = lax.all_gather(wo, ALL, axis=0, tiled=True)
        ffn_all = lax.all_gather(ffn_b, ALL, axis=0, tiled=False)
        ffn_all = ffn_all.reshape(groups, devices, 2, depth, cols).transpose(2, 0, 3, 1, 4)
        ffn_all = ffn_all.reshape(2, groups * depth, devices * cols)
        weights = [wo_full, ffn_all[0], ffn_all[1]]

    routes_x = marks[:, :TOPK]
    tile = 128
    tiles = local_rows // tile
    pieces = tiles // 2
    index = jnp.arange(tiles, dtype=jnp.int32)
    low = index < pieces
    here = jnp.where(low, place * block + index * tile, (2 * devices - 1 - place) * block + (index - pieces) * tile)
    lower = jnp.where(low, marks[0, TOPK], marks[block, TOPK]) * block
    where = jnp.stack([here, lower, jnp.full((tiles,), place)]).astype(jnp.int32)

    h, kv, gates = embed_call(x, routes_x, wk)
    kv = kv.reshape(2, block, LANES)
    kv_x = swap_x(kv)
    me = flat.reshape(1) if manual else jnp.zeros((1,), jnp.int32)
    if manual:
        chunk = after(chunk, kv)
        a_own = chunk[:, :6]
        b_own = chunk[:, 6:]
        a_own = jnp.stack([a_own, swap_y(a_own)])
        b_own = jnp.stack([b_own, swap_x(b_own)])
        a_far, b_far = swap_x(a_own), swap_y(b_own)
        weights = [a_own, a_far, b_own, b_far]
        near, far = after((near, far), (a_own, b_own))
    q, wq_full = query_call(me, h, routes_x, near, far)
    o, logs, keys, values = attend_call(where, q, [kv, swap_core(kv), kv_x, swap_core(kv_x)], tile)
    if manual:
        own = [swap_core(a_own), swap_core(b_own)]
        a_far, b_far = after((a_far, b_far), logs)
        weights += [own[0], swap_core(a_far), own[1], swap_core(b_far)]
        cotangent = after(cotangent, (q, own))
    else:
        cotangent = after(cotangent, q)
    dy = deal(cotangent, halves(cotangent, place), place, logs)
    out, dmid, do, deltas, dlogits, gain2, *grads = middle_call(
        groups, flat.reshape(1), x, dy, o, gates, routes_x, wk, weights
    )
    returned = send_back(out, place)

    def back(start, count, carried, before):
        return attend_back_call(
            start, count, pieces, groups, where, q, do, logs, deltas, routes_x, keys, values, carried, h, before
        )

    def split(parts, turn_a, turn_b, swap_a, swap_b):
        a_keep, a_in, b_keep, b_in = parts
        a_out = added(at(a_keep, 1 - turn_a), at(a_in, 1 - turn_a))
        b_out = added(at(b_keep, 1 - turn_b), at(b_in, 1 - turn_b))
        a_keep = added(at(a_keep, turn_a), at(a_in, turn_a))
        b_keep = added(at(b_keep, turn_b), at(b_in, turn_b))
        return (a_keep, swap_a(a_out), b_keep, swap_b(b_out))

    if manual:
        a_keep, a_send, b_keep, b_send = grads
        parts = split((a_keep, swap_core(a_send), b_keep, swap_core(b_send)), my_x, my_y, swap_x, swap_y)
    part_0, *carried = back(0, 2, (), ())
    if manual:
        carried, parts = tied(carried, parts)
        parts = split(parts, my_y, my_x, swap_y, swap_x)
    part_1, *carried = back(2, 1, carried, ())
    if manual:
        carried, parts = tied(carried, parts)
        both = jnp.concatenate([added(*parts[:2]), added(*parts[2:])], 1)
        moving = [swap_z(at(both, my_z ^ turn), turn) for turn in (1, 2, 3)]
        chunk_keep = at(both, my_z)
    part_2, kv_keep, kv_send, gq_keep, gq_send = back(3, 1, carried, (part_0, part_1))
    all_parts = [part_0, part_1, part_2]
    kv_in = swap_core(kv_send)
    kv_out = added(kv_keep[1], kv_in[1])
    kv_keep = added(kv_keep[0], kv_in[0]).reshape(local_rows, LANES)
    kv_recv = swap_x(kv_out).reshape(local_rows, LANES)
    dh = query_back_call(dlogits, wq_full, wk, after(all_parts, (kv_out, kv_keep)))
    if manual:
        gq_in = swap_core(gq_send)
        gq_send = added(at(gq_keep, 1 - my_y), at(gq_in, 1 - my_y))
        gq_keep = added(at(gq_keep, my_y), at(gq_in, my_y))
        gq_y = added(gq_keep, swap_y(gq_send))
        gq, returned = tied(gq_y, returned)
        gq_out = [at(gq, my_z ^ turn) for turn in (1, 2, 3)]
        dh, gq_out = tied(dh, gq_out)
        gq_in = [swap_z(part, turn) for part, turn in zip(gq_out, (1, 2, 3))]
        gq = at(gq, my_z)
    grad, gk = post_call(x, h, dmid, dh, kv_keep, kv_recv, dlogits, gain2, wk)
    if manual:
        gk = lax.all_to_all(gk.reshape(groups * devices, -1, 2 * LANES), ALL, 0, 0, tiled=True)
        gq = sum((part.astype(F32) for part in gq_in), gq.astype(F32)).astype(BF16)
        grad, gq = tied(grad, gq)
        gq_raw = at(gq, my_x).astype(F32) + swap_x(at(gq, 1 - my_x)).astype(F32)
    input_grad = put_back(grad, send_back(grad, place), place).astype(F32)
    layer_out = put_back(out, returned, place)

    if manual:
        chunk_raw = sum((part.astype(F32) for part in moving), chunk_keep.astype(F32))
        rows = depth
        ffn_raw = jnp.stack([chunk_raw[:rows], chunk_raw[rows + 32 : 2 * rows + 32]])
        go_raw = jnp.concatenate(
            [chunk_raw[rows : rows + 16], chunk_raw[rows + 16 : rows + 32], chunk_raw[2 * rows + 32 :]], 1
        )
    else:
        g1, g2, go = grads
        ffn_local = jnp.stack([g1, g2]).reshape(2, groups, depth, devices, cols).transpose(1, 3, 0, 2, 4)
        ffn_local = ffn_local.reshape(groups * devices * 2 * depth, cols)
        ffn_raw = lax.psum_scatter(ffn_local, ALL, scatter_dimension=0, tiled=True).astype(F32)
        ffn_raw = ffn_raw.reshape(2, depth, cols)
        go_raw = lax.psum_scatter(go, ALL, scatter_dimension=0, tiled=True).astype(F32)
        gq_raw = lax.psum_scatter(gq_keep, ALL, scatter_dimension=0, tiled=True).astype(F32)
        gk_raw = lax.psum_scatter(gk, ALL, scatter_dimension=0, tiled=True).astype(F32)
    if manual:
        squares, gk_raw = squares_call(gq_raw, go_raw, ffn_raw, gk)
        squares = lax.all_to_all(squares, ALL, 0, 0, tiled=True)
    else:
        squares = sum(jnp.sum(part * part) for part in (gq_raw, go_raw, gk_raw, ffn_raw))
        squares = lax.psum(squares, ALL) / (8 * LANES)
        squares = jnp.broadcast_to(squares, (1, 8, LANES))
    attn_grad, attn_second_new, attn_new, ffn_grad, ffn_second_new, ffn_new, grad_norm, gain_grad = update_call(
        rates, squares, gq_raw, go_raw, gk_raw, ffn_raw,
        (attn_param, attn_first, attn_second), (ffn_param, ffn_first, ffn_second),
    )
    return (
        layer_out,
        input_grad,
        attn_grad,
        attn_second_new,
        attn_new,
        ffn_grad,
        ffn_second_new,
        ffn_new,
        grad_norm.reshape(()),
        gain_grad,
    )


def solution(mesh):
    by_row = P(ALL, None)
    by_ffn = P(None, "dp", "mp")
    return jax.shard_map(
        shards,
        mesh=mesh,
        in_specs=(by_row, by_row, by_row, P(ALL), by_row, by_row, by_row, by_ffn, by_ffn, by_ffn, P()),
        out_specs=(by_row, by_row, by_row, by_row, by_row, by_ffn, by_ffn, by_ffn, P(), by_row),
        check_vma=False,
    )
```

```python
import functools
import math

import jax
import jax.numpy as jnp
from jax import lax
from jax.experimental import pallas as pl
from jax.experimental.pallas import tpu as pltpu
from jax.sharding import PartitionSpec as P

HD = 64
E = 24
TOPK = 8
ADAM_STEP = 7
AC = 3226
SPAN = E * HD
PAIRS = E // 2
LANES = 128

NORM_EPS = 1e-05
MASKED = -1e30
CLIP_NORM = 0.1
BETA_FIRST = 0.9
BETA_SECOND = 0.95
ADAM_EPS = 1e-08
WEIGHT_DECAY = 0.1

SCALE = HD ** (-0.5)
LOG2E = math.log2(math.e)
SAFE_SCORE = 40.0
SAFE_VALUE = 1e15
VMEM = 58 << 20

F32 = jnp.float32
BF16 = jnp.bfloat16


def dot(left, right):
    return jnp.dot(left, right, preferred_element_type=F32)


def dot_last(left, right):
    return lax.dot_general(left, right, (((1,), (1,)), ((), ())), preferred_element_type=F32)


def dot_first(left, right):
    return lax.dot_general(left, right, (((0,), (0,)), ((), ())), preferred_element_type=F32)


def turned(values):
    return values.astype(F32).T.astype(values.dtype)


def standardize(values):
    centred = values - jnp.mean(values, -1, keepdims=True)
    factor = lax.rsqrt(jnp.mean(centred * centred, -1, keepdims=True) + NORM_EPS)
    return (centred * factor, factor)


def norm_back(grad_normal, normal, factor):
    return factor * (
        grad_normal
        - jnp.mean(grad_normal, -1, keepdims=True)
        - normal * jnp.mean(grad_normal * normal, -1, keepdims=True)
    )


def lane_index(rows):
    return lax.broadcasted_iota(jnp.int32, (rows, LANES), 1)


def column(values, index, rows):
    return jnp.broadcast_to(values[:, index : index + 1], (rows, LANES))


def pick_pairs(table, chosen):
    picked = jnp.zeros(chosen.shape, table.dtype)
    for pair in range(PAIRS):
        picked = jnp.where(chosen == 2 * pair, table[:, pair * LANES : (pair + 1) * LANES], picked)
    return picked


def place_pairs(parts, chosen):
    columns = []
    for pair in range(PAIRS):
        total = jnp.zeros(chosen[0].shape, parts[0].dtype)
        for part, choice in zip(parts, chosen):
            total = jnp.where(choice == 2 * pair, part, total)
        columns.append(total)
    return jnp.concatenate(columns, 1)


def choices(routes, rows, dtype):
    half = (lane_index(rows) >= HD).astype(jnp.int32)
    return [(column(routes, slot, rows) - half).astype(F32).astype(dtype) for slot in range(TOPK)]


def gains_of(tail):
    return tail.astype(F32).T


def flat_of(index):
    x, y, z = index // 8, index // 4 % 2, index % 4
    return ((z * 2 + y) * 2 + x) * 2


def embed_kernel(x_ref, routes_ref, w_ref, h_ref, kv_ref, gate_ref):
    rows = x_ref.shape[0]
    gain = gains_of(w_ref[:, LANES:])[E : E + 1]
    normal, _ = standardize(x_ref[...].astype(F32))
    h = (normal * gain).astype(BF16)
    h_ref[...] = h
    proj = dot(h, w_ref[...])
    kv_ref[...] = proj[:, :LANES].astype(BF16)
    logits = proj[:, LANES:]
    routes = routes_ref[...]
    lane = lane_index(rows)
    columns = [column(routes, slot, rows) for slot in range(TOPK)]
    chosen = jnp.zeros((rows, LANES), jnp.bool_)
    for route in columns:
        chosen = chosen | (lane == route)
    peak = jnp.max(jnp.where(chosen, logits, MASKED), -1, keepdims=True)
    expo = jnp.where(chosen, jnp.exp(jnp.where(chosen, logits - peak, 0.0)), 0.0)
    dense = expo / jnp.sum(expo, -1, keepdims=True)
    gates = jnp.zeros((rows, LANES), F32)
    for slot, route in enumerate(columns):
        hit = jnp.where(lane == route, dense, 0.0)
        gates = jnp.where(lane == slot, jnp.sum(hit, -1, keepdims=True), gates)
    gate_ref[...] = gates


def embed_call(x, routes, weights, tile=256):
    rows, width = x.shape
    by_row = lambda count: pl.BlockSpec((tile, count), lambda i: (i, 0))
    return pl.pallas_call(
        embed_kernel,
        grid=(rows // tile,),
        in_specs=[by_row(width), by_row(TOPK), pl.BlockSpec(weights.shape, lambda i: (0, 0))],
        out_specs=[by_row(width), by_row(LANES), by_row(LANES)],
        out_shape=[
            jax.ShapeDtypeStruct((rows, width), BF16),
            jax.ShapeDtypeStruct((rows, LANES), BF16),
            jax.ShapeDtypeStruct((rows, LANES), F32),
        ],
        compiler_params=pltpu.CompilerParams(vmem_limit_bytes=12 << 20),
        cost_estimate=pl.CostEstimate(
            flops=4 * rows * width * LANES, bytes_accessed=8 * rows * width, transcendentals=0
        ),
        name="embed",
    )(x, routes, weights)


def query_kernel(me_ref, h_ref, routes_ref, near_ref, far_ref, q_ref, w_ref, sems):
    rows = h_ref.shape[0]
    pieces, piece, _ = near_ref.shape

    @pl.when(pl.program_id(0) == 0)
    def _():
        copies = []
        for core, part in enumerate((near_ref, far_ref)):
            for index in range(pieces):
                owner = me_ref[0] ^ (flat_of(index) + core)
                first = pl.multiple_of(owner * piece, piece)
                copies.append(
                    pltpu.make_async_copy(
                        part.at[index], w_ref.at[pl.ds(first, piece), :], sems.at[core * pieces + index]
                    )
                )
        for copy in copies:
            copy.start()
        for copy in copies:
            copy.wait()

    table = dot(h_ref[...], w_ref[...]).astype(BF16)
    for slot, choice in enumerate(choices(routes_ref[...], rows, BF16)):
        q_ref[slot] = pick_pairs(table, choice)


def query_call(me, h, routes, near, far, tile=256):
    rows, width = h.shape
    pieces, piece, cols = near.shape
    by_row = lambda count: pl.BlockSpec((tile, count), lambda i, s: (i, 0))
    return pl.pallas_call(
        query_kernel,
        grid_spec=pltpu.PrefetchScalarGridSpec(
            num_scalar_prefetch=1,
            grid=(rows // tile,),
            in_specs=[
                by_row(width),
                by_row(TOPK),
                pl.BlockSpec(memory_space=pl.ANY),
                pl.BlockSpec(memory_space=pl.ANY),
            ],
            out_specs=[
                pl.BlockSpec((TOPK, tile, LANES), lambda i, s: (0, i, 0)),
                pl.BlockSpec((width, cols), lambda i, s: (0, 0)),
            ],
            scratch_shapes=[pltpu.SemaphoreType.DMA((2 * pieces,))],
        ),
        out_shape=[
            jax.ShapeDtypeStruct((TOPK, rows, LANES), BF16),
            jax.ShapeDtypeStruct((width, cols), BF16),
        ],
        compiler_params=pltpu.CompilerParams(vmem_limit_bytes=16 << 20),
        cost_estimate=pl.CostEstimate(
            flops=2 * rows * width * cols, bytes_accessed=8 * rows * width + 2 * width * cols, transcendentals=0
        ),
        name="query",
    )(me, h, routes, near, far)


def spread_keyval(device, kv_refs, key_ref, value_ref):
    devices = len(kv_refs)
    _, block, _ = kv_refs[0].shape
    low_half = lane_index(block) < HD
    for index in range(devices):
        for high in range(2):
            rows = kv_refs[index][high].astype(F32)
            rolled = pltpu.roll(rows, HD, 1)
            span = block_of(device ^ index, high, devices, block)
            key_ref[span, :] = jnp.where(low_half, rows, rolled).astype(BF16)
            value_ref[span, :] = jnp.where(low_half, rolled, rows).astype(BF16)


def block_of(device, high, devices, block):
    place = 2 * devices - 1 - device if high else device
    return pl.ds(pl.multiple_of(place * block, block), block)


def attend_kernel(place_ref, q_ref, *refs):
    *kv_refs, o_ref, log_ref, key_ref, plain_ref, value_ref, acc_ref, peak_ref, bound_ref = refs
    step = pl.program_id(0)
    slots, tile, _ = q_ref.shape
    rows = slots * tile
    width = 512

    @pl.when(step == 0)
    def _():
        spread_keyval(place_ref[2, 0], kv_refs, key_ref, plain_ref)
        value_ref[:, :LANES] = plain_ref[...]
        value_ref[:, LANES:] = jnp.ones((value_ref.shape[0], LANES), BF16)
        keys = key_ref[...].astype(F32)
        bound_ref[0] = jnp.max(jnp.sum(keys * keys, -1, keepdims=True)) * 0.5
        bound_ref[1] = jnp.max(jnp.abs(plain_ref[...].astype(F32)))

    here = place_ref[0, step]
    lower = pl.multiple_of(place_ref[1, step], width)
    q = q_ref[...].reshape(rows, LANES)
    qf = q.astype(F32)
    longest = jnp.max(jnp.sum(qf * qf, -1, keepdims=True))
    plain = (longest * bound_ref[0] <= (SAFE_SCORE / SCALE) ** 2) & (bound_ref[1] <= SAFE_VALUE)
    full = (here - lower) // width
    last = pl.multiple_of(lower + full * width, width)
    token = lax.broadcasted_iota(jnp.int32, (tile, width), 0) + here
    allowed = (lax.broadcasted_iota(jnp.int32, (tile, width), 1) + last) <= token
    allowed = jnp.broadcast_to(allowed[None], (slots, tile, width)).reshape(rows, width)

    def finish(out, logs):
        o_ref[...] = out.astype(o_ref.dtype).reshape(slots, tile, LANES)
        logs = logs.reshape(slots, tile, LANES)
        lane = lane_index(tile)
        packed = jnp.zeros((tile, LANES), F32)
        for slot in range(slots):
            packed = jnp.where(lane == slot, logs[slot], packed)
        log_ref[...] = packed

    pairs = full // 2

    @pl.when(plain)
    def _():
        for count, edge_width in ((0, width // 2), (0, width), (1, width // 2), (1, width)):

            @pl.when((full % 2 == count) & ((here - last >= width // 2) == (edge_width == width)))
            def _(count=count, edge_width=edge_width):
                inner = count * width
                span = pl.ds(pl.multiple_of(lower + pairs * 2 * width, width), inner + edge_width)
                expo = jnp.exp2(dot_last(q, key_ref[span, :]) * (SCALE * LOG2E))
                edge = jnp.where(allowed[:, :edge_width], expo[:, inner:], 0.0).astype(BF16)
                expo = jnp.concatenate([expo[:, :inner].astype(BF16), edge], 1) if count else edge
                acc_ref[...] = dot(expo, value_ref[span, :])

        def body(index, carry):
            span = pl.ds(pl.multiple_of(lower + index * 2 * width, width), 2 * width)
            expo = jnp.exp2(dot_last(q, key_ref[span, :]) * (SCALE * LOG2E)).astype(BF16)
            acc_ref[...] += dot(expo, value_ref[span, :])
            return carry

        lax.fori_loop(0, pairs, body, 0)
        total = acc_ref[:, LANES:]
        finish(acc_ref[:, :LANES] / total, jnp.log2(total))

    @pl.when(jnp.logical_not(plain))
    def _():
        def scaled(span):
            return dot_last(q, key_ref[span, :]) * (SCALE * LOG2E)

        scores = jnp.where(allowed, scaled(pl.ds(last, width)), MASKED)
        peak = jnp.max(scores, -1, keepdims=True)
        peak_ref[...] = jnp.broadcast_to(peak, (rows, LANES))
        acc_ref[...] = dot(jnp.exp2(scores - peak).astype(BF16), value_ref[pl.ds(last, width), :])

        def body(index, carry):
            span = pl.ds(pl.multiple_of(lower + index * width, width), width)
            scores = scaled(span)
            before = peak_ref[:, :1]
            peak = jnp.maximum(before, jnp.max(scores, -1, keepdims=True))
            peak_ref[...] = jnp.broadcast_to(peak, (rows, LANES))
            expo = jnp.exp2(scores - peak).astype(BF16)
            acc_ref[...] = acc_ref[...] * jnp.exp2(before - peak) + dot(expo, value_ref[span, :])
            return carry

        lax.fori_loop(0, full, body, 0)
        total = acc_ref[:, LANES:]
        finish(acc_ref[:, :LANES] / total, peak_ref[...] + jnp.log2(total))


def attend_call(place, q, kv, tile=128):
    slots, rows, _ = q.shape
    count = len(kv) * kv[0].shape[0] * kv[0].shape[1]
    return pl.pallas_call(
        attend_kernel,
        grid_spec=pltpu.PrefetchScalarGridSpec(
            num_scalar_prefetch=1,
            grid=(rows // tile,),
            in_specs=[
                pl.BlockSpec((slots, tile, LANES), lambda i, s: (0, i, 0)),
                *[pl.BlockSpec(part.shape, lambda i, s: (0, 0, 0)) for part in kv],
            ],
            out_specs=[
                pl.BlockSpec((slots, tile, LANES), lambda i, s: (0, i, 0)),
                pl.BlockSpec((tile, LANES), lambda i, s: (i, 0)),
                pl.BlockSpec((count, LANES), lambda i, s: (0, 0)),
                pl.BlockSpec((count, LANES), lambda i, s: (0, 0)),
            ],
            scratch_shapes=[
                pltpu.VMEM((count, 2 * LANES), BF16),
                pltpu.VMEM((slots * tile, 2 * LANES), F32),
                pltpu.VMEM((slots * tile, LANES), F32),
                pltpu.SMEM((2,), F32),
            ],
        ),
        out_shape=[
            jax.ShapeDtypeStruct((slots, rows, LANES), BF16),
            jax.ShapeDtypeStruct((rows, LANES), F32),
            jax.ShapeDtypeStruct((count, LANES), BF16),
            jax.ShapeDtypeStruct((count, LANES), BF16),
        ],
        compiler_params=pltpu.CompilerParams(vmem_limit_bytes=24 << 20),
        cost_estimate=pl.CostEstimate(
            flops=8 * slots * rows * count * LANES, bytes_accessed=8 * slots * rows * LANES, transcendentals=0
        ),
        name="attend",
    )(place, q, *kv)


def attend_back_kernel(first, final, tile_of, groups, before, *refs):
    refs = list(refs)
    take = lambda count: [refs.pop(0) for _ in range(count)]
    place_ref, q_ref, do_ref, log_ref, delta_ref, routes_ref, key_ref, value_ref = take(8)
    if not first:
        (sums_in,) = take(1)
    if final:
        (h_ref,) = take(1)
        before_refs = take(before)
    (all_ref,) = take(1)
    outs = take(4 if final else 1)
    dq_ref, dkey_ref, dvalue_ref, sems = take(4)
    step = pl.program_id(0)
    steps = pl.num_programs(0)
    slots, tile, _ = q_ref.shape
    rows = slots * tile
    width = 512

    def carry_copies():
        return [
            pltpu.make_async_copy(sums_in.at[0], dkey_ref.at[pl.ds(0, HD), :], sems.at[0]),
            pltpu.make_async_copy(sums_in.at[1], dvalue_ref.at[pl.ds(0, HD), :], sems.at[1]),
        ]

    @pl.when(step == 0)
    def _():
        if first:
            dkey_ref[:HD] = jnp.zeros_like(dkey_ref[:HD])
            dvalue_ref[:HD] = jnp.zeros_like(dvalue_ref[:HD])
        else:
            for copy in carry_copies():
                copy.start()
        dkey_ref[HD:] = jnp.zeros_like(dkey_ref[HD:])
        dvalue_ref[HD:] = jnp.zeros_like(dvalue_ref[HD:])

    here = place_ref[0, tile_of(step)]
    lower = place_ref[1, tile_of(step)]
    q = q_ref[...].reshape(rows, LANES)
    do = do_ref[...].reshape(rows, LANES)
    logs = log_ref[...]
    deltas = delta_ref[...]
    logs = jnp.concatenate([column(logs, slot, tile) for slot in range(slots)], 0)
    deltas = jnp.concatenate([column(deltas, slot, tile) for slot in range(slots)], 0)
    full = (here - lower) // width
    last = pl.multiple_of(lower + full * width, width)
    token = lax.broadcasted_iota(jnp.int32, (tile, width), 0) + here
    allowed = (lax.broadcasted_iota(jnp.int32, (tile, width), 1) + last) <= token
    allowed = jnp.broadcast_to(allowed[None], (slots, tile, width)).reshape(rows, width)

    if not first:

        @pl.when(step == 0)
        def _():
            for copy in carry_copies():
                copy.wait()

    def one(start, size, masked):
        wide = lambda values: jnp.concatenate([values] * (size // LANES), 1)
        span = pl.ds(start, size)
        keys = key_ref[span, :]
        scores = dot_last(q, keys)
        probs = jnp.exp2(scores * (SCALE * LOG2E) - wide(logs))
        if masked:
            probs = jnp.where(allowed[:, :size], probs, 0.0)
        dprobs = dot_last(do, value_ref[span, :])
        dscores = (probs * (dprobs - wide(deltas))).astype(BF16)
        dvalue_ref[:, span] += dot_first(do, probs.astype(BF16))
        dkey_ref[:, span] += dot_first(q, dscores)
        return dot(dscores, keys)

    for size in (width // 2, width):

        @pl.when((here - last >= width // 2) == (size == width))
        def _(size=size):
            dq_ref[...] = one(last, size, True)

    def body(index, carry):
        dq_ref[...] += one(pl.multiple_of(lower + index * width, width), width, False)
        return carry

    lax.fori_loop(0, full, body, 0)

    def sum_copies():
        return [
            pltpu.make_async_copy(dkey_ref.at[pl.ds(0, HD), :], outs[0].at[0], sems.at[0]),
            pltpu.make_async_copy(dvalue_ref.at[pl.ds(0, HD), :], outs[0].at[1], sems.at[1]),
        ]

    if not final:

        @pl.when(step == steps - 1)
        def _():
            dkey_ref[:HD] += dkey_ref[HD:]
            dvalue_ref[:HD] += dvalue_ref[HD:]
            for copy in sum_copies():
                copy.start()

    dq = (dq_ref[...] * SCALE).astype(BF16).reshape(slots, tile, LANES)
    mine = pl.ds(pl.multiple_of(step * tile, tile), tile)
    all_ref[mine, :] = place_pairs([dq[slot] for slot in range(slots)], choices(routes_ref[...], tile, BF16))

    @pl.when(step == steps - 1)
    def _():
        if not final:
            for copy in sum_copies():
                copy.wait()
            return
        kv_keep, kv_send, gq_keep, gq_send = outs
        _, _, block, _ = kv_keep.shape
        device = place_ref[2, 0]
        for index in range(4):
            target = kv_send if index % 2 else kv_keep
            for high in range(2):
                span = block_of(device ^ index, high, 4, block)
                dkeys = (dkey_ref[:HD, span] + dkey_ref[HD:, span]) * SCALE
                dvalues = dvalue_ref[:HD, span] + dvalue_ref[HD:, span]
                target[index // 2, high] = jnp.concatenate([dkeys, dvalues], 0).T.astype(BF16)
        gq = dot_first(h_ref[...], in_rows([*before_refs, all_ref]))
        if groups == 8:
            scatter_rows(gq, gq_keep, gq_send, device % 2)
        else:
            gq_keep[...] = gq.astype(BF16)
            gq_send[...] = jnp.zeros_like(gq_send)


def in_rows(parts):
    half = lambda part: part.shape[0] // 2
    return jnp.concatenate([part[: half(part)] for part in parts] + [part[half(part) :] for part in parts], 0)


def scatter_rows(grad, keep, send, core):
    for x in range(2):
        for y in range(2):
            for z in range(4):
                base = (((z * 2 + y) * 2 + x) * 2) * 16
                low = grad[base : base + 16].astype(BF16)
                high = grad[base + 16 : base + 32].astype(BF16)
                keep[y, z, x] = jnp.where(core == 0, low, high)
                send[y, z, x] = jnp.where(core == 0, high, low)


def attend_back_call(start, count, tiles, groups, where, q, do, logs, deltas, routes, keys, values, carried, h, before):
    slots, rows, _ = q.shape
    length = keys.shape[0]
    width = h.shape[1]
    tile = rows // (2 * tiles)
    first, final = start == 0, start + count == tiles

    def tile_of(step):
        return jnp.where(step < count, start + step, tiles + start + step - count)

    whole = lambda shape: pl.BlockSpec(shape, lambda i, s: (0,) * len(shape))
    anywhere = pl.BlockSpec(memory_space=pl.ANY)
    by_slot = pl.BlockSpec((slots, tile, LANES), lambda i, s: (0, tile_of(i), 0))
    by_row = lambda cols: pl.BlockSpec((tile, cols), lambda i, s: (tile_of(i), 0))
    in_specs = [
        by_slot, by_slot, by_row(LANES), by_row(LANES), by_row(TOPK), whole(keys.shape), whole(values.shape),
    ]
    in_specs += [anywhere] * len(carried)
    extra = [h, *before] if final else []
    in_specs += [whole(array.shape) for array in extra]
    out_specs = [whole((2 * count * tile, SPAN))]
    out_shape = [jax.ShapeDtypeStruct((2 * count * tile, SPAN), BF16)]
    if final:
        kv_shape = (2, 2, rows // 2, LANES)
        gq_shape = (2, 4, 2, 16, SPAN) if groups == 8 else (width, SPAN)
        off_shape = gq_shape if groups == 8 else (8, LANES)
        for shape in (kv_shape, kv_shape, gq_shape, off_shape):
            out_specs.append(whole(shape))
            out_shape.append(jax.ShapeDtypeStruct(shape, BF16))
    else:
        out_specs.append(anywhere)
        out_shape.append(jax.ShapeDtypeStruct((2, HD, length), F32))
    return pl.pallas_call(
        functools.partial(attend_back_kernel, first, final, tile_of, groups, len(before)),
        grid_spec=pltpu.PrefetchScalarGridSpec(
            num_scalar_prefetch=1,
            grid=(2 * count,),
            in_specs=in_specs,
            out_specs=out_specs,
            scratch_shapes=[
                pltpu.VMEM((slots * tile, LANES), F32),
                pltpu.VMEM((LANES, length), F32),
                pltpu.VMEM((LANES, length), F32),
                pltpu.SemaphoreType.DMA((2,)),
            ],
        ),
        out_shape=out_shape,
        compiler_params=pltpu.CompilerParams(vmem_limit_bytes=20 << 20),
        cost_estimate=pl.CostEstimate(
            flops=10 * slots * 2 * count * tile * length * LANES, bytes_accessed=16 * slots * tile * LANES, transcendentals=0
        ),
        name="attend_back",
    )(where, q, do, logs, deltas, routes, keys, values, *carried, *extra)


def query_back_kernel(dlog_ref, wq_ref, wr_ref, *refs):
    *all_refs, dh_ref = refs
    rows = in_rows(all_refs)
    dh_ref[...] = dot_last(rows, wq_ref[...]) + dot_last(dlog_ref[...], wr_ref[...])


def query_back_call(dlogits, wq, wk, parts):
    rows = dlogits.shape[0]
    width = wq.shape[0]
    cols = lambda size, index: pl.BlockSpec((width, size), lambda i: (0, index))
    whole = lambda shape: pl.BlockSpec(shape, lambda i: (0,) * len(shape))
    return pl.pallas_call(
        query_back_kernel,
        grid=(1,),
        in_specs=[
            whole(dlogits.shape), cols(SPAN, 0), cols(LANES, 1), *[whole(part.shape) for part in parts],
        ],
        out_specs=whole((rows, width)),
        out_shape=jax.ShapeDtypeStruct((rows, width), F32),
        compiler_params=pltpu.CompilerParams(vmem_limit_bytes=24 << 20),
        cost_estimate=pl.CostEstimate(
            flops=2 * rows * width * (SPAN + LANES), bytes_accessed=4 * rows * (SPAN + width), transcendentals=0
        ),
        name="query_back",
    )(dlogits, wq, wk, *parts)


def middle_kernel(groups, *refs):
    refs = list(refs)
    take = lambda count: [refs.pop(0) for _ in range(count)]
    core_ref, x_hbm, dy_hbm, o_hbm, gate_ref, routes_ref, tail_ref = take(7)
    weights_in = take(8 if groups == 8 else 3)
    out_hbm, ring_hbm, swap_hbm, dmid_hbm, do_hbm, delta_ref, dlog_ref, gain_ref = take(8)
    outs_hbm = take(4 if groups == 8 else 3)
    x_ref, dy_ref, o_ref, comb_ref, mid_ref, normal_ref, acc_ref, dh_ref, dcomb_ref, out_ref, do_ref = take(11)
    wo_in, w1_in, w2_in = take(3)
    in_sems, out_sems = take(2)
    outs = refs
    rows, width = x_ref.shape
    part = 256
    cols = 512
    count = [0]

    def copy(source, target):
        count[0] += 1
        return pltpu.make_async_copy(source, target, in_sems.at[count[0] - 1])

    slot_copies = [copy(o_hbm.at[slot], o_ref.at[slot]) for slot in range(TOPK)]
    x_copy, dy_copy = copy(x_hbm, x_ref), copy(dy_hbm, dy_ref)
    if groups == 8:
        flat = core_ref[0]
        my_x, my_y, core = flat // 2 % 2, flat // 4 % 2, flat % 2
        wo_copies, w1_copies, w2_copies = [], [], []
        for index in range(8):
            other_core, other = index // 4, index % 4
            for y_turn in range(2):
                y = my_y ^ y_turn
                part_a = weights_in[4 * other_core + (other // 2)]
                x = my_x ^ (other // 2)
                mp = 2 * x + (core ^ other_core)
                across = pl.ds(pl.multiple_of(mp * cols, cols), cols)
                if other % 2 == 0:
                    wo_copies.append(copy(part_a.at[y_turn, :, 4:6], wo_in.at[:, y, mp, 0:2]))
                    w1_copies.append(copy(part_a.at[y_turn, :, 0:4], w1_in.at[:, y, :, :, across]))
                else:
                    part_b = weights_in[4 * other_core + 2 + y_turn]
                    x_turn = other // 2
                    wo_copies.append(copy(part_b.at[x_turn, :, 4:5], wo_in.at[:, y, mp, 2:3]))
                    w2_copies.append(copy(part_b.at[x_turn, :, 0:4], w2_in.at[:, y, :, :, across]))
    else:
        wo_copies, w1_copies, w2_copies = [
            [copy(source, target)] for source, target in zip(weights_in, (wo_in, w1_in, w2_in))
        ]
    for one in (*slot_copies, *wo_copies, x_copy, *w1_copies, dy_copy, *w2_copies):
        one.start()
    view = lambda ref: ref[...].reshape(width, -1)
    third = lambda ref, index: ref[:, :, :, index].reshape(width, cols)

    gain = gains_of(tail_ref[...])[E + 1 : E + 2]
    for one in slot_copies:
        one.wait()

    def combine(index, carry):
        mine = pl.ds(pl.multiple_of(index * part, part), part)
        gates = gate_ref[mine, :]
        weighted = [(column(gates, slot, part) * o_ref[slot, mine, :].astype(F32)).astype(BF16) for slot in range(TOPK)]
        comb_ref[mine, :] = place_pairs(weighted, choices(routes_ref[mine, :], part, BF16))
        return carry

    lax.fori_loop(0, rows // part, combine, 0)
    for one in (*wo_copies, x_copy):
        one.wait()
    mid = x_ref[...].astype(F32)
    if groups == 8:
        for index in range(3):
            mid = mid + dot_last(comb_ref[:, index * cols : (index + 1) * cols], third(wo_in, index))
    else:
        mid = mid + dot_last(comb_ref[...], wo_in[...])
    mid_ref[...] = mid
    normal, factor = standardize(mid)
    normal_ref[...] = normal
    h2 = (normal * gain).astype(BF16)
    for one in (*w1_copies, dy_copy, *w2_copies):
        one.wait()
    dy = dy_ref[...]
    w1, w2 = view(w1_in), view(w2_in)

    for index in range(w1.shape[1] // cols):
        span = slice(index * cols, (index + 1) * cols)
        up, down = w1[:, span], w2[:, span]
        pre = dot(h2, up)
        dact = dot(dy, down)
        sigma = jax.nn.sigmoid(pre)
        act = (pre * sigma).astype(BF16)
        dpre = (dact * (sigma * (1.0 + pre * (1.0 - sigma)))).astype(BF16)
        branch = dot_last(act, down)
        dh2 = dot_last(dpre, up)
        if index == 0:
            acc_ref[...] = branch
            dh_ref[...] = dh2
        else:
            acc_ref[...] += branch
            dh_ref[...] += dh2
        g1 = dot_first(h2, dpre).astype(BF16)
        g2 = dot_first(dy, act).astype(BF16)
        if groups != 8:
            outs[0][:, span] = g1
            outs[1][:, span] = g2
            continue
        for mine, (a, b) in ((True, (outs[0], outs[2])), (False, (outs[1], outs[3]))):

            @pl.when((core_ref[0] % 2 == index % 2) == mine)
            def _(a=a, b=b, g1=g1, g2=g2, x=index // 2):
                for owner in range(8):
                    piece = slice(owner * 64, owner * 64 + 64)
                    a[x, owner % 2, owner // 2, :64] = g1[piece]
                    b[owner % 2, x, owner // 2, :64] = g2[piece]

    out_ref[...] = (mid_ref[...] + acc_ref[...]).astype(BF16)
    out_copy = pltpu.make_async_copy(out_ref, out_hbm, out_sems.at[0])
    out_copy.start()
    half = rows // 2
    sends = [
        pltpu.make_async_copy(
            out_ref.at[pl.ds(pl.multiple_of(core_ref[1 + index], half), half), :], target, out_sems.at[7 + index]
        )
        for index, target in enumerate((ring_hbm, swap_hbm))
    ]
    for one in sends:
        one.start()
    dh2 = dh_ref[...]
    normal = normal_ref[...]
    gain_ref[...] = jnp.sum(dh2 * normal, 0, keepdims=True)
    dmid = dy.astype(F32) + norm_back(dh2 * gain, normal, factor)
    mid_ref[...] = dmid
    dmid_copy = pltpu.make_async_copy(mid_ref, dmid_hbm, out_sems.at[1])
    dmid_copy.start()
    dmid_b = dmid.astype(BF16)
    if groups == 8:
        for index in range(3):
            span = slice(index * cols, (index + 1) * cols)
            dcomb_ref[:, span] = dot(dmid_b, third(wo_in, index)).astype(BF16)
    else:
        dcomb_ref[...] = dot(dmid_b, wo_in[...]).astype(BF16)
    go = dot_first(dmid_b, comb_ref[...]).astype(BF16)
    if groups == 8:
        for core in range(2):

            @pl.when(core_ref[0] % 2 == core)
            def _(pairs=((outs[0], outs[2]), (outs[1], outs[3])), core=core):
                for owner in range(32):
                    z, y, x, c = owner // 8, owner // 4 % 2, owner // 2 % 2, owner % 2
                    a, b = pairs[c ^ core]
                    mine = slice(owner * 16, owner * 16 + 16)
                    a[x, y, z, 64:80] = go[mine, :512]
                    a[x, y, z, 80:] = go[mine, 512:1024]
                    b[y, x, z, 64:] = go[mine, 1024:]
    else:
        outs[2][...] = go

    grad_copies = [
        pltpu.make_async_copy(source, target, out_sems.at[3 + index])
        for index, (source, target) in enumerate(zip(outs, outs_hbm))
    ]
    for one in grad_copies:
        one.start()

    def spread(index, carry):
        mine = pl.ds(pl.multiple_of(index * part, part), part)
        gates = gate_ref[mine, :]
        routes = routes_ref[mine, :]
        lane = lane_index(part)
        dcomb = dcomb_ref[mine, :]
        gate_grads = jnp.zeros((part, LANES), F32)
        for slot, choice in enumerate(choices(routes, part, BF16)):
            picked = pick_pairs(dcomb, choice).astype(F32)
            do_ref[slot, mine, :] = (column(gates, slot, part) * picked).astype(BF16)
            total = jnp.sum(o_ref[slot, mine, :].astype(F32) * picked, -1, keepdims=True)
            gate_grads = jnp.where(lane == slot, total, gate_grads)
        weighted = gates * gate_grads
        delta_ref[mine, :] = weighted
        dsel = weighted - gates * jnp.sum(weighted, -1, keepdims=True)
        dlogits = jnp.zeros((part, LANES), F32)
        for slot in range(TOPK):
            dlogits = jnp.where(lane == column(routes, slot, part), column(dsel, slot, part), dlogits)
        dlog_ref[mine, :] = dlogits.astype(BF16)
        return carry

    lax.fori_loop(0, rows // part, spread, 0)
    do_copy = pltpu.make_async_copy(do_ref, do_hbm, out_sems.at[2])
    do_copy.start()
    for one in (out_copy, *sends, dmid_copy, do_copy, *grad_copies):
        one.wait()


def middle_call(groups, core, x, dy, o, gates, routes, front, weights):
    rows, width = x.shape
    hidden = 2048
    whole = lambda shape: pl.BlockSpec(shape, lambda i, s: (0,) * len(shape))
    anywhere = pl.BlockSpec(memory_space=pl.ANY)
    if groups == 8:
        grads = [(2, 2, 4, 96, 512), (2, 2, 4, 96, 512), (2, 2, 4, 80, 512), (2, 2, 4, 80, 512)]
        held = [(4, 2, 4, 3, 16, 512), (4, 2, 4, 16, hidden), (4, 2, 4, 16, hidden)]
    else:
        grads = [(width, hidden), (width, hidden), (width, SPAN)]
        held = [(width, SPAN), (width, hidden), (width, hidden)]
    return pl.pallas_call(
        functools.partial(middle_kernel, groups),
        grid_spec=pltpu.PrefetchScalarGridSpec(
            num_scalar_prefetch=1,
            grid=(1,),
            in_specs=[
                anywhere, anywhere, anywhere, whole(gates.shape), whole(routes.shape),
                pl.BlockSpec((width, LANES), lambda i, s: (0, 1)), *[anywhere] * len(weights),
            ],
            out_specs=[
                *[anywhere] * 5, whole((rows, LANES)), whole((rows, LANES)), whole((1, width)),
                *[anywhere] * len(grads),
            ],
            scratch_shapes=[
                pltpu.VMEM((rows, width), BF16),
                pltpu.VMEM((rows, width), BF16),
                pltpu.VMEM((TOPK, rows, LANES), BF16),
                pltpu.VMEM((rows, SPAN), BF16),
                pltpu.VMEM((rows, width), F32),
                pltpu.VMEM((rows, width), F32),
                pltpu.VMEM((rows, width), F32),
                pltpu.VMEM((rows, width), F32),
                pltpu.VMEM((rows, SPAN), BF16),
                pltpu.VMEM((rows, width), BF16),
                pltpu.VMEM((TOPK, rows, LANES), BF16),
                *[pltpu.VMEM(shape, BF16) for shape in held],
                pltpu.SemaphoreType.DMA((42,)),
                pltpu.SemaphoreType.DMA((9,)),
                *[pltpu.VMEM(shape, BF16) for shape in grads],
            ],
        ),
        out_shape=[
            jax.ShapeDtypeStruct((rows, width), BF16),
            jax.ShapeDtypeStruct((rows // 2, width), BF16),
            jax.ShapeDtypeStruct((rows // 2, width), BF16),
            jax.ShapeDtypeStruct((rows, width), F32),
            jax.ShapeDtypeStruct((TOPK, rows, LANES), BF16),
            jax.ShapeDtypeStruct((rows, LANES), F32),
            jax.ShapeDtypeStruct((rows, LANES), BF16),
            jax.ShapeDtypeStruct((1, width), F32),
            *[jax.ShapeDtypeStruct(shape, BF16) for shape in grads],
        ],
        compiler_params=pltpu.CompilerParams(vmem_limit_bytes=(45 if groups == 8 else 56) << 20),
        cost_estimate=pl.CostEstimate(
            flops=2 * rows * width * (6 * hidden + 3 * SPAN), bytes_accessed=16 * rows * width, transcendentals=0
        ),
        name="middle",
    )(core, x, dy, o, gates, routes, front, *weights)


def post_kernel(x_ref, h_ref, dmid_ref, dh_ref, keep_ref, recv_ref, dlog_ref, gain2_ref, w_ref, grad_ref, gk_ref, sum_ref):
    step = pl.program_id(0)
    gain = gains_of(w_ref[:, LANES:])[E : E + 1]
    normal, factor = standardize(x_ref[...].astype(F32))
    dkv = (keep_ref[...].astype(F32) + recv_ref[...].astype(F32)).astype(BF16)
    dh = dh_ref[...] + dot_last(dkv, w_ref[:, :LANES])
    grad_ref[...] = (dmid_ref[...] + norm_back(dh * gain, normal, factor)).astype(grad_ref.dtype)
    gain1 = jnp.sum(dh * normal, 0, keepdims=True)
    width = gain1.shape[1]
    row = lax.broadcasted_iota(jnp.int32, (LANES, width), 0)
    gain2 = jnp.where(step == 0, gain2_ref[...], 0.0)
    gains = jnp.where(row == E, gain1, jnp.where(row == E + 1, gain2, 0.0))
    h_turned = turned(h_ref[...])
    keyval = dot(h_turned, dkv)
    router = dot(h_turned, dlog_ref[...]) + gains.T

    @pl.when(step == 0)
    def _():
        sum_ref[:, :LANES] = keyval
        sum_ref[:, LANES:] = router

    @pl.when(step > 0)
    def _():
        sum_ref[:, :LANES] += keyval
        sum_ref[:, LANES:] += router

    @pl.when(step == pl.num_programs(0) - 1)
    def _():
        gk_ref[...] = sum_ref[...].astype(BF16)


def post_call(x, h, dmid, dh, keep, recv, dlogits, gain2, weights, tile=256):
    rows, width = x.shape
    by_row = lambda cols: pl.BlockSpec((tile, cols), lambda i: (i, 0))
    return pl.pallas_call(
        post_kernel,
        grid=(rows // tile,),
        in_specs=[
            by_row(width), by_row(width), by_row(width), by_row(width), by_row(LANES), by_row(LANES), by_row(LANES),
            pl.BlockSpec((1, width), lambda i: (0, 0)),
            pl.BlockSpec((width, 2 * LANES), lambda i: (0, 0)),
        ],
        out_specs=[by_row(width), pl.BlockSpec((width, 2 * LANES), lambda i: (0, 0))],
        out_shape=[
            jax.ShapeDtypeStruct((rows, width), BF16),
            jax.ShapeDtypeStruct((width, 2 * LANES), BF16),
        ],
        scratch_shapes=[pltpu.VMEM((width, 2 * LANES), F32)],
        compiler_params=pltpu.CompilerParams(vmem_limit_bytes=16 << 20),
        cost_estimate=pl.CostEstimate(
            flops=6 * rows * width * LANES, bytes_accessed=16 * rows * width, transcendentals=0
        ),
        name="finish",
    )(x, h, dmid, dh, keep, recv, dlogits, gain2, weights)


RING = ((0, 1), (1, 2), (2, 3), (3, 0))
SWAP = ((1, 3), (3, 1))


def halves(rows, place):
    half = rows.shape[0] // 2
    outer = (place == 0) | (place == 3)
    first = lax.dynamic_slice_in_dim(rows, jnp.where(outer, half, 0), half, 0)
    second = lax.dynamic_slice_in_dim(rows, jnp.where(place == 1, half, 0), half, 0)
    return first, second


def deal(rows, sent, place, ready=None):
    half = rows.shape[0] // 2
    ring = lax.ppermute(sent[0], "mp", RING)
    swap = lax.ppermute(sent[1], "mp", SWAP)
    if ready is not None:
        ring, swap = after((ring, swap), ready)
    low = jnp.where(place == 0, rows[:half], jnp.where(place == 3, swap, ring))
    high = jnp.where(place == 2, rows[half:], jnp.where(place == 1, swap, ring))
    return jnp.concatenate([low, high], 0)


def send_back(sent):
    first, second = sent
    ring = lax.ppermute(first, "mp", tuple((b, a) for a, b in RING))
    return ring, lax.ppermute(second, "mp", SWAP)


def put_back(rows, returned, place):
    half = rows.shape[0] // 2
    ring, swap = returned
    top = jnp.where(place == 0, rows[:half], jnp.where(place == 3, swap, ring))
    bottom = jnp.where(place == 2, rows[half:], jnp.where(place == 1, swap, ring))
    return jnp.concatenate([top, bottom], 0)


OTHER_CORE = ((0, 1), (1, 0), (2, 3), (3, 2))
OTHER_X = ((0, 2), (2, 0), (1, 3), (3, 1))


def swap_core(values):
    return lax.ppermute(values, "mp", OTHER_CORE)


def swap_x(values):
    return lax.ppermute(values, "mp", OTHER_X)


def swap_y(values):
    return lax.ppermute(values, "dp", tuple((i, i ^ 1) for i in range(8)))


def swap_z(values, turn):
    return lax.ppermute(values, "dp", tuple((i, i ^ (2 * turn)) for i in range(8)))


def at(values, index):
    return lax.dynamic_index_in_dim(values, index, 0, keepdims=False)


def added(left, right):
    return (left.astype(F32) + right.astype(F32)).astype(BF16)


def gather_z(shard, my_z):
    turns = [shard] + [swap_z(shard, turn) for turn in (1, 2, 3)]
    rows = []
    for z in range(4):
        row = turns[3]
        for turn in (2, 1, 0):
            row = jnp.where(my_z == z ^ turn, turns[turn], row)
        rows.append(row)
    return jnp.stack(rows)


def after(values, others):
    return lax.optimization_barrier((values, others))[0]


def tied(first, second):
    return lax.optimization_barrier((first, second))


def adam_step(param, first, second, grad, rate, decay):
    first_new = BETA_FIRST * first + (1.0 - BETA_FIRST) * grad
    second_new = BETA_SECOND * second + (1.0 - BETA_SECOND) * grad * grad
    first_hat = first_new / (1.0 - BETA_FIRST**ADAM_STEP)
    second_hat = second_new / (1.0 - BETA_SECOND**ADAM_STEP)
    param_new = param - rate * (first_hat / (jnp.sqrt(second_hat) + ADAM_EPS) + decay * param)
    return (second_new, param_new)


def update_kernel(
    rates_ref, squares_ref, gq_ref, go_ref, gk_ref, ffn_ref,
    ap_ref, am_ref, av_ref, fp_ref, fm_ref, fv_ref,
    ag_ref, avn_ref, apn_ref, fg_ref, fvn_ref, fpn_ref, norm_ref, gain_ref,
):
    norm = jnp.sqrt(jnp.sum(jnp.sum(squares_ref[...], 0), keepdims=True))
    norm_ref[...] = norm
    factor = jnp.minimum(1.0, CLIP_NORM / norm)
    tail = AC - 2 * SPAN
    for source, span, rate in (
        (gq_ref, slice(0, SPAN), rates_ref[0]),
        (go_ref, slice(SPAN, 2 * SPAN), rates_ref[1]),
        (gk_ref, slice(2 * SPAN, AC), None),
    ):
        decay = WEIGHT_DECAY
        grad = source[...] * factor
        if rate is None:
            grad = grad[:, :tail]
            place = lax.broadcasted_iota(jnp.int32, (1, tail), 1)
            rate = jnp.where(
                place < 2 * HD, rates_ref[2], jnp.where(place < 2 * HD + E, rates_ref[3], rates_ref[4])
            )
            decay = jnp.where(place < 2 * HD + E, WEIGHT_DECAY, 0.0)
            gain_ref[...] = grad[:, tail - 2 :]
        ag_ref[:, span] = grad
        avn_ref[:, span], apn_ref[:, span] = adam_step(
            ap_ref[:, span], am_ref[:, span], av_ref[:, span], grad, rate, decay
        )
    for index in range(2):
        grad = ffn_ref[index] * factor
        fg_ref[index] = grad
        fvn_ref[index], fpn_ref[index] = adam_step(
            fp_ref[index], fm_ref[index], fv_ref[index], grad, rates_ref[5 + index], WEIGHT_DECAY
        )


def squares_kernel(gq_ref, go_ref, ffn_ref, gk_ref, sums_ref, gk_out_ref):
    gk = jnp.sum(gk_ref[...].astype(F32), 0)
    gk_out_ref[...] = gk
    total = jnp.zeros((8, LANES), F32)
    for part in (gq_ref[...], go_ref[...], gk, ffn_ref[...].reshape(-1, ffn_ref.shape[-1])):
        square = part * part
        for row in range(0, square.shape[0], 8):
            for col in range(0, square.shape[1], LANES):
                total = total + square[row : row + 8, col : col + LANES]
    sums_ref[...] = jnp.broadcast_to(total[None], sums_ref.shape)


def squares_call(gq, go, ffn, gk):
    return pl.pallas_call(
        squares_kernel,
        out_shape=[
            jax.ShapeDtypeStruct((gk.shape[0], 8, LANES), F32),
            jax.ShapeDtypeStruct(gk.shape[1:], F32),
        ],
        compiler_params=pltpu.CompilerParams(vmem_limit_bytes=8 << 20),
        name="squares",
    )(gq, go, ffn, gk)


def update_call(rates, squares, gq, go, gk, ffn, attn, ffn_state):
    rows = gq.shape[0]
    attn_shape = jax.ShapeDtypeStruct(attn[0].shape, F32)
    ffn_shape = jax.ShapeDtypeStruct(ffn.shape, F32)
    whole = pl.BlockSpec(memory_space=pltpu.VMEM)
    return pl.pallas_call(
        update_kernel,
        in_specs=[pl.BlockSpec(memory_space=pltpu.SMEM)] + [whole] * 11,
        out_specs=[whole] * 8,
        out_shape=[
            attn_shape, attn_shape, attn_shape, ffn_shape, ffn_shape, ffn_shape,
            jax.ShapeDtypeStruct((1, 1), F32), jax.ShapeDtypeStruct((rows, 2), F32),
        ],
        compiler_params=pltpu.CompilerParams(vmem_limit_bytes=24 << 20),
        name="update",
    )(rates, squares, gq, go, gk, ffn, *attn, *ffn_state)


ALL = ("dp", "mp")


def shards(
    tokens, cotangent, routes, starts, attn_param, attn_first, attn_second, ffn_param, ffn_first, ffn_second, rates
):
    local_rows, width = tokens.shape
    place = lax.axis_index("mp")
    devices = lax.axis_size("mp")
    groups = lax.axis_size("dp")
    block = local_rows // 2
    manual = groups == 8
    _, depth, cols = ffn_param.shape
    my_x, my_y, my_z = place // 2, lax.axis_index("dp") % 2, lax.axis_index("dp") // 2
    flat = (lax.axis_index("dp") * devices + place).astype(jnp.int32)

    marks = jnp.concatenate([routes, starts[:, None] // block], 1).astype(BF16)
    marks = jnp.pad(marks, ((0, 0), (0, 16 - TOPK - 1))).T
    dealt = [tokens[:block], marks[:, :block], tokens[block:], marks[:, block:]]
    dealt = jnp.concatenate([part.reshape(-1, width) for part in dealt], 0)
    extra = dealt.shape[0] // 2 - block
    sent = halves(dealt, place)
    dealt = deal(dealt, sent, place)
    x = jnp.concatenate([dealt[:block], dealt[block + extra : 2 * block + extra]], 0)
    marks = [dealt[block : block + extra], dealt[2 * block + extra :]]
    marks = jnp.concatenate([part.reshape(16, block) for part in marks], 1).T[:, : TOPK + 1].astype(jnp.int32)

    attn_b = attn_param.astype(BF16)
    ffn_b = ffn_param.astype(BF16)
    pad = jnp.zeros((attn_b.shape[0], 2 * LANES - (AC - 2 * SPAN)), BF16)
    wk = jnp.concatenate([attn_b[:, 2 * SPAN :], pad], 1)
    wq = attn_b[:, :SPAN]
    wo = attn_b[:, SPAN : 2 * SPAN]
    if manual:
        wk, wq = after((wk, wq), sent)
        wk = lax.all_to_all(jnp.broadcast_to(wk, (groups * devices, *wk.shape)), ALL, 0, 0, tiled=True)
        wk = wk.reshape(-1, 2 * LANES)
        along = jnp.stack([wq] + [swap_z(wq, turn) for turn in (1, 2, 3)])
        along = jnp.stack([along, swap_y(along)])
        (along, x, marks), (ffn_b, wo) = tied((along, x, marks), (ffn_b, wo))
        near = jnp.stack([along, swap_x(along)]).reshape(16, *wq.shape)
        far = swap_core(near)
        chunk = [ffn_b[0].reshape(-1, 16, cols), wo[None, :, :cols], wo[None, :, cols : 2 * cols]]
        chunk += [ffn_b[1].reshape(-1, 16, cols), wo[None, :, 2 * cols :]]
        chunk = gather_z(jnp.concatenate(chunk, 0), my_z)
    else:
        wk = lax.all_gather(wk, ALL, axis=0, tiled=True)
        wq_all = lax.all_gather(wq, ALL, axis=0, tiled=True).reshape(4, 2, 2, 2, 16, -1)
        wq_all = wq_all.transpose(3, 2, 1, 0, 4, 5).reshape(2, 16, 16, -1)
        near, far = wq_all[0], wq_all[1]
        wo_full = lax.all_gather(wo, ALL, axis=0, tiled=True)
        ffn_all = lax.all_gather(ffn_b, ALL, axis=0, tiled=False)
        ffn_all = ffn_all.reshape(groups, devices, 2, depth, cols).transpose(2, 0, 3, 1, 4)
        ffn_all = ffn_all.reshape(2, groups * depth, devices * cols)
        weights = [wo_full, ffn_all[0], ffn_all[1]]

    routes_x = marks[:, :TOPK]
    tile = 128
    tiles = local_rows // tile
    pieces = tiles // 2
    index = jnp.arange(tiles, dtype=jnp.int32)
    low = index < pieces
    here = jnp.where(low, place * block + index * tile, (2 * devices - 1 - place) * block + (index - pieces) * tile)
    lower = jnp.where(low, marks[0, TOPK], marks[block, TOPK]) * block
    where = jnp.stack([here, lower, jnp.full((tiles,), place)]).astype(jnp.int32)

    h, kv, gates = embed_call(x, routes_x, wk)
    kv = kv.reshape(2, block, LANES)
    kv_x = swap_x(kv)
    me = flat.reshape(1) if manual else jnp.zeros((1,), jnp.int32)
    if manual:
        chunk = after(chunk, kv)
        a_own = chunk[:, :6]
        b_own = chunk[:, 6:]
        a_own = jnp.stack([a_own, swap_y(a_own)])
        b_own = jnp.stack([b_own, swap_x(b_own)])
        a_far, b_far = swap_x(a_own), swap_y(b_own)
        weights = [a_own, a_far, b_own, b_far]
        near, far = after((near, far), (a_own, b_own))
    q, wq_full = query_call(me, h, routes_x, near, far)
    o, logs, keys, values = attend_call(where, q, [kv, swap_core(kv), kv_x, swap_core(kv_x)], tile)
    if manual:
        own = [swap_core(a_own), swap_core(b_own)]
        a_far, b_far = after((a_far, b_far), logs)
        weights += [own[0], swap_core(a_far), own[1], swap_core(b_far)]
        cotangent = after(cotangent, (q, own))
    else:
        cotangent = after(cotangent, q)
    dy = deal(cotangent, halves(cotangent, place), place, logs)
    scalars = jnp.stack([flat, jnp.where((place == 0) | (place == 3), block, 0), jnp.where(place == 1, block, 0)])
    out, out_ring, out_swap, dmid, do, deltas, dlogits, gain2, *grads = middle_call(
        groups, scalars.astype(jnp.int32), x, dy, o, gates, routes_x, wk, weights
    )
    returned = send_back((out_ring, out_swap))

    def back(start, count, carried, before):
        return attend_back_call(
            start, count, pieces, groups, where, q, do, logs, deltas, routes_x, keys, values, carried, h, before
        )

    def split(parts, turn_a, turn_b, swap_a, swap_b):
        a_keep, a_in, b_keep, b_in = parts
        a_out = added(at(a_keep, 1 - turn_a), at(a_in, 1 - turn_a))
        b_out = added(at(b_keep, 1 - turn_b), at(b_in, 1 - turn_b))
        a_keep = added(at(a_keep, turn_a), at(a_in, turn_a))
        b_keep = added(at(b_keep, turn_b), at(b_in, turn_b))
        return (a_keep, swap_a(a_out), b_keep, swap_b(b_out))

    if manual:
        a_keep, a_send, b_keep, b_send = grads
        parts = split((a_keep, swap_core(a_send), b_keep, swap_core(b_send)), my_x, my_y, swap_x, swap_y)
    part_0, *carried = back(0, 2, (), ())
    if manual:
        carried, parts = tied(carried, parts)
        parts = split(parts, my_y, my_x, swap_y, swap_x)
    part_1, *carried = back(2, 1, carried, ())
    if manual:
        carried, parts = tied(carried, parts)
        both = jnp.concatenate([added(*parts[:2]), added(*parts[2:])], 1)
        moving = [swap_z(at(both, my_z ^ turn), turn) for turn in (1, 2, 3)]
        chunk_keep = at(both, my_z)
    part_2, kv_keep, kv_send, gq_keep, gq_send = back(3, 1, carried, (part_0, part_1))
    all_parts = [part_0, part_1, part_2]
    kv_in = swap_core(kv_send)
    kv_out = added(kv_keep[1], kv_in[1])
    kv_keep = added(kv_keep[0], kv_in[0]).reshape(local_rows, LANES)
    kv_recv = swap_x(kv_out).reshape(local_rows, LANES)
    dh = query_back_call(dlogits, wq_full, wk, after(all_parts, (kv_out, kv_keep)))
    if manual:
        gq_in = swap_core(gq_send)
        gq_send = added(at(gq_keep, 1 - my_y), at(gq_in, 1 - my_y))
        gq_keep = added(at(gq_keep, my_y), at(gq_in, my_y))
        gq_y = added(gq_keep, swap_y(gq_send))
        gq, returned = tied(gq_y, returned)
        gq_out = [at(gq, my_z ^ turn) for turn in (1, 2, 3)]
        dh, gq_out = tied(dh, gq_out)
        gq_in = [swap_z(part, turn) for part, turn in zip(gq_out, (1, 2, 3))]
        gq = at(gq, my_z)
    grad, gk = post_call(x, h, dmid, dh, kv_keep, kv_recv, dlogits, gain2, wk)
    if manual:
        gk = lax.all_to_all(gk.reshape(groups * devices, -1, 2 * LANES), ALL, 0, 0, tiled=True)
        gq = sum((part.astype(F32) for part in gq_in), gq.astype(F32)).astype(BF16)
        grad, gq = tied(grad, gq)
        gq_raw = at(gq, my_x).astype(F32) + swap_x(at(gq, 1 - my_x)).astype(F32)
    input_grad = put_back(grad, send_back(halves(grad, place)), place).astype(F32)
    layer_out = put_back(out, returned, place)

    if manual:
        chunk_raw = sum((part.astype(F32) for part in moving), chunk_keep.astype(F32))
        rows = depth
        ffn_raw = jnp.stack([chunk_raw[:rows], chunk_raw[rows + 32 : 2 * rows + 32]])
        go_raw = jnp.concatenate(
            [chunk_raw[rows : rows + 16], chunk_raw[rows + 16 : rows + 32], chunk_raw[2 * rows + 32 :]], 1
        )
    else:
        g1, g2, go = grads
        ffn_local = jnp.stack([g1, g2]).reshape(2, groups, depth, devices, cols).transpose(1, 3, 0, 2, 4)
        ffn_local = ffn_local.reshape(groups * devices * 2 * depth, cols)
        ffn_raw = lax.psum_scatter(ffn_local, ALL, scatter_dimension=0, tiled=True).astype(F32)
        ffn_raw = ffn_raw.reshape(2, depth, cols)
        go_raw = lax.psum_scatter(go, ALL, scatter_dimension=0, tiled=True).astype(F32)
        gq_raw = lax.psum_scatter(gq_keep, ALL, scatter_dimension=0, tiled=True).astype(F32)
        gk_raw = lax.psum_scatter(gk, ALL, scatter_dimension=0, tiled=True).astype(F32)
    if manual:
        squares, gk_raw = squares_call(gq_raw, go_raw, ffn_raw, gk)
        squares = lax.all_to_all(squares, ALL, 0, 0, tiled=True)
    else:
        squares = sum(jnp.sum(part * part) for part in (gq_raw, go_raw, gk_raw, ffn_raw))
        squares = lax.psum(squares, ALL) / (8 * LANES)
        squares = jnp.broadcast_to(squares, (1, 8, LANES))
    attn_grad, attn_second_new, attn_new, ffn_grad, ffn_second_new, ffn_new, grad_norm, gain_grad = update_call(
        rates, squares, gq_raw, go_raw, gk_raw, ffn_raw,
        (attn_param, attn_first, attn_second), (ffn_param, ffn_first, ffn_second),
    )
    return (
        layer_out,
        input_grad,
        attn_grad,
        attn_second_new,
        attn_new,
        ffn_grad,
        ffn_second_new,
        ffn_new,
        grad_norm.reshape(()),
        gain_grad,
    )


def solution(mesh):
    by_row = P(ALL, None)
    by_ffn = P(None, "dp", "mp")
    return jax.shard_map(
        shards,
        mesh=mesh,
        in_specs=(by_row, by_row, by_row, P(ALL), by_row, by_row, by_row, by_ffn, by_ffn, by_ffn, P()),
        out_specs=(by_row, by_row, by_row, by_row, by_row, by_ffn, by_ffn, by_ffn, P(), by_row),
        check_vma=False,
    )
```

```python
import functools
import math

import jax
import jax.numpy as jnp
from jax import lax
from jax.experimental import pallas as pl
from jax.experimental.pallas import tpu as pltpu
from jax.sharding import PartitionSpec as P

HD = 64
E = 24
TOPK = 8
ADAM_STEP = 7
AC = 3226
SPAN = E * HD
PAIRS = E // 2
LANES = 128

NORM_EPS = 1e-05
MASKED = -1e30
CLIP_NORM = 0.1
BETA_FIRST = 0.9
BETA_SECOND = 0.95
ADAM_EPS = 1e-08
WEIGHT_DECAY = 0.1

SCALE = HD ** (-0.5)
LOG2E = math.log2(math.e)
SAFE_SCORE = 40.0
SAFE_VALUE = 1e15
VMEM = 58 << 20

F32 = jnp.float32
BF16 = jnp.bfloat16


def dot(left, right):
    return jnp.dot(left, right, preferred_element_type=F32)


def dot_last(left, right):
    return lax.dot_general(left, right, (((1,), (1,)), ((), ())), preferred_element_type=F32)


def dot_first(left, right):
    return lax.dot_general(left, right, (((0,), (0,)), ((), ())), preferred_element_type=F32)


def turned(values):
    return values.astype(F32).T.astype(values.dtype)


def standardize(values):
    centred = values - jnp.mean(values, -1, keepdims=True)
    factor = lax.rsqrt(jnp.mean(centred * centred, -1, keepdims=True) + NORM_EPS)
    return (centred * factor, factor)


def norm_back(grad_normal, normal, factor):
    return factor * (
        grad_normal
        - jnp.mean(grad_normal, -1, keepdims=True)
        - normal * jnp.mean(grad_normal * normal, -1, keepdims=True)
    )


def lane_index(rows):
    return lax.broadcasted_iota(jnp.int32, (rows, LANES), 1)


def column(values, index, rows):
    return jnp.broadcast_to(values[:, index : index + 1], (rows, LANES))


def pick_pairs(table, chosen):
    picked = jnp.zeros(chosen.shape, table.dtype)
    for pair in range(PAIRS):
        picked = jnp.where(chosen == 2 * pair, table[:, pair * LANES : (pair + 1) * LANES], picked)
    return picked


def place_pairs(parts, chosen):
    columns = []
    for pair in range(PAIRS):
        total = jnp.zeros(chosen[0].shape, parts[0].dtype)
        for part, choice in zip(parts, chosen):
            total = jnp.where(choice == 2 * pair, part, total)
        columns.append(total)
    return jnp.concatenate(columns, 1)


def choices(routes, rows, dtype):
    half = (lane_index(rows) >= HD).astype(jnp.int32)
    return [(column(routes, slot, rows) - half).astype(F32).astype(dtype) for slot in range(TOPK)]


def gains_of(tail):
    return tail.astype(F32).T


def flat_of(index):
    x, y, z = index // 8, index // 4 % 2, index % 4
    return ((z * 2 + y) * 2 + x) * 2


def embed_kernel(x_ref, routes_ref, w_ref, h_ref, kv_ref, gate_ref):
    rows = x_ref.shape[0]
    gain = gains_of(w_ref[:, LANES:])[E : E + 1]
    normal, _ = standardize(x_ref[...].astype(F32))
    h = (normal * gain).astype(BF16)
    h_ref[...] = h
    proj = dot(h, w_ref[...])
    kv_ref[...] = proj[:, :LANES].astype(BF16)
    logits = proj[:, LANES:]
    routes = routes_ref[...]
    lane = lane_index(rows)
    columns = [column(routes, slot, rows) for slot in range(TOPK)]
    chosen = jnp.zeros((rows, LANES), jnp.bool_)
    for route in columns:
        chosen = chosen | (lane == route)
    peak = jnp.max(jnp.where(chosen, logits, MASKED), -1, keepdims=True)
    expo = jnp.where(chosen, jnp.exp(jnp.where(chosen, logits - peak, 0.0)), 0.0)
    dense = expo / jnp.sum(expo, -1, keepdims=True)
    gates = jnp.zeros((rows, LANES), F32)
    for slot, route in enumerate(columns):
        hit = jnp.where(lane == route, dense, 0.0)
        gates = jnp.where(lane == slot, jnp.sum(hit, -1, keepdims=True), gates)
    gate_ref[...] = gates


def embed_call(x, routes, weights, tile=512):
    rows, width = x.shape
    by_row = lambda count: pl.BlockSpec((tile, count), lambda i: (i, 0))
    return pl.pallas_call(
        embed_kernel,
        grid=(rows // tile,),
        in_specs=[by_row(width), by_row(TOPK), pl.BlockSpec(weights.shape, lambda i: (0, 0))],
        out_specs=[by_row(width), by_row(LANES), by_row(LANES)],
        out_shape=[
            jax.ShapeDtypeStruct((rows, width), BF16),
            jax.ShapeDtypeStruct((rows, LANES), BF16),
            jax.ShapeDtypeStruct((rows, LANES), F32),
        ],
        compiler_params=pltpu.CompilerParams(vmem_limit_bytes=12 << 20),
        cost_estimate=pl.CostEstimate(
            flops=60 * rows * width * LANES, bytes_accessed=8 * rows * width, transcendentals=0
        ),
        name="embed",
    )(x, routes, weights)


def query_kernel(me_ref, h_ref, routes_ref, near_ref, far_ref, q_ref, w_ref, sems):
    rows = h_ref.shape[0]
    pieces, piece, _ = near_ref.shape

    @pl.when(pl.program_id(0) == 0)
    def _():
        copies = []
        for core, part in enumerate((near_ref, far_ref)):
            for index in range(pieces):
                owner = me_ref[0] ^ (flat_of(index) + core)
                first = pl.multiple_of(owner * piece, piece)
                copies.append(
                    pltpu.make_async_copy(
                        part.at[index], w_ref.at[pl.ds(first, piece), :], sems.at[core * pieces + index]
                    )
                )
        for copy in copies:
            copy.start()
        for copy in copies:
            copy.wait()

    table = dot(h_ref[...], w_ref[...]).astype(BF16)
    for slot, choice in enumerate(choices(routes_ref[...], rows, BF16)):
        q_ref[slot] = pick_pairs(table, choice)


def query_call(me, h, routes, near, far, tile=512):
    rows, width = h.shape
    pieces, piece, cols = near.shape
    by_row = lambda count: pl.BlockSpec((tile, count), lambda i, s: (i, 0))
    return pl.pallas_call(
        query_kernel,
        grid_spec=pltpu.PrefetchScalarGridSpec(
            num_scalar_prefetch=1,
            grid=(rows // tile,),
            in_specs=[
                by_row(width),
                by_row(TOPK),
                pl.BlockSpec(memory_space=pl.ANY),
                pl.BlockSpec(memory_space=pl.ANY),
            ],
            out_specs=[
                pl.BlockSpec((TOPK, tile, LANES), lambda i, s: (0, i, 0)),
                pl.BlockSpec((width, cols), lambda i, s: (0, 0)),
            ],
            scratch_shapes=[pltpu.SemaphoreType.DMA((2 * pieces,))],
        ),
        out_shape=[
            jax.ShapeDtypeStruct((TOPK, rows, LANES), BF16),
            jax.ShapeDtypeStruct((width, cols), BF16),
        ],
        compiler_params=pltpu.CompilerParams(vmem_limit_bytes=16 << 20),
        cost_estimate=pl.CostEstimate(
            flops=8 * rows * width * cols, bytes_accessed=8 * rows * width + 2 * width * cols, transcendentals=0
        ),
        name="query",
    )(me, h, routes, near, far)


def spread_keyval(device, kv_refs, key_ref, value_ref):
    devices = len(kv_refs)
    _, block, _ = kv_refs[0].shape
    low_half = lane_index(block) < HD
    for index in range(devices):
        for high in range(2):
            rows = kv_refs[index][high].astype(F32)
            rolled = pltpu.roll(rows, HD, 1)
            span = block_of(device ^ index, high, devices, block)
            key_ref[span, :] = jnp.where(low_half, rows, rolled).astype(BF16)
            value_ref[span, :] = jnp.where(low_half, rolled, rows).astype(BF16)


def block_of(device, high, devices, block):
    place = 2 * devices - 1 - device if high else device
    return pl.ds(pl.multiple_of(place * block, block), block)


def attend_kernel(place_ref, q_ref, *refs):
    *kv_refs, o_ref, log_ref, key_ref, plain_ref, value_ref, acc_ref, peak_ref, bound_ref = refs
    step = pl.program_id(0)
    slots, tile, _ = q_ref.shape
    rows = slots * tile
    width = 512

    @pl.when(step == 0)
    def _():
        spread_keyval(place_ref[2, 0], kv_refs, key_ref, plain_ref)
        value_ref[:, :LANES] = plain_ref[...]
        value_ref[:, LANES:] = jnp.ones((value_ref.shape[0], LANES), BF16)
        keys = key_ref[...].astype(F32)
        bound_ref[0] = jnp.max(jnp.sum(keys * keys, -1, keepdims=True)) * 0.5
        bound_ref[1] = jnp.max(jnp.abs(plain_ref[...].astype(F32)))

    here = place_ref[0, step]
    lower = pl.multiple_of(place_ref[1, step], width)
    q = q_ref[...].reshape(rows, LANES)
    qf = q.astype(F32)
    longest = jnp.max(jnp.sum(qf * qf, -1, keepdims=True))
    plain = (longest * bound_ref[0] <= (SAFE_SCORE / SCALE) ** 2) & (bound_ref[1] <= SAFE_VALUE)
    full = (here - lower) // width
    last = pl.multiple_of(lower + full * width, width)
    token = lax.broadcasted_iota(jnp.int32, (tile, width), 0) + here
    allowed = (lax.broadcasted_iota(jnp.int32, (tile, width), 1) + last) <= token
    allowed = jnp.broadcast_to(allowed[None], (slots, tile, width)).reshape(rows, width)

    def finish(out, logs):
        o_ref[...] = out.astype(o_ref.dtype).reshape(slots, tile, LANES)
        logs = logs.reshape(slots, tile, LANES)
        lane = lane_index(tile)
        packed = jnp.zeros((tile, LANES), F32)
        for slot in range(slots):
            packed = jnp.where(lane == slot, logs[slot], packed)
        log_ref[...] = packed

    pairs = full // 2

    @pl.when(plain)
    def _():
        for count, edge_width in ((0, width // 2), (0, width), (1, width // 2), (1, width)):

            @pl.when((full % 2 == count) & ((here - last >= width // 2) == (edge_width == width)))
            def _(count=count, edge_width=edge_width):
                inner = count * width
                span = pl.ds(pl.multiple_of(lower + pairs * 2 * width, width), inner + edge_width)
                expo = jnp.exp2(dot_last(q, key_ref[span, :]) * (SCALE * LOG2E))
                edge = jnp.where(allowed[:, :edge_width], expo[:, inner:], 0.0).astype(BF16)
                expo = jnp.concatenate([expo[:, :inner].astype(BF16), edge], 1) if count else edge
                acc_ref[...] = dot(expo, value_ref[span, :])

        def body(index, carry):
            span = pl.ds(pl.multiple_of(lower + index * 2 * width, width), 2 * width)
            expo = jnp.exp2(dot_last(q, key_ref[span, :]) * (SCALE * LOG2E)).astype(BF16)
            acc_ref[...] += dot(expo, value_ref[span, :])
            return carry

        lax.fori_loop(0, pairs, body, 0)
        total = acc_ref[:, LANES:]
        finish(acc_ref[:, :LANES] / total, jnp.log2(total))

    @pl.when(jnp.logical_not(plain))
    def _():
        def scaled(span):
            return dot_last(q, key_ref[span, :]) * (SCALE * LOG2E)

        scores = jnp.where(allowed, scaled(pl.ds(last, width)), MASKED)
        peak = jnp.max(scores, -1, keepdims=True)
        peak_ref[...] = jnp.broadcast_to(peak, (rows, LANES))
        acc_ref[...] = dot(jnp.exp2(scores - peak).astype(BF16), value_ref[pl.ds(last, width), :])

        def body(index, carry):
            span = pl.ds(pl.multiple_of(lower + index * width, width), width)
            scores = scaled(span)
            before = peak_ref[:, :1]
            peak = jnp.maximum(before, jnp.max(scores, -1, keepdims=True))
            peak_ref[...] = jnp.broadcast_to(peak, (rows, LANES))
            expo = jnp.exp2(scores - peak).astype(BF16)
            acc_ref[...] = acc_ref[...] * jnp.exp2(before - peak) + dot(expo, value_ref[span, :])
            return carry

        lax.fori_loop(0, full, body, 0)
        total = acc_ref[:, LANES:]
        finish(acc_ref[:, :LANES] / total, peak_ref[...] + jnp.log2(total))


def attend_call(place, q, kv, tile=128):
    slots, rows, _ = q.shape
    count = len(kv) * kv[0].shape[0] * kv[0].shape[1]
    return pl.pallas_call(
        attend_kernel,
        grid_spec=pltpu.PrefetchScalarGridSpec(
            num_scalar_prefetch=1,
            grid=(rows // tile,),
            in_specs=[
                pl.BlockSpec((slots, tile, LANES), lambda i, s: (0, i, 0)),
                *[pl.BlockSpec(part.shape, lambda i, s: (0, 0, 0)) for part in kv],
            ],
            out_specs=[
                pl.BlockSpec((slots, tile, LANES), lambda i, s: (0, i, 0)),
                pl.BlockSpec((tile, LANES), lambda i, s: (i, 0)),
                pl.BlockSpec((count, LANES), lambda i, s: (0, 0)),
                pl.BlockSpec((count, LANES), lambda i, s: (0, 0)),
            ],
            scratch_shapes=[
                pltpu.VMEM((count, 2 * LANES), BF16),
                pltpu.VMEM((slots * tile, 2 * LANES), F32),
                pltpu.VMEM((slots * tile, LANES), F32),
                pltpu.SMEM((2,), F32),
            ],
        ),
        out_shape=[
            jax.ShapeDtypeStruct((slots, rows, LANES), BF16),
            jax.ShapeDtypeStruct((rows, LANES), F32),
            jax.ShapeDtypeStruct((count, LANES), BF16),
            jax.ShapeDtypeStruct((count, LANES), BF16),
        ],
        compiler_params=pltpu.CompilerParams(vmem_limit_bytes=24 << 20),
        cost_estimate=pl.CostEstimate(
            flops=8 * slots * rows * count * LANES, bytes_accessed=8 * slots * rows * LANES, transcendentals=0
        ),
        name="attend",
    )(place, q, *kv)


def attend_back_kernel(first, final, tile_of, groups, before, *refs):
    refs = list(refs)
    take = lambda count: [refs.pop(0) for _ in range(count)]
    place_ref, q_ref, do_ref, log_ref, delta_ref, routes_ref, key_ref, value_ref = take(8)
    if not first:
        (sums_in,) = take(1)
    if final:
        (h_ref,) = take(1)
        before_refs = take(before)
    (all_ref,) = take(1)
    outs = take(4 if final else 1)
    dq_ref, dkey_ref, dvalue_ref, sems = take(4)
    step = pl.program_id(0)
    steps = pl.num_programs(0)
    slots, tile, _ = q_ref.shape
    rows = slots * tile
    width = 512

    def carry_copies():
        return [
            pltpu.make_async_copy(sums_in.at[0], dkey_ref.at[pl.ds(0, HD), :], sems.at[0]),
            pltpu.make_async_copy(sums_in.at[1], dvalue_ref.at[pl.ds(0, HD), :], sems.at[1]),
        ]

    @pl.when(step == 0)
    def _():
        if first:
            dkey_ref[:HD] = jnp.zeros_like(dkey_ref[:HD])
            dvalue_ref[:HD] = jnp.zeros_like(dvalue_ref[:HD])
        else:
            for copy in carry_copies():
                copy.start()
        dkey_ref[HD:] = jnp.zeros_like(dkey_ref[HD:])
        dvalue_ref[HD:] = jnp.zeros_like(dvalue_ref[HD:])

    here = place_ref[0, tile_of(step)]
    lower = place_ref[1, tile_of(step)]
    q = q_ref[...].reshape(rows, LANES)
    do = do_ref[...].reshape(rows, LANES)
    logs = log_ref[...]
    deltas = delta_ref[...]
    logs = jnp.concatenate([column(logs, slot, tile) for slot in range(slots)], 0)
    deltas = jnp.concatenate([column(deltas, slot, tile) for slot in range(slots)], 0)
    full = (here - lower) // width
    last = pl.multiple_of(lower + full * width, width)
    token = lax.broadcasted_iota(jnp.int32, (tile, width), 0) + here
    allowed = (lax.broadcasted_iota(jnp.int32, (tile, width), 1) + last) <= token
    allowed = jnp.broadcast_to(allowed[None], (slots, tile, width)).reshape(rows, width)

    if not first:

        @pl.when(step == 0)
        def _():
            for copy in carry_copies():
                copy.wait()

    def one(start, size, masked):
        wide = lambda values: jnp.concatenate([values] * (size // LANES), 1)
        span = pl.ds(start, size)
        keys = key_ref[span, :]
        scores = dot_last(q, keys)
        probs = jnp.exp2(scores * (SCALE * LOG2E) - wide(logs))
        if masked:
            probs = jnp.where(allowed[:, :size], probs, 0.0)
        dprobs = dot_last(do, value_ref[span, :])
        dscores = (probs * (dprobs - wide(deltas))).astype(BF16)
        dvalue_ref[:, span] += dot_first(do, probs.astype(BF16))
        dkey_ref[:, span] += dot_first(q, dscores)
        return dot(dscores, keys)

    for size in (width // 2, width):

        @pl.when((here - last >= width // 2) == (size == width))
        def _(size=size):
            dq_ref[...] = one(last, size, True)

    def body(index, carry):
        dq_ref[...] += one(pl.multiple_of(lower + index * width, width), width, False)
        return carry

    lax.fori_loop(0, full, body, 0)

    def sum_copies():
        return [
            pltpu.make_async_copy(dkey_ref.at[pl.ds(0, HD), :], outs[0].at[0], sems.at[0]),
            pltpu.make_async_copy(dvalue_ref.at[pl.ds(0, HD), :], outs[0].at[1], sems.at[1]),
        ]

    if not final:

        @pl.when(step == steps - 1)
        def _():
            dkey_ref[:HD] += dkey_ref[HD:]
            dvalue_ref[:HD] += dvalue_ref[HD:]
            for copy in sum_copies():
                copy.start()

    dq = (dq_ref[...] * SCALE).astype(BF16).reshape(slots, tile, LANES)
    mine = pl.ds(pl.multiple_of(step * tile, tile), tile)
    all_ref[mine, :] = place_pairs([dq[slot] for slot in range(slots)], choices(routes_ref[...], tile, BF16))

    @pl.when(step == steps - 1)
    def _():
        if not final:
            for copy in sum_copies():
                copy.wait()
            return
        kv_keep, kv_send, gq_keep, gq_send = outs
        _, _, block, _ = kv_keep.shape
        device = place_ref[2, 0]
        for index in range(4):
            target = kv_send if index % 2 else kv_keep
            for high in range(2):
                span = block_of(device ^ index, high, 4, block)
                dkeys = (dkey_ref[:HD, span] + dkey_ref[HD:, span]) * SCALE
                dvalues = dvalue_ref[:HD, span] + dvalue_ref[HD:, span]
                target[index // 2, high] = jnp.concatenate([dkeys, dvalues], 0).T.astype(BF16)
        gq = dot_first(h_ref[...], in_rows([*before_refs, all_ref]))
        if groups == 8:
            scatter_rows(gq, gq_keep, gq_send, device % 2)
        else:
            gq_keep[...] = gq.astype(BF16)
            gq_send[...] = jnp.zeros_like(gq_send)


def in_rows(parts):
    half = lambda part: part.shape[0] // 2
    return jnp.concatenate([part[: half(part)] for part in parts] + [part[half(part) :] for part in parts], 0)


def scatter_rows(grad, keep, send, core):
    for x in range(2):
        for y in range(2):
            for z in range(4):
                base = (((z * 2 + y) * 2 + x) * 2) * 16
                low = grad[base : base + 16].astype(BF16)
                high = grad[base + 16 : base + 32].astype(BF16)
                keep[y, z, x] = jnp.where(core == 0, low, high)
                send[y, z, x] = jnp.where(core == 0, high, low)


def attend_back_call(start, count, tiles, groups, where, q, do, logs, deltas, routes, keys, values, carried, h, before):
    slots, rows, _ = q.shape
    length = keys.shape[0]
    width = h.shape[1]
    tile = rows // (2 * tiles)
    first, final = start == 0, start + count == tiles

    def tile_of(step):
        return jnp.where(step < count, start + step, tiles + start + step - count)

    whole = lambda shape: pl.BlockSpec(shape, lambda i, s: (0,) * len(shape))
    anywhere = pl.BlockSpec(memory_space=pl.ANY)
    by_slot = pl.BlockSpec((slots, tile, LANES), lambda i, s: (0, tile_of(i), 0))
    by_row = lambda cols: pl.BlockSpec((tile, cols), lambda i, s: (tile_of(i), 0))
    in_specs = [
        by_slot, by_slot, by_row(LANES), by_row(LANES), by_row(TOPK), whole(keys.shape), whole(values.shape),
    ]
    in_specs += [anywhere] * len(carried)
    extra = [h, *before] if final else []
    in_specs += [whole(array.shape) for array in extra]
    out_specs = [whole((2 * count * tile, SPAN))]
    out_shape = [jax.ShapeDtypeStruct((2 * count * tile, SPAN), BF16)]
    if final:
        kv_shape = (2, 2, rows // 2, LANES)
        gq_shape = (2, 4, 2, 16, SPAN) if groups == 8 else (width, SPAN)
        off_shape = gq_shape if groups == 8 else (8, LANES)
        for shape in (kv_shape, kv_shape, gq_shape, off_shape):
            out_specs.append(whole(shape))
            out_shape.append(jax.ShapeDtypeStruct(shape, BF16))
    else:
        out_specs.append(anywhere)
        out_shape.append(jax.ShapeDtypeStruct((2, HD, length), F32))
    return pl.pallas_call(
        functools.partial(attend_back_kernel, first, final, tile_of, groups, len(before)),
        grid_spec=pltpu.PrefetchScalarGridSpec(
            num_scalar_prefetch=1,
            grid=(2 * count,),
            in_specs=in_specs,
            out_specs=out_specs,
            scratch_shapes=[
                pltpu.VMEM((slots * tile, LANES), F32),
                pltpu.VMEM((LANES, length), F32),
                pltpu.VMEM((LANES, length), F32),
                pltpu.SemaphoreType.DMA((2,)),
            ],
        ),
        out_shape=out_shape,
        compiler_params=pltpu.CompilerParams(vmem_limit_bytes=20 << 20),
        cost_estimate=pl.CostEstimate(
            flops=10 * slots * 2 * count * tile * length * LANES, bytes_accessed=16 * slots * tile * LANES, transcendentals=0
        ),
        name="attend_back",
    )(where, q, do, logs, deltas, routes, keys, values, *carried, *extra)


def query_back_kernel(dlog_ref, wq_ref, wr_ref, *refs):
    *all_refs, dh_ref = refs
    rows = in_rows(all_refs)
    dh_ref[...] = dot_last(rows, wq_ref[...]) + dot_last(dlog_ref[...], wr_ref[...])


def query_back_call(dlogits, wq, wk, parts):
    rows = dlogits.shape[0]
    width = wq.shape[0]
    cols = lambda size, index: pl.BlockSpec((width, size), lambda i: (0, index))
    whole = lambda shape: pl.BlockSpec(shape, lambda i: (0,) * len(shape))
    return pl.pallas_call(
        query_back_kernel,
        grid=(1,),
        in_specs=[
            whole(dlogits.shape), cols(SPAN, 0), cols(LANES, 1), *[whole(part.shape) for part in parts],
        ],
        out_specs=whole((rows, width)),
        out_shape=jax.ShapeDtypeStruct((rows, width), F32),
        compiler_params=pltpu.CompilerParams(vmem_limit_bytes=24 << 20),
        cost_estimate=pl.CostEstimate(
            flops=6 * rows * width * (SPAN + LANES), bytes_accessed=4 * rows * (SPAN + width), transcendentals=0
        ),
        name="query_back",
    )(dlogits, wq, wk, *parts)


def middle_kernel(groups, *refs):
    refs = list(refs)
    take = lambda count: [refs.pop(0) for _ in range(count)]
    core_ref, x_hbm, dy_hbm, o_hbm, gate_ref, routes_ref, tail_ref = take(7)
    weights_in = take(8 if groups == 8 else 3)
    out_hbm, ring_hbm, swap_hbm, dmid_hbm, do_hbm, delta_ref, dlog_ref, gain_ref = take(8)
    outs_hbm = take(4 if groups == 8 else 3)
    x_ref, dy_ref, o_ref, comb_ref, mid_ref, normal_ref, acc_ref, dh_ref, dcomb_ref, out_ref, do_ref = take(11)
    wo_in, w1_in, w2_in = take(3)
    in_sems, out_sems = take(2)
    outs = refs
    rows, width = x_ref.shape
    part = 256
    cols = 512
    count = [0]

    def copy(source, target):
        count[0] += 1
        return pltpu.make_async_copy(source, target, in_sems.at[count[0] - 1])

    slot_copies = [copy(o_hbm.at[slot], o_ref.at[slot]) for slot in range(TOPK)]
    x_copy, dy_copy = copy(x_hbm, x_ref), copy(dy_hbm, dy_ref)
    if groups == 8:
        flat = core_ref[0]
        my_x, my_y, core = flat // 2 % 2, flat // 4 % 2, flat % 2
        wo_copies, w1_copies, w2_copies = [], [], []
        for index in range(8):
            other_core, other = index // 4, index % 4
            for y_turn in range(2):
                y = my_y ^ y_turn
                part_a = weights_in[4 * other_core + (other // 2)]
                x = my_x ^ (other // 2)
                mp = 2 * x + (core ^ other_core)
                across = pl.ds(pl.multiple_of(mp * cols, cols), cols)
                if other % 2 == 0:
                    wo_copies.append(copy(part_a.at[y_turn, :, 4:6], wo_in.at[:, y, mp, 0:2]))
                    w1_copies.append(copy(part_a.at[y_turn, :, 0:4], w1_in.at[:, y, :, :, across]))
                else:
                    part_b = weights_in[4 * other_core + 2 + y_turn]
                    x_turn = other // 2
                    wo_copies.append(copy(part_b.at[x_turn, :, 4:5], wo_in.at[:, y, mp, 2:3]))
                    w2_copies.append(copy(part_b.at[x_turn, :, 0:4], w2_in.at[:, y, :, :, across]))
    else:
        wo_copies, w1_copies, w2_copies = [
            [copy(source, target)] for source, target in zip(weights_in, (wo_in, w1_in, w2_in))
        ]
    for one in (*slot_copies, *wo_copies, x_copy, *w1_copies, dy_copy, *w2_copies):
        one.start()
    view = lambda ref: ref[...].reshape(width, -1)
    third = lambda ref, index: ref[:, :, :, index].reshape(width, cols)

    gain = gains_of(tail_ref[...])[E + 1 : E + 2]
    for one in slot_copies:
        one.wait()

    def combine(index, carry):
        mine = pl.ds(pl.multiple_of(index * part, part), part)
        gates = gate_ref[mine, :]
        weighted = [(column(gates, slot, part) * o_ref[slot, mine, :].astype(F32)).astype(BF16) for slot in range(TOPK)]
        comb_ref[mine, :] = place_pairs(weighted, choices(routes_ref[mine, :], part, BF16))
        return carry

    lax.fori_loop(0, rows // part, combine, 0)
    for one in (*wo_copies, x_copy):
        one.wait()
    mid = x_ref[...].astype(F32)
    if groups == 8:
        for index in range(3):
            mid = mid + dot_last(comb_ref[:, index * cols : (index + 1) * cols], third(wo_in, index))
    else:
        mid = mid + dot_last(comb_ref[...], wo_in[...])
    mid_ref[...] = mid
    normal, factor = standardize(mid)
    normal_ref[...] = normal
    h2 = (normal * gain).astype(BF16)
    for one in (*w1_copies, dy_copy, *w2_copies):
        one.wait()
    dy = dy_ref[...]
    w1, w2 = view(w1_in), view(w2_in)

    for index in range(w1.shape[1] // cols):
        span = slice(index * cols, (index + 1) * cols)
        up, down = w1[:, span], w2[:, span]
        pre = dot(h2, up)
        dact = dot(dy, down)
        sigma = jax.nn.sigmoid(pre)
        act = (pre * sigma).astype(BF16)
        dpre = (dact * (sigma * (1.0 + pre * (1.0 - sigma)))).astype(BF16)
        branch = dot_last(act, down)
        dh2 = dot_last(dpre, up)
        if index == 0:
            acc_ref[...] = branch
            dh_ref[...] = dh2
        else:
            acc_ref[...] += branch
            dh_ref[...] += dh2
        g1 = dot_first(h2, dpre).astype(BF16)
        g2 = dot_first(dy, act).astype(BF16)
        if groups != 8:
            outs[0][:, span] = g1
            outs[1][:, span] = g2
            continue
        for mine, (a, b) in ((True, (outs[0], outs[2])), (False, (outs[1], outs[3]))):

            @pl.when((core_ref[0] % 2 == index % 2) == mine)
            def _(a=a, b=b, g1=g1, g2=g2, x=index // 2):
                for owner in range(8):
                    piece = slice(owner * 64, owner * 64 + 64)
                    a[x, owner % 2, owner // 2, :64] = g1[piece]
                    b[owner % 2, x, owner // 2, :64] = g2[piece]

    out_ref[...] = (mid_ref[...] + acc_ref[...]).astype(BF16)
    out_copy = pltpu.make_async_copy(out_ref, out_hbm, out_sems.at[0])
    out_copy.start()
    half = rows // 2
    sends = [
        pltpu.make_async_copy(
            out_ref.at[pl.ds(pl.multiple_of(core_ref[1 + index], half), half), :], target, out_sems.at[7 + index]
        )
        for index, target in enumerate((ring_hbm, swap_hbm))
    ]
    for one in sends:
        one.start()
    dh2 = dh_ref[...]
    normal = normal_ref[...]
    gain_ref[...] = jnp.sum(dh2 * normal, 0, keepdims=True)
    dmid = dy.astype(F32) + norm_back(dh2 * gain, normal, factor)
    mid_ref[...] = dmid
    dmid_copy = pltpu.make_async_copy(mid_ref, dmid_hbm, out_sems.at[1])
    dmid_copy.start()
    dmid_b = dmid.astype(BF16)
    if groups == 8:
        for index in range(3):
            span = slice(index * cols, (index + 1) * cols)
            dcomb_ref[:, span] = dot(dmid_b, third(wo_in, index)).astype(BF16)
    else:
        dcomb_ref[...] = dot(dmid_b, wo_in[...]).astype(BF16)
    go = dot_first(dmid_b, comb_ref[...]).astype(BF16)
    if groups == 8:
        for core in range(2):

            @pl.when(core_ref[0] % 2 == core)
            def _(pairs=((outs[0], outs[2]), (outs[1], outs[3])), core=core):
                for owner in range(32):
                    z, y, x, c = owner // 8, owner // 4 % 2, owner // 2 % 2, owner % 2
                    a, b = pairs[c ^ core]
                    mine = slice(owner * 16, owner * 16 + 16)
                    a[x, y, z, 64:80] = go[mine, :512]
                    a[x, y, z, 80:] = go[mine, 512:1024]
                    b[y, x, z, 64:] = go[mine, 1024:]
    else:
        outs[2][...] = go

    grad_copies = [
        pltpu.make_async_copy(source, target, out_sems.at[3 + index])
        for index, (source, target) in enumerate(zip(outs, outs_hbm))
    ]
    for one in grad_copies:
        one.start()

    def spread(index, carry):
        mine = pl.ds(pl.multiple_of(index * part, part), part)
        gates = gate_ref[mine, :]
        routes = routes_ref[mine, :]
        lane = lane_index(part)
        dcomb = dcomb_ref[mine, :]
        gate_grads = jnp.zeros((part, LANES), F32)
        for slot, choice in enumerate(choices(routes, part, BF16)):
            picked = pick_pairs(dcomb, choice).astype(F32)
            do_ref[slot, mine, :] = (column(gates, slot, part) * picked).astype(BF16)
            total = jnp.sum(o_ref[slot, mine, :].astype(F32) * picked, -1, keepdims=True)
            gate_grads = jnp.where(lane == slot, total, gate_grads)
        weighted = gates * gate_grads
        delta_ref[mine, :] = weighted
        dsel = weighted - gates * jnp.sum(weighted, -1, keepdims=True)
        dlogits = jnp.zeros((part, LANES), F32)
        for slot in range(TOPK):
            dlogits = jnp.where(lane == column(routes, slot, part), column(dsel, slot, part), dlogits)
        dlog_ref[mine, :] = dlogits.astype(BF16)
        return carry

    lax.fori_loop(0, rows // part, spread, 0)
    do_copy = pltpu.make_async_copy(do_ref, do_hbm, out_sems.at[2])
    do_copy.start()
    for one in (out_copy, *sends, dmid_copy, do_copy, *grad_copies):
        one.wait()


def middle_call(groups, core, x, dy, o, gates, routes, front, weights):
    rows, width = x.shape
    hidden = 2048
    whole = lambda shape: pl.BlockSpec(shape, lambda i, s: (0,) * len(shape))
    anywhere = pl.BlockSpec(memory_space=pl.ANY)
    if groups == 8:
        grads = [(2, 2, 4, 96, 512), (2, 2, 4, 96, 512), (2, 2, 4, 80, 512), (2, 2, 4, 80, 512)]
        held = [(4, 2, 4, 3, 16, 512), (4, 2, 4, 16, hidden), (4, 2, 4, 16, hidden)]
    else:
        grads = [(width, hidden), (width, hidden), (width, SPAN)]
        held = [(width, SPAN), (width, hidden), (width, hidden)]
    return pl.pallas_call(
        functools.partial(middle_kernel, groups),
        grid_spec=pltpu.PrefetchScalarGridSpec(
            num_scalar_prefetch=1,
            grid=(1,),
            in_specs=[
                anywhere, anywhere, anywhere, whole(gates.shape), whole(routes.shape),
                pl.BlockSpec((width, LANES), lambda i, s: (0, 1)), *[anywhere] * len(weights),
            ],
            out_specs=[
                *[anywhere] * 5, whole((rows, LANES)), whole((rows, LANES)), whole((1, width)),
                *[anywhere] * len(grads),
            ],
            scratch_shapes=[
                pltpu.VMEM((rows, width), BF16),
                pltpu.VMEM((rows, width), BF16),
                pltpu.VMEM((TOPK, rows, LANES), BF16),
                pltpu.VMEM((rows, SPAN), BF16),
                pltpu.VMEM((rows, width), F32),
                pltpu.VMEM((rows, width), F32),
                pltpu.VMEM((rows, width), F32),
                pltpu.VMEM((rows, width), F32),
                pltpu.VMEM((rows, SPAN), BF16),
                pltpu.VMEM((rows, width), BF16),
                pltpu.VMEM((TOPK, rows, LANES), BF16),
                *[pltpu.VMEM(shape, BF16) for shape in held],
                pltpu.SemaphoreType.DMA((42,)),
                pltpu.SemaphoreType.DMA((9,)),
                *[pltpu.VMEM(shape, BF16) for shape in grads],
            ],
        ),
        out_shape=[
            jax.ShapeDtypeStruct((rows, width), BF16),
            jax.ShapeDtypeStruct((rows // 2, width), BF16),
            jax.ShapeDtypeStruct((rows // 2, width), BF16),
            jax.ShapeDtypeStruct((rows, width), F32),
            jax.ShapeDtypeStruct((TOPK, rows, LANES), BF16),
            jax.ShapeDtypeStruct((rows, LANES), F32),
            jax.ShapeDtypeStruct((rows, LANES), BF16),
            jax.ShapeDtypeStruct((1, width), F32),
            *[jax.ShapeDtypeStruct(shape, BF16) for shape in grads],
        ],
        compiler_params=pltpu.CompilerParams(vmem_limit_bytes=(45 if groups == 8 else 56) << 20),
        cost_estimate=pl.CostEstimate(
            flops=2 * rows * width * (6 * hidden + 3 * SPAN), bytes_accessed=16 * rows * width, transcendentals=0
        ),
        name="middle",
    )(core, x, dy, o, gates, routes, front, *weights)


def post_kernel(x_ref, h_ref, dmid_ref, dh_ref, keep_ref, recv_ref, dlog_ref, gain2_ref, w_ref, grad_ref, gk_ref, sum_ref):
    step = pl.program_id(0)
    gain = gains_of(w_ref[:, LANES:])[E : E + 1]
    normal, factor = standardize(x_ref[...].astype(F32))
    dkv = (keep_ref[...].astype(F32) + recv_ref[...].astype(F32)).astype(BF16)
    dh = dh_ref[...] + dot_last(dkv, w_ref[:, :LANES])
    grad_ref[...] = (dmid_ref[...] + norm_back(dh * gain, normal, factor)).astype(grad_ref.dtype)
    gain1 = jnp.sum(dh * normal, 0, keepdims=True)
    width = gain1.shape[1]
    row = lax.broadcasted_iota(jnp.int32, (LANES, width), 0)
    gain2 = jnp.where(step == 0, gain2_ref[...], 0.0)
    gains = jnp.where(row == E, gain1, jnp.where(row == E + 1, gain2, 0.0))
    h_turned = turned(h_ref[...])
    keyval = dot(h_turned, dkv)
    router = dot(h_turned, dlog_ref[...]) + gains.T

    @pl.when(step == 0)
    def _():
        sum_ref[:, :LANES] = keyval
        sum_ref[:, LANES:] = router

    @pl.when(step > 0)
    def _():
        sum_ref[:, :LANES] += keyval
        sum_ref[:, LANES:] += router

    @pl.when(step == pl.num_programs(0) - 1)
    def _():
        gk_ref[...] = sum_ref[...].astype(BF16)


def post_call(x, h, dmid, dh, keep, recv, dlogits, gain2, weights, tile=256):
    rows, width = x.shape
    by_row = lambda cols: pl.BlockSpec((tile, cols), lambda i: (i, 0))
    return pl.pallas_call(
        post_kernel,
        grid=(rows // tile,),
        in_specs=[
            by_row(width), by_row(width), by_row(width), by_row(width), by_row(LANES), by_row(LANES), by_row(LANES),
            pl.BlockSpec((1, width), lambda i: (0, 0)),
            pl.BlockSpec((width, 2 * LANES), lambda i: (0, 0)),
        ],
        out_specs=[by_row(width), pl.BlockSpec((width, 2 * LANES), lambda i: (0, 0))],
        out_shape=[
            jax.ShapeDtypeStruct((rows, width), BF16),
            jax.ShapeDtypeStruct((width, 2 * LANES), BF16),
        ],
        scratch_shapes=[pltpu.VMEM((width, 2 * LANES), F32)],
        compiler_params=pltpu.CompilerParams(vmem_limit_bytes=16 << 20),
        cost_estimate=pl.CostEstimate(
            flops=60 * rows * width * LANES, bytes_accessed=16 * rows * width, transcendentals=0
        ),
        name="finish",
    )(x, h, dmid, dh, keep, recv, dlogits, gain2, weights)


RING = ((0, 1), (1, 2), (2, 3), (3, 0))
SWAP = ((1, 3), (3, 1))


def halves(rows, place):
    half = rows.shape[0] // 2
    outer = (place == 0) | (place == 3)
    first = lax.dynamic_slice_in_dim(rows, jnp.where(outer, half, 0), half, 0)
    second = lax.dynamic_slice_in_dim(rows, jnp.where(place == 1, half, 0), half, 0)
    return first, second


def deal(rows, sent, place, ready=None):
    half = rows.shape[0] // 2
    ring = lax.ppermute(sent[0], "mp", RING)
    swap = lax.ppermute(sent[1], "mp", SWAP)
    if ready is not None:
        ring, swap = after((ring, swap), ready)
    low = jnp.where(place == 0, rows[:half], jnp.where(place == 3, swap, ring))
    high = jnp.where(place == 2, rows[half:], jnp.where(place == 1, swap, ring))
    return jnp.concatenate([low, high], 0)


def send_back(sent):
    first, second = sent
    ring = lax.ppermute(first, "mp", tuple((b, a) for a, b in RING))
    return ring, lax.ppermute(second, "mp", SWAP)


def put_back(rows, returned, place):
    half = rows.shape[0] // 2
    ring, swap = returned
    top = jnp.where(place == 0, rows[:half], jnp.where(place == 3, swap, ring))
    bottom = jnp.where(place == 2, rows[half:], jnp.where(place == 1, swap, ring))
    return jnp.concatenate([top, bottom], 0)


OTHER_CORE = ((0, 1), (1, 0), (2, 3), (3, 2))
OTHER_X = ((0, 2), (2, 0), (1, 3), (3, 1))


def swap_core(values):
    return lax.ppermute(values, "mp", OTHER_CORE)


def swap_x(values):
    return lax.ppermute(values, "mp", OTHER_X)


def swap_y(values):
    return lax.ppermute(values, "dp", tuple((i, i ^ 1) for i in range(8)))


def swap_z(values, turn):
    return lax.ppermute(values, "dp", tuple((i, i ^ (2 * turn)) for i in range(8)))


def at(values, index):
    return lax.dynamic_index_in_dim(values, index, 0, keepdims=False)


def added(left, right):
    return (left.astype(F32) + right.astype(F32)).astype(BF16)


def gather_z(shard, my_z):
    turns = [shard] + [swap_z(shard, turn) for turn in (1, 2, 3)]
    rows = []
    for z in range(4):
        row = turns[3]
        for turn in (2, 1, 0):
            row = jnp.where(my_z == z ^ turn, turns[turn], row)
        rows.append(row)
    return jnp.stack(rows)


def after(values, others):
    return lax.optimization_barrier((values, others))[0]


def tied(first, second):
    return lax.optimization_barrier((first, second))


def adam_step(param, first, second, grad, rate, decay):
    first_new = BETA_FIRST * first + (1.0 - BETA_FIRST) * grad
    second_new = BETA_SECOND * second + (1.0 - BETA_SECOND) * grad * grad
    first_hat = first_new / (1.0 - BETA_FIRST**ADAM_STEP)
    second_hat = second_new / (1.0 - BETA_SECOND**ADAM_STEP)
    param_new = param - rate * (first_hat / (jnp.sqrt(second_hat) + ADAM_EPS) + decay * param)
    return (second_new, param_new)


def update_kernel(
    rates_ref, squares_ref, gq_ref, go_ref, gk_ref, ffn_ref,
    ap_ref, am_ref, av_ref, fp_ref, fm_ref, fv_ref,
    ag_ref, avn_ref, apn_ref, fg_ref, fvn_ref, fpn_ref, norm_ref, gain_ref,
):
    norm = jnp.sqrt(jnp.sum(jnp.sum(squares_ref[...], 0), keepdims=True))
    norm_ref[...] = norm
    factor = jnp.minimum(1.0, CLIP_NORM / norm)
    tail = AC - 2 * SPAN
    for source, span, rate in (
        (gq_ref, slice(0, SPAN), rates_ref[0]),
        (go_ref, slice(SPAN, 2 * SPAN), rates_ref[1]),
        (gk_ref, slice(2 * SPAN, AC), None),
    ):
        decay = WEIGHT_DECAY
        grad = source[...] * factor
        if rate is None:
            grad = grad[:, :tail]
            place = lax.broadcasted_iota(jnp.int32, (1, tail), 1)
            rate = jnp.where(
                place < 2 * HD, rates_ref[2], jnp.where(place < 2 * HD + E, rates_ref[3], rates_ref[4])
            )
            decay = jnp.where(place < 2 * HD + E, WEIGHT_DECAY, 0.0)
            gain_ref[...] = grad[:, tail - 2 :]
        ag_ref[:, span] = grad
        avn_ref[:, span], apn_ref[:, span] = adam_step(
            ap_ref[:, span], am_ref[:, span], av_ref[:, span], grad, rate, decay
        )
    for index in range(2):
        grad = ffn_ref[index] * factor
        fg_ref[index] = grad
        fvn_ref[index], fpn_ref[index] = adam_step(
            fp_ref[index], fm_ref[index], fv_ref[index], grad, rates_ref[5 + index], WEIGHT_DECAY
        )


def squares_kernel(gq_ref, go_ref, ffn_ref, gk_ref, sums_ref, gk_out_ref):
    gk = jnp.sum(gk_ref[...].astype(F32), 0)
    gk_out_ref[...] = gk
    total = jnp.zeros((8, LANES), F32)
    for part in (gq_ref[...], go_ref[...], gk, ffn_ref[...].reshape(-1, ffn_ref.shape[-1])):
        square = part * part
        for row in range(0, square.shape[0], 8):
            for col in range(0, square.shape[1], LANES):
                total = total + square[row : row + 8, col : col + LANES]
    sums_ref[...] = jnp.broadcast_to(total[None], sums_ref.shape)


def squares_call(gq, go, ffn, gk):
    return pl.pallas_call(
        squares_kernel,
        out_shape=[
            jax.ShapeDtypeStruct((gk.shape[0], 8, LANES), F32),
            jax.ShapeDtypeStruct(gk.shape[1:], F32),
        ],
        compiler_params=pltpu.CompilerParams(vmem_limit_bytes=8 << 20),
        name="squares",
    )(gq, go, ffn, gk)


def update_call(rates, squares, gq, go, gk, ffn, attn, ffn_state):
    rows = gq.shape[0]
    attn_shape = jax.ShapeDtypeStruct(attn[0].shape, F32)
    ffn_shape = jax.ShapeDtypeStruct(ffn.shape, F32)
    whole = pl.BlockSpec(memory_space=pltpu.VMEM)
    return pl.pallas_call(
        update_kernel,
        in_specs=[pl.BlockSpec(memory_space=pltpu.SMEM)] + [whole] * 11,
        out_specs=[whole] * 8,
        out_shape=[
            attn_shape, attn_shape, attn_shape, ffn_shape, ffn_shape, ffn_shape,
            jax.ShapeDtypeStruct((1, 1), F32), jax.ShapeDtypeStruct((rows, 2), F32),
        ],
        compiler_params=pltpu.CompilerParams(vmem_limit_bytes=24 << 20),
        name="update",
    )(rates, squares, gq, go, gk, ffn, *attn, *ffn_state)


ALL = ("dp", "mp")


def shards(
    tokens, cotangent, routes, starts, attn_param, attn_first, attn_second, ffn_param, ffn_first, ffn_second, rates
):
    local_rows, width = tokens.shape
    place = lax.axis_index("mp")
    devices = lax.axis_size("mp")
    groups = lax.axis_size("dp")
    block = local_rows // 2
    manual = groups == 8
    _, depth, cols = ffn_param.shape
    my_x, my_y, my_z = place // 2, lax.axis_index("dp") % 2, lax.axis_index("dp") // 2
    flat = (lax.axis_index("dp") * devices + place).astype(jnp.int32)

    marks = jnp.concatenate([routes, starts[:, None] // block], 1).astype(BF16)
    marks = jnp.pad(marks, ((0, 0), (0, 16 - TOPK - 1))).T
    dealt = [tokens[:block], marks[:, :block], tokens[block:], marks[:, block:]]
    dealt = jnp.concatenate([part.reshape(-1, width) for part in dealt], 0)
    extra = dealt.shape[0] // 2 - block
    sent = halves(dealt, place)
    dealt = deal(dealt, sent, place)
    x = jnp.concatenate([dealt[:block], dealt[block + extra : 2 * block + extra]], 0)
    marks = [dealt[block : block + extra], dealt[2 * block + extra :]]
    marks = jnp.concatenate([part.reshape(16, block) for part in marks], 1).T[:, : TOPK + 1].astype(jnp.int32)

    attn_b = attn_param.astype(BF16)
    ffn_b = ffn_param.astype(BF16)
    pad = jnp.zeros((attn_b.shape[0], 2 * LANES - (AC - 2 * SPAN)), BF16)
    wk = jnp.concatenate([attn_b[:, 2 * SPAN :], pad], 1)
    wq = attn_b[:, :SPAN]
    wo = attn_b[:, SPAN : 2 * SPAN]
    if manual:
        wk, wq = after((wk, wq), sent)
        wk = lax.all_to_all(jnp.broadcast_to(wk, (groups * devices, *wk.shape)), ALL, 0, 0, tiled=True)
        wk = wk.reshape(-1, 2 * LANES)
        along = jnp.stack([wq] + [swap_z(wq, turn) for turn in (1, 2, 3)])
        along = jnp.stack([along, swap_y(along)])
        (along, x, marks), (ffn_b, wo) = tied((along, x, marks), (ffn_b, wo))
        near = jnp.stack([along, swap_x(along)]).reshape(16, *wq.shape)
        far = swap_core(near)
        chunk = [ffn_b[0].reshape(-1, 16, cols), wo[None, :, :cols], wo[None, :, cols : 2 * cols]]
        chunk += [ffn_b[1].reshape(-1, 16, cols), wo[None, :, 2 * cols :]]
        chunk = gather_z(jnp.concatenate(chunk, 0), my_z)
    else:
        wk = lax.all_gather(wk, ALL, axis=0, tiled=True)
        wq_all = lax.all_gather(wq, ALL, axis=0, tiled=True).reshape(4, 2, 2, 2, 16, -1)
        wq_all = wq_all.transpose(3, 2, 1, 0, 4, 5).reshape(2, 16, 16, -1)
        near, far = wq_all[0], wq_all[1]
        wo_full = lax.all_gather(wo, ALL, axis=0, tiled=True)
        ffn_all = lax.all_gather(ffn_b, ALL, axis=0, tiled=False)
        ffn_all = ffn_all.reshape(groups, devices, 2, depth, cols).transpose(2, 0, 3, 1, 4)
        ffn_all = ffn_all.reshape(2, groups * depth, devices * cols)
        weights = [wo_full, ffn_all[0], ffn_all[1]]

    routes_x = marks[:, :TOPK]
    tile = 128
    tiles = local_rows // tile
    pieces = tiles // 2
    index = jnp.arange(tiles, dtype=jnp.int32)
    low = index < pieces
    here = jnp.where(low, place * block + index * tile, (2 * devices - 1 - place) * block + (index - pieces) * tile)
    lower = jnp.where(low, marks[0, TOPK], marks[block, TOPK]) * block
    where = jnp.stack([here, lower, jnp.full((tiles,), place)]).astype(jnp.int32)

    h, kv, gates = embed_call(x, routes_x, wk)
    kv = kv.reshape(2, block, LANES)
    kv_x = swap_x(kv)
    me = flat.reshape(1) if manual else jnp.zeros((1,), jnp.int32)
    if manual:
        chunk = after(chunk, kv)
        a_own = chunk[:, :6]
        b_own = chunk[:, 6:]
        a_own = jnp.stack([a_own, swap_y(a_own)])
        b_own = jnp.stack([b_own, swap_x(b_own)])
        a_far, b_far = swap_x(a_own), swap_y(b_own)
        weights = [a_own, a_far, b_own, b_far]
        near, far = after((near, far), (a_own, b_own))
    q, wq_full = query_call(me, h, routes_x, near, far)
    o, logs, keys, values = attend_call(where, q, [kv, swap_core(kv), kv_x, swap_core(kv_x)], tile)
    if manual:
        own = [swap_core(a_own), swap_core(b_own)]
        a_far, b_far = after((a_far, b_far), logs)
        weights += [own[0], swap_core(a_far), own[1], swap_core(b_far)]
        cotangent = after(cotangent, (q, own))
    else:
        cotangent = after(cotangent, q)
    dy = deal(cotangent, halves(cotangent, place), place, logs)
    scalars = jnp.stack([flat, jnp.where((place == 0) | (place == 3), block, 0), jnp.where(place == 1, block, 0)])
    out, out_ring, out_swap, dmid, do, deltas, dlogits, gain2, *grads = middle_call(
        groups, scalars.astype(jnp.int32), x, dy, o, gates, routes_x, wk, weights
    )
    returned = send_back((out_ring, out_swap))

    def back(start, count, carried, before):
        return attend_back_call(
            start, count, pieces, groups, where, q, do, logs, deltas, routes_x, keys, values, carried, h, before
        )

    def split(parts, turn_a, turn_b, swap_a, swap_b):
        a_keep, a_in, b_keep, b_in = parts
        a_out = added(at(a_keep, 1 - turn_a), at(a_in, 1 - turn_a))
        b_out = added(at(b_keep, 1 - turn_b), at(b_in, 1 - turn_b))
        a_keep = added(at(a_keep, turn_a), at(a_in, turn_a))
        b_keep = added(at(b_keep, turn_b), at(b_in, turn_b))
        return (a_keep, swap_a(a_out), b_keep, swap_b(b_out))

    if manual:
        a_keep, a_send, b_keep, b_send = grads
        parts = split((a_keep, swap_core(a_send), b_keep, swap_core(b_send)), my_x, my_y, swap_x, swap_y)
    part_0, *carried = back(0, 2, (), ())
    if manual:
        carried, parts = tied(carried, parts)
        parts = split(parts, my_y, my_x, swap_y, swap_x)
    part_1, *carried = back(2, 1, carried, ())
    if manual:
        carried, parts = tied(carried, parts)
        both = jnp.concatenate([added(*parts[:2]), added(*parts[2:])], 1)
        pieces_out = [at(both, my_z ^ turn) for turn in (1, 2, 3)]
        pieces_out, carried = tied(pieces_out, carried)
        moving = [swap_z(part, turn) for part, turn in zip(pieces_out, (1, 2, 3))]
        chunk_keep = at(both, my_z)
    part_2, kv_keep, kv_send, gq_keep, gq_send = back(3, 1, carried, (part_0, part_1))
    all_parts = [part_0, part_1, part_2]
    kv_in = swap_core(kv_send)
    kv_out = added(kv_keep[1], kv_in[1])
    kv_keep = added(kv_keep[0], kv_in[0]).reshape(local_rows, LANES)
    kv_recv = swap_x(kv_out).reshape(local_rows, LANES)
    dh = query_back_call(dlogits, wq_full, wk, after(all_parts, (kv_out, kv_keep)))
    if manual:
        gq_in = swap_core(gq_send)
        gq_send = added(at(gq_keep, 1 - my_y), at(gq_in, 1 - my_y))
        gq_keep = added(at(gq_keep, my_y), at(gq_in, my_y))
        gq_y = added(gq_keep, swap_y(gq_send))
        gq, returned = tied(gq_y, returned)
        gq_out = [at(gq, my_z ^ turn) for turn in (1, 2, 3)]
        dh, gq_out = tied(dh, gq_out)
        gq_in = [swap_z(part, turn) for part, turn in zip(gq_out, (1, 2, 3))]
        gq = at(gq, my_z)
    grad, gk = post_call(x, h, dmid, dh, kv_keep, kv_recv, dlogits, gain2, wk)
    if manual:
        gk = lax.all_to_all(gk.reshape(groups * devices, -1, 2 * LANES), ALL, 0, 0, tiled=True)
        gq = sum((part.astype(F32) for part in gq_in), gq.astype(F32)).astype(BF16)
        grad, gq = tied(grad, gq)
        gq_raw = at(gq, my_x).astype(F32) + swap_x(at(gq, 1 - my_x)).astype(F32)
    input_grad = put_back(grad, send_back(halves(grad, place)), place).astype(F32)
    layer_out = put_back(out, returned, place)

    if manual:
        chunk_raw = sum((part.astype(F32) for part in moving), chunk_keep.astype(F32))
        rows = depth
        ffn_raw = jnp.stack([chunk_raw[:rows], chunk_raw[rows + 32 : 2 * rows + 32]])
        go_raw = jnp.concatenate(
            [chunk_raw[rows : rows + 16], chunk_raw[rows + 16 : rows + 32], chunk_raw[2 * rows + 32 :]], 1
        )
    else:
        g1, g2, go = grads
        ffn_local = jnp.stack([g1, g2]).reshape(2, groups, depth, devices, cols).transpose(1, 3, 0, 2, 4)
        ffn_local = ffn_local.reshape(groups * devices * 2 * depth, cols)
        ffn_raw = lax.psum_scatter(ffn_local, ALL, scatter_dimension=0, tiled=True).astype(F32)
        ffn_raw = ffn_raw.reshape(2, depth, cols)
        go_raw = lax.psum_scatter(go, ALL, scatter_dimension=0, tiled=True).astype(F32)
        gq_raw = lax.psum_scatter(gq_keep, ALL, scatter_dimension=0, tiled=True).astype(F32)
        gk_raw = lax.psum_scatter(gk, ALL, scatter_dimension=0, tiled=True).astype(F32)
    if manual:
        squares, gk_raw = squares_call(gq_raw, go_raw, ffn_raw, gk)
        squares = lax.all_to_all(squares, ALL, 0, 0, tiled=True)
    else:
        squares = sum(jnp.sum(part * part) for part in (gq_raw, go_raw, gk_raw, ffn_raw))
        squares = lax.psum(squares, ALL) / (8 * LANES)
        squares = jnp.broadcast_to(squares, (1, 8, LANES))
    attn_grad, attn_second_new, attn_new, ffn_grad, ffn_second_new, ffn_new, grad_norm, gain_grad = update_call(
        rates, squares, gq_raw, go_raw, gk_raw, ffn_raw,
        (attn_param, attn_first, attn_second), (ffn_param, ffn_first, ffn_second),
    )
    return (
        layer_out,
        input_grad,
        attn_grad,
        attn_second_new,
        attn_new,
        ffn_grad,
        ffn_second_new,
        ffn_new,
        grad_norm.reshape(()),
        gain_grad,
    )


def solution(mesh):
    by_row = P(ALL, None)
    by_ffn = P(None, "dp", "mp")
    return jax.shard_map(
        shards,
        mesh=mesh,
        in_specs=(by_row, by_row, by_row, P(ALL), by_row, by_row, by_row, by_ffn, by_ffn, by_ffn, P()),
        out_specs=(by_row, by_row, by_row, by_row, by_row, by_ffn, by_ffn, by_ffn, P(), by_row),
        check_vma=False,
    )
```
